32 devices in a mesh: rep: 4 (over y, x), fsdp: 8 (over z, core).
Axes of the slice: x: 2, y: 2, z: 4, core: 2. Of those that a mesh axis runs over, the one named last changes fastest.
Arguments:
- tokens: bfloat16 [32, 256, 1152], P(('rep', 'fsdp')), may hold values from -6 to 6
- conditioning: bfloat16 [32, 4, 1152], P(('rep', 'fsdp')), may hold values from -6 to 6
- segment_ids: int32 [32, 256], P(('rep', 'fsdp')), may hold values from 0 to 3, as said below
- heights: int32 [32, 4], P(('rep', 'fsdp')), may hold values from 4 to 32, as said below
- widths: int32 [32, 4], P(('rep', 'fsdp')), may hold values from 4 to 32, as said below
- pad_mask: int32 [32, 256], P(('rep', 'fsdp')), may hold values from 0 to 1, as said below
- modulation_weight: bfloat16 [1152, 6912], P(None, 'fsdp'), may hold values from -0.1875 to 0.1875
- modulation_bias: bfloat16 [6912], P('fsdp'), may hold values from -3 to 3
- projection_weight: bfloat16 [1152, 3456], P('fsdp'), may hold values from -0.1875 to 0.1875
- projection_bias: bfloat16 [3456], P('fsdp'), may hold values from -3 to 3
- output_weight: bfloat16 [1152, 1152], P('fsdp'), may hold values from -1.5 to 1.5
- output_bias: bfloat16 [1152], P('fsdp'), may hold values from -3 to 3
- gate_weight: bfloat16 [1152, 3072], P('fsdp'), may hold values from -0.1875 to 0.1875
- up_weight: bfloat16 [1152, 3072], P('fsdp'), may hold values from -0.1875 to 0.1875
- down_weight: bfloat16 [3072, 1152], P('fsdp'), may hold values from -0.109375 to 0.109375
- cotangent: bfloat16 [32, 256, 1152], P(('rep', 'fsdp')), may hold values from -6 to 6
Outputs:
- block_output: bfloat16 [32, 256, 1152], P(('rep', 'fsdp'))
- tokens_gradient: float32 [32, 256, 1152], P(('rep', 'fsdp'))
- conditioning_gradient: float32 [32, 4, 1152], P(('rep', 'fsdp'))
- modulation_weight_gradient: float32 [1152, 6912], P(None, 'fsdp')
- modulation_bias_gradient: float32 [6912], P('fsdp')
- projection_weight_gradient: float32 [1152, 3456], P('fsdp')
- projection_bias_gradient: float32 [3456], P('fsdp')
- output_weight_gradient: float32 [1152, 1152], P('fsdp')
- output_bias_gradient: float32 [1152], P('fsdp')
- gate_weight_gradient: float32 [1152, 3072], P('fsdp')
- up_weight_gradient: float32 [1152, 3072], P('fsdp')
- down_weight_gradient: float32 [3072, 1152], P('fsdp')
The draws below stay inside these ranges and needn't reach their ends.
Inputs may be any that keep to these rules, and one draw needn't show every extreme that they name: `segment_ids`: in each row the used image slots 0, 1, ... lie end to end in slot order, slot k covering heights[k] * widths[k] tokens; tokens after the last image carry the id of the first unused slot. `heights`: each slot's grid holds 64 to 256 tokens with aspect between 1:4 and 4:1; a row uses as many leading slots as fit its 256 tokens, at least one; unused slots hold such grids too. `widths`: as for heights. `pad_mask`: 1 exactly on the tokens of the row's used images, 0 on the tokens after them.
All inputs are finite; a program needn't handle non-finite values.
Results may differ from the reference program's by a relative error of at most 0.023.
The reference program's roundings to bfloat16 on the way count: a program that leaves them out, or rounds other values in their place, can miss the bound.
Values may be sent and summed in bfloat16 or wider, within the bound.
No kernel may reach another device: no remote copies, remote signals or barrier semaphores. Data moves between devices by JAX's collectives and lax.ppermute only.
A program may use at most 384 MiB of HBM per device.

```python
import math
import jax
import jax.numpy as jnp
import numpy as np
from jax import lax

D = 1152
HEADS = 16
FF = 3072
SEQ = 256
SLOTS = 4
ROWS = 32


shape_table = np.array([[8, 8], [4, 16], [16, 4], [6, 12], [12, 6], [8, 12], [12, 8], [10, 10], [6, 16], [16, 6], [8, 16], [16, 8], [12, 12], [6, 24], [24, 6], [10, 16], [16, 10], [14, 14], [12, 16], [16, 12], [8, 32], [32, 8], [16, 16]], np.int32)


forced_picks = np.array([[21, 1, 20, 2], [0, 1, 2, 0], [12, 7, 0, 0]], np.int32)


def packing(key):
    table = jnp.asarray(shape_table)
    picks = jax.random.randint(jax.random.fold_in(key, 11), (ROWS, SLOTS), 0, shape_table.shape[0])
    picks = picks.at[0:3].set(jnp.asarray(forced_picks))
    grid_heights = table[picks, 0]
    grid_widths = table[picks, 1]
    grid_sizes = grid_heights * grid_widths
    ends = jnp.cumsum(grid_sizes, axis=1)
    used = (ends <= SEQ).astype(jnp.int32)
    row_total = jnp.sum(grid_sizes * used, axis=1)
    positions = jnp.arange(SEQ, dtype=jnp.int32)
    segments = jnp.sum(used[:, None, :] * (positions[None, :, None] >= ends[:, None, :]).astype(jnp.int32), axis=2)
    valid = (positions[None, :] < row_total[:, None]).astype(jnp.int32)
    return (segments, grid_heights, grid_widths, valid)


def draw_segment_ids(key, part):
    return packing(key)[0]


def draw_heights(key, part):
    return packing(key)[1]


def draw_widths(key, part):
    return packing(key)[2]


def draw_pad_mask(key, part):
    return packing(key)[3]


def block_levels(stream_key, extent, cuts, smallest, top_value):
    gain = 1.0
    for dim, blocks in cuts:
        draws = jax.random.uniform(jax.random.fold_in(jax.random.fold_in(stream_key, 6), dim), (blocks,), jnp.float32, smallest / len(cuts), top_value / len(cuts))
        gain = gain * jnp.repeat(jnp.exp(draws), extent[dim] // blocks).reshape((-1,) + (1,) * (len(extent) - 1 - dim))
    return gain


def bell_draw(key, dims, spread, reach, cuts=(), kind=jnp.bfloat16):
    result = jax.random.normal(key, dims, jnp.float32) * spread
    if len(cuts) > 0:
        result = block_levels(key, dims, cuts, -0.22, 0.18) * result
    return jnp.clip(result, min=-reach, max=reach).astype(kind)


def setup_inputs(seed: int = 0) -> dict:
    seeds = jax.random.split(jax.random.key(seed), 17)
    return {
        "tokens": bell_draw(seeds[0], (ROWS, SEQ, D), 1.0, 6.0, ((0, 32),)),
        "conditioning": bell_draw(seeds[1], (ROWS, SLOTS, D), 1.0, 6.0, ((0, 32),)),
        "segment_ids": draw_segment_ids(jax.random.fold_in(seeds[16], 71), 0),
        "heights": draw_heights(jax.random.fold_in(seeds[16], 71), 0),
        "widths": draw_widths(jax.random.fold_in(seeds[16], 71), 0),
        "pad_mask": draw_pad_mask(jax.random.fold_in(seeds[16], 71), 0),
        "modulation_weight": bell_draw(seeds[6], (D, 6 * D), D ** -0.5, 0.1875, ((1, 8),)),
        "modulation_bias": bell_draw(seeds[7], (6 * D,), 0.5, 3.0, ((0, 8),)),
        "projection_weight": bell_draw(seeds[8], (D, 3 * D), D ** -0.5, 0.1875, ((0, 8),)),
        "projection_bias": bell_draw(seeds[9], (3 * D,), 0.5, 3.0, ((0, 8),)),
        "output_weight": bell_draw(seeds[10], (D, D), (max(D // 64, 1)) ** -0.5, 1.5, ((0, 8),)),
        "output_bias": bell_draw(seeds[11], (D,), 0.5, 3.0, ((0, 8),)),
        "gate_weight": bell_draw(seeds[12], (D, FF), D ** -0.5, 0.1875, ((0, 8),)),
        "up_weight": bell_draw(seeds[13], (D, FF), D ** -0.5, 0.1875, ((0, 8),)),
        "down_weight": bell_draw(seeds[14], (FF, D), FF ** -0.5, 0.109375, ((0, 8),)),
        "cotangent": bell_draw(seeds[15], (ROWS, SEQ, D), 1.0, 6.0, ((0, 32),)),
    }


@jax.custom_vjp
def low(v):
    return lax.optimization_barrier(v.astype(jnp.bfloat16)).astype(jnp.float32)

@jax.custom_vjp
def low_back(v):
    return v

def low_keep(v):
    return (low(v), None)

def low_pass(kept, grad):
    return (grad,)

def back_keep(v):
    return (v, None)

def back_low(kept, grad):
    return (low(grad),)
low.defvjp(low_keep, low_pass)
low_back.defvjp(back_keep, back_low)

def product(form, left, right):
    return jnp.einsum(form, left, right, precision=lax.Precision.HIGHEST)

def normalize(values):
    centered = values - lax.optimization_barrier(jnp.mean(values, axis=-1, keepdims=True))
    variance = lax.optimization_barrier(jnp.mean(centered * centered, axis=-1, keepdims=True))
    return centered * lax.rsqrt(variance + 1e-06)

def token_places(segment_ids, heights, widths):
    slot_count = heights.shape[1]
    token_count = segment_ids.shape[1]
    slot_ids = jnp.arange(slot_count, dtype=jnp.int32)
    member_ints = (segment_ids[:, :, None] == slot_ids[None, None, :]).astype(jnp.int32)
    before_ints = (slot_ids[None, None, :] < segment_ids[:, :, None]).astype(jnp.int32)
    grid_sizes = heights * widths
    starts = lax.optimization_barrier(jnp.sum(before_ints * grid_sizes[:, None, :], axis=2))
    offsets = jnp.arange(token_count, dtype=jnp.int32)[None, :] - starts
    row_width = lax.optimization_barrier(jnp.sum(member_ints * widths[:, None, :], axis=2))
    return (member_ints.astype(jnp.float32), offsets // row_width, offsets % row_width)

def rotary_tables(grid_rows, grid_columns, head_width):
    pair_count = head_width // 4
    frequency = 10000.0 ** (-jnp.arange(pair_count, dtype=jnp.float32) / pair_count)
    places = jnp.stack([grid_rows, grid_columns], axis=-1).astype(jnp.float32)
    turned = places[..., None] * frequency
    return (jnp.cos(turned)[:, :, None], jnp.sin(turned)[:, :, None])

def rotate(vectors, cosine_table, sine_table):
    full_shape = vectors.shape
    split_view = vectors.reshape(full_shape[:-1] + (2, 2, full_shape[-1] // 4))
    first_half = split_view[..., 0, :]
    second = split_view[..., 1, :]
    turned = jnp.stack([first_half * cosine_table - second * sine_table, first_half * sine_table + second * cosine_table], axis=-2)
    return turned.reshape(full_shape)

def block_rows(weights, tokens, conditioning, segment_ids, heights, widths):
    modulation_weight, modulation_bias, projection_weight, projection_bias, output_weight, output_bias, gate_weight, up_weight, down_weight = weights
    model_width = tokens.shape[-1]
    head_width = model_width // HEADS
    members, grid_rows, grid_columns = token_places(segment_ids, heights, widths)
    cosine_table, sine_table = rotary_tables(grid_rows, grid_columns, head_width)
    activated = low(jax.nn.silu(conditioning))
    modulation = low_back(product('rkd,dc->rkc', activated, modulation_weight) + modulation_bias)
    per_token = product('rsk,rkc->rsc', members, modulation)
    shift_one, scale_one, gate_one, shift_two, scale_two, gate_two = jnp.split(per_token, 6, axis=-1)
    hidden_one = low(normalize(tokens) * (1.0 + scale_one) + shift_one)
    projected = low_back(product('rsd,dc->rsc', hidden_one, projection_weight) + projection_bias)
    query_part, key_part, value_part = jnp.split(projected, 3, axis=-1)
    head_shape = tokens.shape[:2] + (HEADS, head_width)
    query_rot = low(rotate(query_part.reshape(head_shape), cosine_table, sine_table))
    key_rot = low(rotate(key_part.reshape(head_shape), cosine_table, sine_table))
    value_low = low(value_part.reshape(head_shape))
    scores = low_back(product('rqhe,rkhe->rhqk', query_rot, key_rot) * (1.0 / math.sqrt(head_width)))
    same_image = segment_ids[:, :, None] == segment_ids[:, None, :]
    scores = jnp.where(same_image[:, None], scores, -1e+30)
    exponent = jnp.exp(scores - lax.optimization_barrier(jnp.max(scores, axis=-1, keepdims=True)))
    attention_probs = exponent / lax.optimization_barrier(jnp.sum(exponent, axis=-1, keepdims=True))
    attended = product('rhqk,rkhe->rqhe', low(attention_probs), value_low)
    attended = low(low_back(attended)).reshape(tokens.shape)
    branch = low_back(product('rsd,dc->rsc', attended, output_weight) + output_bias)
    middle = tokens + gate_one * branch
    hidden_two = low(normalize(middle) * (1.0 + scale_two) + shift_two)
    gate_value = low_back(product('rsd,df->rsf', hidden_two, gate_weight))
    up_value = low_back(product('rsd,df->rsf', hidden_two, up_weight))
    hidden_three = low(jax.nn.silu(gate_value) * up_value)
    feed = low_back(product('rsf,fd->rsd', hidden_three, down_weight))
    return middle + gate_two * feed

def reference(tokens, conditioning, segment_ids, heights, widths, pad_mask, modulation_weight, modulation_bias, projection_weight, projection_bias, output_weight, output_bias, gate_weight, up_weight, down_weight, cotangent):
    weights = tuple((matrix.astype(jnp.float32) for matrix in (modulation_weight, modulation_bias, projection_weight, projection_bias, output_weight, output_bias, gate_weight, up_weight, down_weight)))
    row_count = tokens.shape[0]
    group_rows = math.gcd(row_count, 16)

    def grouped(array):
        return array.reshape((row_count // group_rows, group_rows) + array.shape[1:])
    checked = jax.checkpoint(block_rows)

    def forward(weight_set, tokens_float, cond_float):
        outputs = lax.map(lambda group_items: checked(weight_set, group_items[0], group_items[1], group_items[2], group_items[3], group_items[4]), (grouped(tokens_float), grouped(cond_float), grouped(segment_ids), grouped(heights), grouped(widths)))
        return outputs.reshape(tokens_float.shape)
    tokens_float = tokens.astype(jnp.float32)
    cond_float = conditioning.astype(jnp.float32)
    outputs, pullback = jax.vjp(forward, weights, tokens_float, cond_float)
    masked = cotangent.astype(jnp.float32) * pad_mask.astype(jnp.float32)[:, :, None]
    weight_grads, tokens_gradient, conditioning_gradient = pullback(masked)
    return (outputs.astype(jnp.bfloat16), tokens_gradient, conditioning_gradient, weight_grads[0], weight_grads[1], weight_grads[2], weight_grads[3], weight_grads[4], weight_grads[5], weight_grads[6], weight_grads[7], weight_grads[8])
```

```python
import math

import jax
import jax.numpy as jnp
from jax import lax
from jax.sharding import PartitionSpec as P

HEADS = 16
BF = jnp.bfloat16
F32 = jnp.float32


def token_places(segment_ids, heights, widths):
    slot_count = heights.shape[1]
    token_count = segment_ids.shape[1]
    slot_ids = jnp.arange(slot_count, dtype=jnp.int32)
    member_ints = (segment_ids[:, :, None] == slot_ids[None, None, :]).astype(jnp.int32)
    before_ints = (slot_ids[None, None, :] < segment_ids[:, :, None]).astype(jnp.int32)
    grid_sizes = heights * widths
    starts = jnp.sum(before_ints * grid_sizes[:, None, :], axis=2)
    offsets = jnp.arange(token_count, dtype=jnp.int32)[None, :] - starts
    row_width = jnp.sum(member_ints * widths[:, None, :], axis=2)
    return (member_ints.astype(jnp.float32), offsets // row_width, offsets % row_width)


def rotary_tables(grid_rows, grid_columns, head_width):
    pair_count = head_width // 4
    frequency = 10000.0 ** (-jnp.arange(pair_count, dtype=jnp.float32) / pair_count)
    places = jnp.stack([grid_rows, grid_columns], axis=-1).astype(jnp.float32)
    turned = places[..., None] * frequency
    return (jnp.cos(turned)[:, :, None], jnp.sin(turned)[:, :, None])


def rotate(vectors, cosine_table, sine_table):
    full_shape = vectors.shape
    split_view = vectors.reshape(full_shape[:-1] + (2, 2, full_shape[-1] // 4))
    first_half = split_view[..., 0, :]
    second = split_view[..., 1, :]
    turned = jnp.stack(
        [
            first_half * cosine_table - second * sine_table,
            first_half * sine_table + second * cosine_table,
        ],
        axis=-2,
    )
    return turned.reshape(full_shape)


def normalize_keep(values):
    centered = values - jnp.mean(values, axis=-1, keepdims=True)
    variance = jnp.mean(centered * centered, axis=-1, keepdims=True)
    inverse = lax.rsqrt(variance + 1e-06)
    return (centered * inverse, inverse)


def normalize_back(normed, inverse, upstream):
    return inverse * (
        upstream
        - jnp.mean(upstream, axis=-1, keepdims=True)
        - normed * jnp.mean(upstream * normed, axis=-1, keepdims=True)
    )


def matmul(left, right):
    return jnp.dot(left, right, preferred_element_type=jnp.float32)


def matmul_right_t(left, right):
    return lax.dot_general(
        left, right, (((left.ndim - 1,), (1,)), ((), ())), preferred_element_type=jnp.float32
    )


def matmul_left_t(left, right):
    return lax.dot_general(
        left, right, (((0,), (0,)), ((), ())), preferred_element_type=jnp.float32
    )


def silu_slope(values):
    sigmoid = jax.nn.sigmoid(values)
    return sigmoid * (1.0 + values * (1.0 - sigmoid))


def swap_with(value, axis, size, bit):
    return lax.ppermute(value, axis, [(i, i ^ bit) for i in range(size)])


def bits_of(size):
    return [1 << k for k in range(size.bit_length() - 1)]


def reorder(blocks, index, size):
    rest = blocks.shape[1:]
    for bit in bits_of(size):
        paired = blocks.reshape((size // (2 * bit), 2, bit) + rest)
        flipped = jnp.stack([paired[:, 1], paired[:, 0]], axis=1)
        blocks = jnp.where((index & bit) != 0, flipped, paired).reshape((size,) + rest)
    return blocks


def hop_gather(value, axis, size):
    held = value
    for depth, bit in enumerate(reversed(bits_of(size))):
        held = jnp.stack([held, swap_with(held, axis, size, bit)], axis=depth)
    return held.reshape((size,) + value.shape)


def hop_exchange(blocks, axis, size):
    rest = blocks.shape[1:]
    for bit in bits_of(size):
        paired = blocks.reshape((size // (2 * bit), 2, bit) + rest)
        came = swap_with(paired[:, 1], axis, size, bit)
        blocks = jnp.stack([paired[:, 0], came], axis=1).reshape((size,) + rest)
    return blocks


def hop_scatter(blocks, axis, size):
    held = blocks
    for bit in bits_of(size):
        paired = held.reshape((held.shape[0] // 2, 2) + held.shape[1:])
        held = paired[:, 0] + swap_with(paired[:, 1], axis, size, bit)
    return held[0]


def hop_sum(value, axis, size):
    for bit in bits_of(size):
        value = value + swap_with(value, axis, size, bit)
    return value


def gather_blocks(value, axis, size):
    if size != 4:
        return jnp.stack(
            [value] + [swap_with(value, axis, size, j) for j in range(1, size)], axis=0
        )
    half = value.shape[-2] // 2
    top, low = value[..., :half, :], value[..., half:, :]
    top_one = swap_with(top, axis, size, 1)
    low_two = swap_with(low, axis, size, 2)
    low_one = swap_with(low, axis, size, 1)
    top_two = swap_with(top, axis, size, 2)
    top_three = swap_with(top_one, axis, size, 2)
    low_three = swap_with(low_two, axis, size, 1)
    return jnp.stack(
        [
            value,
            jnp.concatenate([top_one, low_one], axis=-2),
            jnp.concatenate([top_two, low_two], axis=-2),
            jnp.concatenate([top_three, low_three], axis=-2),
        ],
        axis=0,
    )


def exchange_blocks(blocks, axis, size):
    return jnp.stack(
        [blocks[0]] + [swap_with(blocks[j], axis, size, j) for j in range(1, size)], axis=0
    )


def scatter_blocks(blocks, axis, size):
    if size != 4:
        total = blocks[0]
        for j in range(1, size):
            total = total + swap_with(blocks[j].astype(BF), axis, size, j).astype(F32)
        return total
    half = blocks.shape[-2] // 2
    top, low = blocks[..., :half, :], blocks[..., half:, :]
    top_three = swap_with(top[3].astype(BF), axis, size, 1)
    low_three = swap_with(low[3].astype(BF), axis, size, 2)
    top_one = swap_with(top[1].astype(BF), axis, size, 1)
    low_two = swap_with(low[2].astype(BF), axis, size, 2)
    top_pair = (top[2] + top_three.astype(F32)).astype(BF)
    low_pair = (low[1] + low_three.astype(F32)).astype(BF)
    top_two = swap_with(top_pair, axis, size, 2)
    low_one = swap_with(low_pair, axis, size, 1)
    return jnp.concatenate(
        [
            top[0] + top_one.astype(F32) + top_two.astype(F32),
            low[0] + low_two.astype(F32) + low_one.astype(F32),
        ],
        axis=-2,
    )


def on_device(
    rep_size,
    fsdp_size,
    tokens,
    conditioning,
    segment_ids,
    heights,
    widths,
    pad_mask,
    modulation_weight,
    modulation_bias,
    projection_weight,
    projection_bias,
    output_weight,
    output_bias,
    gate_weight,
    up_weight,
    down_weight,
    cotangent,
):
    rows, token_count, width = tokens.shape
    slots = conditioning.shape[1]
    head_width = width // HEADS
    local_heads = HEADS // rep_size
    block = width // rep_size
    flat = rows * token_count
    all_rows = rep_size * rows
    all_flat = all_rows * token_count
    score_scale = 1.0 / math.sqrt(head_width)
    shard_ff = down_weight.shape[0]
    piece = shard_ff // rep_size
    block_ff = fsdp_size * piece
    shard_width = projection_weight.shape[0]
    columns = modulation_weight.shape[1]
    r = lax.axis_index("rep")
    f = lax.axis_index("fsdp")

    def rep_block(array, axis):
        return lax.dynamic_index_in_dim(array, r, axis, keepdims=False)

    qkv_shard = rep_block(
        projection_weight.reshape(shard_width, 3, rep_size, block), 2
    ).reshape(shard_width, 3 * block)
    qkv_block = lax.all_gather(qkv_shard, "fsdp", axis=0, tiled=True)
    out_full = lax.all_gather(output_weight, "fsdp", axis=0, tiled=True)
    gate_shard = rep_block(gate_weight.reshape(shard_width, fsdp_size, rep_size, piece), 2)
    up_shard = rep_block(up_weight.reshape(shard_width, fsdp_size, rep_size, piece), 2)
    gate_up_shard = jnp.concatenate(
        [gate_shard.reshape(shard_width, block_ff), up_shard.reshape(shard_width, block_ff)], axis=1
    )
    gate_up_block = lax.all_gather(gate_up_shard, "fsdp", axis=0, tiled=True)
    down_shard = rep_block(down_weight.reshape(rep_size, piece, width), 0)
    down_block = lax.all_gather(down_shard, "fsdp", axis=0, tiled=True)

    cond_float = conditioning.astype(F32)
    activated = jax.nn.silu(cond_float).astype(BF).reshape(rows * slots, width)
    bias_shard = jnp.concatenate([projection_bias, output_bias])
    bias_row = jnp.pad(bias_shard, (0, width - bias_shard.shape[0]))[None]
    gathered = hop_gather(jnp.concatenate([activated, bias_row], axis=0), "fsdp", fsdp_size)
    line_activated = gathered[:, : rows * slots]
    bias_all = reorder(gathered[:, rows * slots, : bias_shard.shape[0]], f, fsdp_size)
    projection_bias_all = bias_all[:, : projection_bias.shape[0]].reshape(3, rep_size, block)
    output_bias_all = bias_all[:, projection_bias.shape[0] :].reshape(width)
    line_modulation = matmul(
        line_activated.reshape(fsdp_size * rows * slots, width), modulation_weight
    ) + modulation_bias.astype(F32)
    own_modulation = reorder(
        hop_exchange(
            line_modulation.reshape(fsdp_size, rows * slots, columns), "fsdp", fsdp_size
        ),
        f,
        fsdp_size,
    )
    modulation = jnp.swapaxes(own_modulation, 0, 1).reshape(rows, slots, 6 * width)
    members, grid_rows, grid_columns = token_places(segment_ids, heights, widths)
    per_token = jnp.einsum("rsk,rkc->rsc", members, modulation, precision=lax.Precision.HIGHEST)
    shift_one, scale_one, gate_one, shift_two, scale_two, gate_two = jnp.split(
        per_token, 6, axis=-1
    )

    places = jnp.stack([segment_ids, grid_rows, grid_columns], axis=1)
    all_places = hop_gather(places, "rep", rep_size).reshape(all_rows, 3, token_count)
    all_segments = all_places[:, 0]
    cosine_table, sine_table = rotary_tables(all_places[:, 1], all_places[:, 2], head_width)
    tokens_float = tokens.astype(F32)
    normed_one, inverse_one = normalize_keep(tokens_float)
    hidden_one = (normed_one * (1.0 + scale_one) + shift_one).astype(BF)
    hidden_one_all = gather_blocks(hidden_one, "rep", rep_size).reshape(all_flat, width)
    masked = cotangent.astype(F32) * pad_mask.astype(F32)[:, :, None]
    feed_back = (gate_two * masked).astype(BF)
    feed_back_all = gather_blocks(feed_back, "rep", rep_size).reshape(all_flat, width)

    projected = matmul(hidden_one_all, qkv_block) + rep_block(projection_bias_all, 1).reshape(
        3 * block
    ).astype(F32)
    query_part, key_part, value_part = jnp.split(
        projected.reshape(all_rows, token_count, 3 * block), 3, axis=-1
    )
    head_shape = (all_rows, token_count, local_heads, head_width)
    query_rot = rotate(query_part.reshape(head_shape), cosine_table, sine_table).astype(BF)
    key_rot = rotate(key_part.reshape(head_shape), cosine_table, sine_table).astype(BF)
    value_low = value_part.reshape(head_shape).astype(BF)
    same_image = (all_segments[:, :, None] == all_segments[:, None, :])[:, None]
    raw_scores = (
        jnp.einsum("rqhe,rkhe->rhqk", query_rot, key_rot, preferred_element_type=F32) * score_scale
    )
    scores = jnp.where(same_image, raw_scores, -1e30)
    exponent = jnp.exp(scores - jnp.max(scores, axis=-1, keepdims=True))
    attention_probs = exponent / jnp.sum(exponent, axis=-1, keepdims=True)
    probs_low = attention_probs.astype(BF)
    attended_heads = jnp.einsum(
        "rhqk,rkhe->rqhe", probs_low, value_low, preferred_element_type=F32
    ).astype(BF)
    attended_blocks = reorder(
        exchange_blocks(
            attended_heads.reshape(rep_size, flat, block), "rep", rep_size
        ),
        r,
        rep_size,
    )
    attended = jnp.swapaxes(attended_blocks, 0, 1).reshape(flat, width)

    branch = (matmul(attended, out_full) + output_bias_all.astype(F32)).reshape(
        rows, token_count, width
    )
    middle = tokens_float + gate_one * branch
    normed_two, inverse_two = normalize_keep(middle)
    hidden_two = (normed_two * (1.0 + scale_two) + shift_two).astype(BF)
    hidden_two_all = gather_blocks(hidden_two, "rep", rep_size).reshape(all_flat, width)

    gate_block, up_block = gate_up_block[:, :block_ff], gate_up_block[:, block_ff:]
    gate_value = matmul(hidden_two_all, gate_block)
    up_value = matmul(hidden_two_all, up_block)
    hidden_three = (jax.nn.silu(gate_value) * up_value).astype(BF)
    hidden_back = matmul_right_t(feed_back_all, down_block)
    gate_back = (hidden_back * up_value * silu_slope(gate_value)).astype(BF)
    up_back = (hidden_back * jax.nn.silu(gate_value)).astype(BF)
    hidden_two_back_part = matmul_right_t(gate_back, gate_block) + matmul_right_t(up_back, up_block)
    hidden_two_back = scatter_blocks(
        hidden_two_back_part.reshape(rep_size, flat, width), "rep", rep_size
    ).reshape(rows, token_count, width)
    down_gradient = lax.psum_scatter(
        matmul_left_t(hidden_three, feed_back_all).astype(BF),
        "fsdp",
        scatter_dimension=0,
        tiled=True,
    )
    gate_up_gradient = lax.psum_scatter(
        jnp.concatenate(
            [matmul_left_t(hidden_two_all, gate_back), matmul_left_t(hidden_two_all, up_back)],
            axis=1,
        ).astype(BF),
        "fsdp",
        scatter_dimension=0,
        tiled=True,
    )
    feed = scatter_blocks(
        matmul(hidden_three, down_block).reshape(rep_size, flat, width), "rep", rep_size
    ).reshape(rows, token_count, width)
    block_output = (middle + gate_two * feed).astype(BF)
    gate_two_back = masked * feed

    middle_back = masked + normalize_back(
        normed_two, inverse_two, hidden_two_back * (1.0 + scale_two)
    )
    gate_one_back = middle_back * branch
    branch_back = (middle_back * gate_one).astype(BF).reshape(flat, width)
    attended_back_own = matmul_right_t(branch_back, out_full).astype(BF)
    attended_back = exchange_blocks(
        reorder(
            jnp.swapaxes(attended_back_own.reshape(flat, rep_size, block), 0, 1), r, rep_size
        ),
        "rep",
        rep_size,
    ).reshape(head_shape)
    output_gradient = hop_sum(
        lax.psum_scatter(
            matmul_left_t(attended, branch_back).astype(BF),
            "fsdp",
            scatter_dimension=0,
            tiled=True,
        ),
        "rep",
        rep_size,
    ).astype(F32)

    probs_back = jnp.einsum(
        "rqhe,rkhe->rhqk", attended_back, value_low, preferred_element_type=F32
    )
    value_back = jnp.einsum(
        "rhqk,rqhe->rkhe", probs_low, attended_back, preferred_element_type=F32
    )
    scores_back = (
        attention_probs
        * (probs_back - jnp.sum(attention_probs * probs_back, axis=-1, keepdims=True))
    ).astype(BF)
    query_back = (
        jnp.einsum("rhqk,rkhe->rqhe", scores_back, key_rot, preferred_element_type=F32)
        * score_scale
    )
    key_back = (
        jnp.einsum("rhqk,rqhe->rkhe", scores_back, query_rot, preferred_element_type=F32)
        * score_scale
    )
    query_back = rotate(query_back, cosine_table, -sine_table)
    key_back = rotate(key_back, cosine_table, -sine_table)
    projected_back = jnp.concatenate(
        [
            query_back.reshape(all_flat, block),
            key_back.reshape(all_flat, block),
            value_back.reshape(all_flat, block),
        ],
        axis=-1,
    ).astype(BF)
    hidden_one_back = scatter_blocks(
        matmul_right_t(projected_back, qkv_block).reshape(rep_size, flat, width), "rep", rep_size
    ).reshape(rows, token_count, width)
    projection_gradient = lax.psum_scatter(
        matmul_left_t(hidden_one_all, projected_back).astype(BF),
        "fsdp",
        scatter_dimension=0,
        tiled=True,
    )
    tokens_gradient = middle_back + normalize_back(
        normed_one, inverse_one, hidden_one_back * (1.0 + scale_one)
    )

    per_token_back = jnp.concatenate(
        [
            hidden_one_back,
            hidden_one_back * normed_one,
            gate_one_back,
            hidden_two_back,
            hidden_two_back * normed_two,
            gate_two_back,
        ],
        axis=-1,
    )
    modulation_back = jnp.einsum(
        "rsk,rsc->rkc", members, per_token_back, precision=lax.Precision.HIGHEST
    ).astype(BF)
    back_blocks = reorder(
        jnp.swapaxes(
            modulation_back.reshape(rows * slots, fsdp_size, columns), 0, 1
        ),
        f,
        fsdp_size,
    )
    line_back = hop_exchange(back_blocks, "fsdp", fsdp_size)
    all_back = hop_gather(line_back, "rep", rep_size).reshape(-1, columns)
    all_activated = hop_gather(line_activated, "rep", rep_size).reshape(-1, width)
    table_gradient = matmul_left_t(all_activated, all_back)
    table_bias_gradient = jnp.sum(all_back.astype(F32), axis=0)
    activated_back = hop_scatter(
        matmul_right_t(line_back.reshape(-1, columns), modulation_weight).reshape(
            fsdp_size, rows * slots, width
        ),
        "fsdp",
        fsdp_size,
    )
    conditioning_gradient = activated_back.reshape(rows, slots, width) * silu_slope(cond_float)

    def all_blocks(value):
        return reorder(gather_blocks(value, "rep", rep_size), r, rep_size).astype(F32)

    down_gradient = all_blocks(down_gradient).reshape(shard_ff, width)
    gate_up_gradient = all_blocks(gate_up_gradient).reshape(
        rep_size, shard_width, 2, fsdp_size, piece
    )
    gate_up_gradient = jnp.transpose(gate_up_gradient, (2, 1, 3, 0, 4)).reshape(
        2, shard_width, fsdp_size * shard_ff
    )
    projection_gradient = jnp.transpose(
        all_blocks(projection_gradient).reshape(rep_size, shard_width, 3, block), (1, 2, 0, 3)
    ).reshape(shard_width, 3 * width)
    bias_sums = hop_sum(
        jnp.concatenate(
            [
                jnp.sum(projected_back.astype(F32), axis=0),
                jnp.sum(branch_back.astype(F32), axis=0),
            ]
        ),
        "fsdp",
        fsdp_size,
    )
    bias_sums = reorder(hop_gather(bias_sums, "rep", rep_size), r, rep_size)
    projection_bias_gradient = jnp.swapaxes(
        bias_sums[:, : 3 * block].reshape(rep_size, 3, block), 0, 1
    ).reshape(fsdp_size, -1)
    output_bias_gradient = jnp.sum(bias_sums[:, 3 * block :], axis=0).reshape(fsdp_size, -1)
    return (
        block_output,
        tokens_gradient,
        conditioning_gradient,
        table_gradient,
        table_bias_gradient,
        projection_gradient,
        lax.dynamic_index_in_dim(projection_bias_gradient, f, 0, keepdims=False),
        output_gradient,
        lax.dynamic_index_in_dim(output_bias_gradient, f, 0, keepdims=False),
        gate_up_gradient[0],
        gate_up_gradient[1],
        down_gradient,
    )


def solution(mesh):
    sizes = dict(mesh.shape)

    def body(*arrays):
        return on_device(sizes["rep"], sizes["fsdp"], *arrays)

    rows = ("rep", "fsdp")
    in_specs = (
        P(rows, None, None),
        P(rows, None, None),
        P(rows, None),
        P(rows, None),
        P(rows, None),
        P(rows, None),
        P(None, "fsdp"),
        P("fsdp"),
        P("fsdp", None),
        P("fsdp"),
        P("fsdp", None),
        P("fsdp"),
        P("fsdp", None),
        P("fsdp", None),
        P("fsdp", None),
        P(rows, None, None),
    )
    out_specs = (
        P(rows, None, None),
        P(rows, None, None),
        P(rows, None, None),
        P(None, "fsdp"),
        P("fsdp"),
        P("fsdp", None),
        P("fsdp"),
        P("fsdp", None),
        P("fsdp"),
        P("fsdp", None),
        P("fsdp", None),
        P("fsdp", None),
    )
    return jax.shard_map(
        body, mesh=mesh, in_specs=in_specs, out_specs=out_specs, check_vma=False
    )
```

```python
import math

import jax
import jax.numpy as jnp
import numpy as np
from jax import lax
from jax.experimental import pallas as pl
from jax.experimental.pallas import tpu as pltpu
from jax.sharding import PartitionSpec as P

HEADS = 16
BF = jnp.bfloat16
F32 = jnp.float32
LANES = 128
CHUNK = 32
GROUP = 8


def wait_for(value, *others):
    return lax.optimization_barrier((value, others))[0]


def swap_with(value, axis, size, bit):
    return lax.ppermute(value, axis, [(i, i ^ bit) for i in range(size)])


def gather(value, axis, size):
    return [value] + [swap_with(value, axis, size, j) for j in range(1, size)]


def send(values, axis, size):
    return [values[0]] + [swap_with(values[j], axis, size, j) for j in range(1, size)]


def exchange(value, axis):
    return lax.all_to_all(value, axis, 0, 0, tiled=True)


def call(order, body, name, scalars, arrays, outs, micros, scratch=(), limit=48):
    shapes = [jax.ShapeDtypeStruct(shape, dtype) for shape, dtype in outs]
    if order:
        first, _ = lax.optimization_barrier((arrays[0], order.pop()))
        arrays = [first] + list(arrays[1:])
    results = pl.pallas_call(
        body,
        name=name,
        out_shape=shapes,
        in_specs=[pl.BlockSpec(memory_space=pltpu.SMEM)] * len(scalars)
        + [pl.BlockSpec(memory_space=pltpu.VMEM)] * len(arrays),
        out_specs=[pl.BlockSpec(memory_space=pltpu.VMEM)] * len(shapes),
        scratch_shapes=[pltpu.VMEM(shape, dtype) for shape, dtype in scratch],
        compiler_params=pltpu.CompilerParams(vmem_limit_bytes=limit << 20),
        cost_estimate=pl.CostEstimate(
            flops=int(micros * 3e9), bytes_accessed=int(micros * 9e6), transcendentals=0
        ),
    )(*scalars, *arrays)
    order.append(results[0])
    return results


def part_shapes(size, tokens, width):
    return [((tokens, width), F32)] + [((tokens, width), BF)] * (size - 1)


def store_parts(parts, refs):
    refs[0][...] = parts[0]
    for j in range(1, len(refs)):
        refs[j][...] = parts[j].astype(BF)


def dot(left, right):
    return jnp.dot(left, right, preferred_element_type=F32)


def dot_rt(left, right):
    return lax.dot_general(left, right, (((1,), (1,)), ((), ())), preferred_element_type=F32)


def dot_lt(left, right):
    return lax.dot_general(left, right, (((0,), (0,)), ((), ())), preferred_element_type=F32)


def pick(modulation, slot_of, first, width):
    total = jnp.zeros((slot_of.shape[0], width), F32)
    for k in range(modulation.shape[0]):
        total = jnp.where(slot_of == k, modulation[k : k + 1, first : first + width], total)
    return total


def normalize_keep(values):
    centered = values - jnp.mean(values, axis=-1, keepdims=True)
    variance = jnp.mean(centered * centered, axis=-1, keepdims=True)
    inverse = lax.rsqrt(variance + 1e-06)
    return centered * inverse, inverse


def normalize_back(normed, inverse, upstream):
    return inverse * (
        upstream
        - jnp.mean(upstream, axis=-1, keepdims=True)
        - normed * jnp.mean(upstream * normed, axis=-1, keepdims=True)
    )


def add_slots(sums, base, count, slot_of, values):
    rows, width = values.shape
    for k in range(count):
        chosen = jnp.where(slot_of == k, values, 0.0)
        sums[base + k] += jnp.sum(chosen.reshape(rows // 8, 8, width), axis=0)


def chunks(tokens, step):
    def body(i, carry):
        step(pl.ds(pl.multiple_of(i * CHUNK, CHUNK), CHUNK))
        return carry

    lax.fori_loop(0, tokens // CHUNK, body, 0)


def silu_slope(values):
    sigmoid = jax.nn.sigmoid(values)
    return sigmoid * (1.0 + values * (1.0 - sigmoid))


def on_device(
    rep_size,
    fsdp_size,
    tokens,
    conditioning,
    segment_ids,
    heights,
    widths,
    pad_mask,
    modulation_weight,
    modulation_bias,
    projection_weight,
    projection_bias,
    output_weight,
    output_bias,
    gate_weight,
    up_weight,
    down_weight,
    cotangent,
):
    rows, count, width = tokens.shape
    assert rows == 1
    slots = conditioning.shape[1]
    head_width = width // HEADS
    local_heads = HEADS // rep_size
    block = width // rep_size
    padded = -(-block // LANES) * LANES
    score_scale = 1.0 / math.sqrt(head_width)
    shard_ff = down_weight.shape[0]
    piece = shard_ff // rep_size
    block_ff = fsdp_size * piece
    shard_width = projection_weight.shape[0]
    columns = modulation_weight.shape[1]
    flat = rep_size * count
    r = lax.axis_index("rep")
    r_index = r.reshape(1).astype(jnp.int32)
    tokens, cotangent = tokens[0], cotangent[0]
    order = []

    def qkv_shard_kernel(r_ref, projection, out):
        for k in range(rep_size):

            @pl.when(r_ref[0] == k)
            def _():
                for t in range(3):
                    first = t * width + k * block
                    out[:, t * block : (t + 1) * block] = projection[:, first : first + block]

    (qkv_shard,) = call(
        order,
        qkv_shard_kernel,
        "qkv_shard",
        [r_index],
        [projection_weight],
        [((shard_width, 3 * block), BF)],
        1.5,
        limit=16,
    )

    slot_ids = jnp.arange(slots, dtype=jnp.int32)
    member_ints = (segment_ids[:, :, None] == slot_ids).astype(jnp.int32)
    before_ints = (slot_ids < segment_ids[:, :, None]).astype(jnp.int32)
    starts = jnp.sum(before_ints * (heights * widths)[:, None, :], axis=2)
    offsets = jnp.arange(count, dtype=jnp.int32)[None, :] - starts
    row_width = jnp.sum(member_ints * widths[:, None, :], axis=2)
    places = jnp.concatenate(
        [segment_ids, offsets // row_width, offsets % row_width, pad_mask], axis=1
    ).astype(BF)
    places = jnp.pad(places, ((0, GROUP - 1), (0, width - 4 * count)))
    token_rows = gather(jnp.concatenate([tokens, places], axis=0), "rep", rep_size)
    cotangent_rows = gather(wait_for(cotangent, token_rows), "rep", rep_size)

    cond_float = conditioning.astype(F32)
    activated = jax.nn.silu(cond_float).astype(BF).reshape(slots, width)
    shard_bias, shard_out_bias = projection_bias.shape[0], output_bias.shape[0]
    bias_row = jnp.pad(
        jnp.concatenate([projection_bias, output_bias]), (0, width - shard_bias - shard_out_bias)
    )[None]
    group_rows = jnp.concatenate(
        [activated, bias_row, jnp.zeros((GROUP - slots - 1, width), BF)], axis=0
    )
    line_rows = lax.all_gather(group_rows, "fsdp", axis=0, tiled=True)

    def modulate_kernel(r_ref, *refs):
        groups, weight, bias = refs[:3]
        out, activated_out, bias_out, out_bias, stack, whole = refs[3:]
        stack[...] = groups[...].astype(F32).reshape(fsdp_size, GROUP, width)
        in_group = lax.rem(lax.broadcasted_iota(jnp.int32, (fsdp_size * GROUP, 1), 0), GROUP)
        rows_low = jnp.where(in_group < slots, groups[...].astype(F32), 0.0).astype(BF)
        activated_out[...] = rows_low
        out[...] = dot_rt(rows_low, weight[...]) + bias[...]
        for k in range(fsdp_size):
            row = stack[k, slots : slots + 1, :]
            whole[:, k * shard_bias : (k + 1) * shard_bias] = row[:, :shard_bias]
            at = slice(k * shard_out_bias, (k + 1) * shard_out_bias)
            out_bias[:, at] = row[:, shard_bias : shard_bias + shard_out_bias]
        bias_out[...] = jnp.zeros_like(bias_out)
        for k in range(rep_size):

            @pl.when(r_ref[0] == k)
            def _():
                for t in range(3):
                    first = t * width + k * block
                    bias_out[:, t * padded : t * padded + block] = whole[:, first : first + block]

    line_modulation, line_activated, own_bias, output_bias_all = call(
        order,
        modulate_kernel,
        "modulate",
        [r_index],
        [line_rows, modulation_weight.T, modulation_bias.astype(F32)[None]],
        [
            ((fsdp_size * GROUP, columns), F32),
            ((fsdp_size * GROUP, width), BF),
            ((1, 3 * padded), F32),
            ((1, width), F32),
        ],
        2.0,
        scratch=[((fsdp_size, GROUP, width), F32), ((1, 3 * width), F32)],
        limit=24,
    )
    own_modulation = lax.all_to_all(line_modulation, "fsdp", 0, 0, tiled=True)

    unit_rows, unit_lanes = math.gcd(piece, shard_width), math.gcd(width, block_ff)
    units = []
    for u in range((piece // unit_rows) * (width // unit_lanes)):
        (a, b), (c, d) = divmod(u, width // unit_lanes), divmod(u, block_ff // unit_lanes)
        units.append(
            (
                a * unit_rows,
                slice(b * unit_lanes, (b + 1) * unit_lanes),
                c * unit_rows,
                slice(2 * block_ff + d * unit_lanes, 2 * block_ff + (d + 1) * unit_lanes),
            )
        )

    def feed_shard_kernel(r_ref, gate, up, down, out):
        for k in range(rep_size):

            @pl.when(r_ref[0] == k)
            def _():
                for j in range(fsdp_size):
                    source = slice(j * shard_ff + k * piece, j * shard_ff + (k + 1) * piece)
                    out[:, j * piece : (j + 1) * piece] = gate[:, source]
                    first = block_ff + j * piece
                    out[:, first : first + piece] = up[:, source]
                for a, lanes, c, packed_lanes in units:
                    out[c : c + unit_rows, packed_lanes] = down[
                        k * piece + a : k * piece + a + unit_rows, lanes
                    ]

    (feed_shard,) = call(
        order,
        feed_shard_kernel,
        "feed_shard",
        [r_index],
        [gate_weight, up_weight, down_weight],
        [((shard_width, 3 * block_ff), BF)],
        1.5,
        limit=16,
    )
    qkv_block = lax.all_gather(qkv_shard, "fsdp", axis=0, tiled=True)
    out_full = lax.all_gather(wait_for(output_weight, qkv_shard), "fsdp", axis=0, tiled=True)
    feed_block = lax.all_gather(feed_shard, "fsdp", axis=0, tiled=True)

    def norm_rows_kernel(*refs):
        out, columns_out, rows_out = refs[rep_size:]
        for j in range(rep_size):
            ref = refs[j]

            def step(at, ref=ref, j=j):
                normed, _ = normalize_keep(ref[at, :].astype(F32))
                out[pl.ds(j * count + at.start, CHUNK), :] = normed

            chunks(count, step)
            line = ref[count:, :].astype(F32)
            for q in range(4):
                rows_out[j, q : q + 1, :] = line[:1, q * count : (q + 1) * count]
            rows_out[j, 4:, :] = jnp.zeros((4, count), F32)
            columns_out[j] = rows_out[j].T

    normed_rows, place_columns, place_rows = call(
        order,
        norm_rows_kernel,
        "first_norm",
        [],
        token_rows,
        [((flat, width), F32), ((rep_size, count, 8), F32), ((rep_size, 8, count), F32)],
        6.0,
        limit=24,
    )
    pair_count = head_width // 4
    lane = np.arange(padded)
    in_head = lane % head_width
    lane_frequency = 10000.0 ** (-(in_head % pair_count) / pair_count)
    of_row = (lane < block) & (in_head < 2 * pair_count)
    of_column = (lane < block) & (in_head >= 2 * pair_count)
    angle = place_columns[:, :, 1:2] * np.where(of_row, lane_frequency, 0.0).astype(
        np.float32
    ) + place_columns[:, :, 2:3] * np.where(of_column, lane_frequency, 0.0).astype(np.float32)
    second = jnp.asarray(((in_head // pair_count) % 2 == 1).astype(np.float32))[None]
    cosine, sine = jnp.cos(angle), jnp.sin(angle)

    def modulation_kernel(arrived, modulation, sent):
        for k in range(fsdp_size):
            at = slice(k * columns, (k + 1) * columns)
            modulation[:, at] = arrived[k * GROUP : k * GROUP + slots, :]
        sent[:, : 2 * width] = modulation[:, : 2 * width]
        sent[:, 2 * width :] = modulation[:, 5 * width :]

    modulation, sent_modulation = call(
        order,
        modulation_kernel,
        "modulation",
        [],
        [wait_for(own_modulation, cosine, cotangent_rows[1:3])],
        [((slots, 6 * width), F32), ((slots, 3 * width), F32)],
        1.0,
        limit=8,
    )
    modulation_rows = gather(sent_modulation, "rep", rep_size)

    def head_mask(h):
        lanes = lax.broadcasted_iota(jnp.int32, (1, padded), 1)
        inside = (lanes >= h * head_width) & (lanes < (h + 1) * head_width)
        return jnp.where(inside, 1.0, 0.0).astype(BF)

    def probabilities(query_head, key, same):
        scores = jnp.where(same, dot_rt(query_head, key) * score_scale, -1e30)
        exponent = jnp.exp(scores - jnp.max(scores, axis=-1, keepdims=True))
        return exponent / jnp.sum(exponent, axis=-1, keepdims=True)

    def turn(values, cosine_row, sine_row, second_row, sense):
        before = pltpu.roll(values, pair_count, 1)
        after = pltpu.roll(values, padded - pair_count, 1)
        other = jnp.where(second_row > 0.5, before, -after)
        return values * cosine_row + (sense * other) * sine_row

    def attention_kernel(r_ref, *refs):
        modulations = refs[:rep_size]
        normed, weight, bias, cos_ref, sin_ref, second_ref, column_ref, row_ref = refs[
            rep_size : rep_size + 8
        ]
        hidden_all, wide, query_out, key_out, value_out, attended_out, modulation_stack = refs[
            rep_size + 8 :
        ]
        for j in range(rep_size):
            modulation_stack[j] = modulations[j][:, : 2 * width]
        for t in range(3):
            wide[:, t * padded : t * padded + block] = weight[:, t * block : (t + 1) * block]
            if padded > block:
                wide[:, t * padded + block : (t + 1) * padded] = jnp.zeros(
                    (width, padded - block), BF
                )

        def row(j, carry):
            first = pl.multiple_of(j * count, count)

            def step(at):
                here = pl.ds(pl.multiple_of(first + at.start, CHUNK), CHUNK)
                slot_of = column_ref[j, at, 0:1]
                scale = pick(modulation_stack[j], slot_of, width, width)
                shift = pick(modulation_stack[j], slot_of, 0, width)
                hidden_all[here, :] = (normed[here, :] * (1.0 + scale) + shift).astype(BF)

            chunks(count, step)
            projected = dot(hidden_all[pl.ds(first, count), :], wide[...]) + bias[...]
            cos_row, sin_row, second_row = cos_ref[j], sin_ref[j], second_ref[...]
            query = turn(projected[:, :padded], cos_row, sin_row, second_row, 1.0).astype(BF)
            key = turn(
                projected[:, padded : 2 * padded], cos_row, sin_row, second_row, 1.0
            ).astype(BF)
            value = projected[:, 2 * padded :].astype(BF)
            query_out[j], key_out[j], value_out[j] = query, key, value
            same = column_ref[j, :, 0:1] == row_ref[j, 0:1, :]
            total = jnp.zeros((count, padded), F32)
            for h in range(local_heads):
                mask = head_mask(h)
                probs = probabilities(query * mask, key, same)
                total = total + dot(probs.astype(BF), value * mask)
            owner = pl.ds(pl.multiple_of((r_ref[0] ^ j) * count, count), count)
            attended_out[owner, :] = total[:, :block].astype(BF)
            return carry

        lax.fori_loop(0, rep_size, row, 0)

    hidden_one_all, wide_weight, query_all, key_all, value_all, attended_heads = call(
        order,
        attention_kernel,
        "attention",
        [r_index],
        modulation_rows
        + [normed_rows, qkv_block, own_bias, cosine, sine, second, place_columns, place_rows],
        [((flat, width), BF), ((width, 3 * padded), BF)]
        + [((rep_size, count, padded), BF)] * 3
        + [((flat, block), BF)],
        22.0,
        scratch=[((rep_size, slots, 2 * width), F32)],
        limit=44,
    )
    own_heads = exchange(attended_heads, "rep")

    def feed_back_kernel(*refs):
        cotangents, modulations = refs[:rep_size], refs[rep_size : 2 * rep_size]
        columns_ref, out = refs[2 * rep_size :]
        for j in range(rep_size):

            def step(at, j=j):
                masked = cotangents[j][at, :].astype(F32) * columns_ref[j, at, 3:4]
                gate = pick(modulations[j], columns_ref[j, at, 0:1], 2 * width, width)
                out[pl.ds(j * count + at.start, CHUNK), :] = (gate * masked).astype(BF)

            chunks(count, step)

    (feed_back_all,) = call(
        order,
        feed_back_kernel,
        "feed_back",
        [],
        cotangent_rows + modulation_rows + [place_columns],
        [((flat, width), BF)],
        4.0,
        limit=24,
    )

    def middle_kernel(
        heads, weight, bias, tokens_ref, modulation, places, branch, normed_out, inverse_out,
        hidden, attended,
    ):
        for k in range(rep_size):
            attended[:, k * block : (k + 1) * block] = heads[k * count : (k + 1) * count, :]
        branch[...] = dot(attended[...], weight[...]) + bias[...]

        def step(here):
            slot_of = places[0, here, 0:1]
            gate = pick(modulation, slot_of, 2 * width, width)
            middle = tokens_ref[here, :].astype(F32) + gate * branch[here, :]
            normed, inverse = normalize_keep(middle)
            normed_out[here, :] = normed
            inverse_out[here, :] = inverse
            scale = pick(modulation, slot_of, 4 * width, width)
            hidden[here, :] = (
                normed * (1.0 + scale) + pick(modulation, slot_of, 3 * width, width)
            ).astype(BF)

        chunks(count, step)

    branch, normed_two, inverse_two, hidden_two, attended = call(
        order,
        middle_kernel,
        "second_norm",
        [],
        [own_heads, out_full, output_bias_all, tokens, modulation, place_columns],
        [((count, width), F32), ((count, width), F32), ((count, 1), F32)]
        + [((count, width), BF)] * 2,
        7.0,
        limit=24,
    )
    hidden_two_rows = gather(hidden_two, "rep", rep_size)
    attended_rows = gather(wait_for(attended, hidden_two_rows), "rep", rep_size)

    step_ff = 256 if block_ff % 256 == 0 else 128

    def feed_kernel(*refs):
        back_all, weight = refs[rep_size : rep_size + 2]
        outs = refs[rep_size + 2 :]
        hidden_all, three, both_back, down = outs[:4]
        parts_out, parts = outs[4:-1], outs[-1]
        for j in range(rep_size):
            hidden_all[j * count : (j + 1) * count, :] = refs[j][...]
        for j in range(fsdp_size):
            for a, lanes, c, packed_lanes in units:
                from_row, to_row = j * shard_width + c, j * piece + a
                down[to_row : to_row + unit_rows, lanes] = weight[
                    from_row : from_row + unit_rows, packed_lanes
                ]

        def row(j, carry):
            here = pl.ds(pl.multiple_of(j * count, count), count)
            hidden, back = hidden_all[here, :], back_all[here, :]
            for c in range(block_ff // step_ff):
                at = slice(c * step_ff, (c + 1) * step_ff)
                up_at = slice(block_ff + c * step_ff, block_ff + (c + 1) * step_ff)
                gate = dot(hidden, weight[:, at])
                up = dot(hidden, weight[:, up_at])
                hidden_back = dot_rt(back, down[at, :])
                sigmoid = jax.nn.sigmoid(gate)
                silu = gate * sigmoid
                three[here, at] = (silu * up).astype(BF)
                slope = sigmoid * (1.0 + gate * (1.0 - sigmoid))
                both_back[here, at] = (hidden_back * up * slope).astype(BF)
                both_back[here, up_at] = (hidden_back * silu).astype(BF)
            parts[j] = dot_rt(both_back[here, :], weight[:, : 2 * block_ff])
            return carry

        lax.fori_loop(0, rep_size, row, 0)
        store_parts(parts, parts_out)

    hidden_two_all, hidden_three, both_back, down_block, *back_parts = call(
        order,
        feed_kernel,
        "feed_forward",
        [],
        hidden_two_rows + [feed_back_all, feed_block],
        [
            ((flat, width), BF),
            ((flat, block_ff), BF),
            ((flat, 2 * block_ff), BF),
            ((block_ff, width), BF),
        ]
        + part_shapes(rep_size, count, width),
        20.0,
        scratch=[((rep_size, count, width), F32)],
        limit=44,
    )
    back_addends = send(back_parts, "rep", rep_size)

    def sent_gradient(value):
        return lax.psum_scatter(value, "fsdp", scatter_dimension=0, tiled=True)

    def feed_gradient_kernel(hidden_all, back_all, three, both_back, out):
        step_width = width // 3
        for m in range(3):
            at = slice(m * step_width, (m + 1) * step_width)
            out[at, : 2 * block_ff] = dot_lt(hidden_all[:, at], both_back[...]).astype(BF)
        together = max(1, fsdp_size // 2)
        for first in range(0, fsdp_size, together):
            gradient = dot_lt(
                three[:, first * piece : (first + together) * piece], back_all[...]
            ).astype(BF)
            for j in range(together):
                for a, lanes, c, packed_lanes in units:
                    to_row = (first + j) * shard_width + c
                    out[to_row : to_row + unit_rows, packed_lanes] = gradient[
                        j * piece + a : j * piece + a + unit_rows, lanes
                    ]

    (feed_gradient,) = call(
        order,
        feed_gradient_kernel,
        "feed_gradient",
        [],
        [hidden_two_all, feed_back_all, hidden_three, both_back],
        [((width, 3 * block_ff), BF)],
        9.0,
        limit=36,
    )
    feed_sum = sent_gradient(feed_gradient)

    def feed_out_kernel(three, down, *outs):
        def make(j):
            return dot(three[j * count : (j + 1) * count, :], down[...])

        outs[0][...] = make(0)
        for j in range(1, rep_size):
            outs[j][...] = make(j).astype(BF)

    feed_parts = call(
        order,
        feed_out_kernel,
        "feed_out",
        [],
        [wait_for(hidden_three, attended_rows), down_block],
        [((count, width), F32)] + [((count, width), BF)] * (rep_size - 1),
        0.1,
        limit=24,
    )

    def middle_back_kernel(*refs):
        addends = refs[:rep_size]
        cotangent_ref, places, modulation, normed_ref, inverse_ref, branch_ref, weight = refs[
            rep_size : rep_size + 7
        ]
        middle_back, sums_out, bias_out, heads_out, backs_out, sums, branch_back = refs[
            rep_size + 7 :
        ]
        sums[...] = jnp.zeros_like(sums)

        def step(here):
            slot_of = places[0, here, 0:1]
            upstream = addends[0][here, :]
            for ref in addends[1:]:
                upstream = upstream + ref[here, :].astype(F32)
            normed = normed_ref[here, :]
            masked = cotangent_ref[here, :].astype(F32) * places[0, here, 3:4]
            scale = pick(modulation, slot_of, 4 * width, width)
            back = masked + normalize_back(normed, inverse_ref[here, :], upstream * (1.0 + scale))
            middle_back[here, :] = back
            gate = pick(modulation, slot_of, 2 * width, width)
            low = (back * gate).astype(BF)
            branch_back[here, :] = low
            add_slots(sums, 0, slots, slot_of, back * branch_ref[here, :])
            add_slots(sums, slots, slots, slot_of, upstream)
            add_slots(sums, 2 * slots, slots, slot_of, upstream * normed)
            sums[3 * slots] += jnp.sum(low.astype(F32).reshape(CHUNK // 8, 8, width), axis=0)

        chunks(count, step)
        total = jnp.sum(sums[...], axis=1)
        sums_out[...] = total[: 3 * slots]
        bias_out[...] = total[3 * slots :]
        heads = dot_rt(branch_back[...], weight[...])
        for k in range(rep_size):
            to, at = slice(k * count, (k + 1) * count), slice(k * block, (k + 1) * block)
            heads_out[to, :] = heads[:, at].astype(BF)
            backs_out[to, :] = branch_back[:, at]

    middle_back, middle_sums, output_bias_sum, sent_heads, sent_backs = call(
        order,
        middle_back_kernel,
        "second_norm_back",
        [],
        back_addends
        + [cotangent, place_columns, modulation, normed_two, inverse_two, branch, out_full],
        [
            ((count, width), F32),
            ((3 * slots, width), F32),
            ((1, width), F32),
            ((flat, block), BF),
            ((flat, block), BF),
        ],
        6.0,
        scratch=[((3 * slots + 1, 8, width), F32), ((count, width), BF)],
        limit=28,
    )
    heads_back = exchange(sent_heads, "rep")
    branch_backs = exchange(wait_for(sent_backs, heads_back), "rep")
    feed_addends = send(wait_for(list(feed_parts), heads_back), "rep", rep_size)
    all_activated = gather(wait_for(line_activated, heads_back), "rep", rep_size)

    def attention_back_kernel(r_ref, *refs):
        heads, query_ref, key_ref, value_ref, wide, cos_ref, sin_ref, second_ref = refs[:8]
        column_ref, row_ref, projected_back, bias_out = refs[8:12]
        parts_out = refs[12:-2]
        parts, head_stack = refs[-2:]
        if padded > block:
            head_stack[:, :, block:] = jnp.zeros((rep_size, count, padded - block), BF)
        for j in range(rep_size):
            owner = pl.ds(pl.multiple_of((r_ref[0] ^ j) * count, count), count)
            head_stack[j, :, :block] = heads[owner, :]
        bias_out[...] = jnp.zeros_like(bias_out)

        def row(j, carry):
            here = pl.ds(pl.multiple_of(j * count, count), count)
            query, key, value, back = query_ref[j], key_ref[j], value_ref[j], head_stack[j]
            same = column_ref[j, :, 0:1] == row_ref[j, 0:1, :]
            query_back = jnp.zeros((count, padded), F32)
            key_back = jnp.zeros((count, padded), F32)
            value_back = jnp.zeros((count, padded), F32)
            for h in range(local_heads):
                mask = head_mask(h)
                query_head, back_head = query * mask, back * mask
                probs = probabilities(query_head, key, same)
                probs_back = dot_rt(back_head, value)
                scores_back = (
                    probs
                    * (probs_back - jnp.sum(probs * probs_back, axis=-1, keepdims=True))
                ).astype(BF)
                value_back = value_back + dot_lt(probs.astype(BF), back_head)
                query_back = query_back + dot(scores_back, key * mask)
                key_back = key_back + dot_lt(scores_back, query_head)
            cos_row, sin_row, second_row = cos_ref[j], sin_ref[j], second_ref[...]
            query_back = turn(query_back * score_scale, cos_row, sin_row, second_row, -1.0)
            key_back = turn(key_back * score_scale, cos_row, sin_row, second_row, -1.0)
            low = [value.astype(BF) for value in (query_back, key_back, value_back)]
            for t in range(3):
                projected_back[here, t * block : (t + 1) * block] = low[t][:, :block]
                bias_out[:, t * padded : (t + 1) * padded] += jnp.sum(
                    low[t].astype(F32), axis=0, keepdims=True
                )
            parts[j] = dot_rt(jnp.concatenate(low, axis=1), wide[...])
            return carry

        lax.fori_loop(0, rep_size, row, 0)
        store_parts(parts, parts_out)

    projected_back, projection_bias_sum, *one_parts = call(
        order,
        attention_back_kernel,
        "attention_back",
        [r_index],
        [heads_back, query_all, key_all, value_all, wide_weight, cosine, sine, second]
        + [place_columns, place_rows],
        [((flat, 3 * block), BF), ((1, 3 * padded), F32)] + part_shapes(rep_size, count, width),
        23.0,
        scratch=[((rep_size, count, width), F32), ((rep_size, count, padded), BF)],
        limit=44,
    )
    one_addends = send(one_parts, "rep", rep_size)

    def attention_gradient_kernel(r_ref, *refs):
        hidden_all, back, backs = refs[:3]
        heads = refs[3 : 3 + rep_size]
        out, head_stack, back_stack = refs[3 + rep_size :]
        for j in range(rep_size):
            owner = pl.ds(pl.multiple_of((r_ref[0] ^ j) * count, count), count)
            head_stack[j * count : (j + 1) * count, :] = heads[j][...]
            back_stack[j * count : (j + 1) * count, :] = backs[owner, :]
        step_width = width // 3
        for m in range(3):
            at = slice(m * step_width, (m + 1) * step_width)
            out[at, : 3 * block] = dot_lt(hidden_all[:, at], back[...]).astype(BF)
            out[at, 3 * block :] = dot_lt(head_stack[:, at], back_stack[...]).astype(BF)

    (attention_gradient,) = call(
        order,
        attention_gradient_kernel,
        "attention_gradient",
        [r_index],
        [wait_for(hidden_one_all, feed_addends, all_activated), projected_back, branch_backs]
        + attended_rows,
        [((width, 4 * block), BF)],
        5.0,
        scratch=[((flat, width), BF), ((flat, block), BF)],
        limit=32,
    )
    attention_sum = sent_gradient(attention_gradient)

    def output_kernel(*refs):
        feeds = refs[:rep_size]
        tokens_ref, branch_ref, cotangent_ref, places, modulation = refs[rep_size : rep_size + 5]
        block_out, sums_out, sums = refs[rep_size + 5 :]
        sums[...] = jnp.zeros_like(sums)

        def step(here):
            slot_of = places[0, here, 0:1]
            feed = feeds[0][here, :]
            for ref in feeds[1:]:
                feed = feed + ref[here, :].astype(F32)
            gate_one = pick(modulation, slot_of, 2 * width, width)
            middle = tokens_ref[here, :].astype(F32) + gate_one * branch_ref[here, :]
            gate_two = pick(modulation, slot_of, 5 * width, width)
            block_out[here, :] = (middle + gate_two * feed).astype(BF)
            masked = cotangent_ref[here, :].astype(F32) * places[0, here, 3:4]
            add_slots(sums, 0, slots, slot_of, masked * feed)

        chunks(count, step)
        sums_out[...] = jnp.sum(sums[...], axis=1)

    block_output, gate_two_sums = call(
        order,
        output_kernel,
        "layer_output",
        [],
        feed_addends + [tokens, branch, cotangent, place_columns, modulation],
        [((count, width), BF), ((slots, width), F32)],
        0.1,
        scratch=[((slots, 8, width), F32)],
        limit=16,
    )

    def first_back_kernel(r_ref, *refs):
        addends = refs[:rep_size]
        tokens_ref, back_ref, modulation, places, middle_ref, gate_two_ref, bias, out_bias = refs[
            rep_size : rep_size + 8
        ]
        gradient, back_blocks, sums, whole, whole_bias, stack = refs[rep_size + 8 :]
        sums[...] = jnp.zeros_like(sums)

        def step(here):
            slot_of = places[0, here, 0:1]
            upstream = addends[0][here, :]
            for ref in addends[1:]:
                upstream = upstream + ref[here, :].astype(F32)
            normed, inverse = normalize_keep(tokens_ref[here, :].astype(F32))
            scale = pick(modulation, slot_of, width, width)
            gradient[here, :] = back_ref[here, :] + normalize_back(
                normed, inverse, upstream * (1.0 + scale)
            )
            add_slots(sums, 0, slots, slot_of, upstream)
            add_slots(sums, slots, slots, slot_of, upstream * normed)

        chunks(count, step)
        total = jnp.sum(sums[...], axis=1)
        whole[:, :width] = total[:slots]
        whole[:, width : 2 * width] = total[slots:]
        for t in range(3):
            at = slice((2 + t) * width, (3 + t) * width)
            whole[:, at] = middle_ref[t * slots : (t + 1) * slots, :]
        whole[:, 5 * width :] = gate_two_ref[...]
        whole_bias[...] = jnp.zeros_like(whole_bias)
        for k in range(rep_size):

            @pl.when(r_ref[0] == k)
            def _():
                for t in range(3):
                    first = t * width + k * block
                    whole_bias[:, first : first + block] = bias[:, t * padded : t * padded + block]

        stack[...] = jnp.zeros_like(stack)
        for k in range(fsdp_size):
            stack[k, :slots, :] = whole[:, k * columns : (k + 1) * columns]
            at = slice(k * shard_bias, (k + 1) * shard_bias)
            stack[k, slots : slots + 1, :shard_bias] = whole_bias[:, at]
            at = slice(k * shard_out_bias, (k + 1) * shard_out_bias)
            lanes = slice(shard_bias, shard_bias + shard_out_bias)
            stack[k, slots : slots + 1, lanes] = out_bias[:, at]
        back_blocks[...] = stack[...].reshape(fsdp_size * GROUP, columns).astype(BF)

    tokens_gradient, back_blocks = call(
        order,
        first_back_kernel,
        "first_norm_back",
        [r_index],
        one_addends
        + [tokens, middle_back, modulation, place_columns, middle_sums, gate_two_sums]
        + [projection_bias_sum, output_bias_sum],
        [((count, width), F32), ((fsdp_size * GROUP, columns), BF)],
        4.0,
        scratch=[
            ((2 * slots, 8, width), F32),
            ((slots, 6 * width), F32),
            ((1, 3 * width), F32),
            ((fsdp_size, GROUP, columns), F32),
        ],
        limit=20,
    )

    line_backs = exchange(back_blocks, "fsdp")
    feed_sums = gather(wait_for(feed_sum, one_addends), "rep", rep_size)

    def conditioning_kernel(groups, weight, out, line_out):
        stack = groups[...].astype(F32)
        bias = jnp.sum(stack.reshape(fsdp_size, GROUP, columns), axis=0)[slots : slots + 1]
        row_ids = lax.broadcasted_iota(jnp.int32, (fsdp_size * GROUP, 1), 0)
        rows_back = jnp.where(lax.rem(row_ids, GROUP) < slots, stack, 0.0)
        line_out[...] = jnp.where(row_ids == slots, bias, rows_back).astype(BF)
        result = dot(rows_back.astype(BF), weight[...])
        for k in range(fsdp_size):
            out[k * slots : (k + 1) * slots, :] = result[k * GROUP : k * GROUP + slots, :]

    activated_backs, line_back = call(
        order,
        conditioning_kernel,
        "conditioning_back",
        [],
        [wait_for(line_backs, feed_sums[1]), modulation_weight.T],
        [((fsdp_size * slots, width), F32), ((fsdp_size * GROUP, columns), BF)],
        2.0,
        limit=24,
    )
    activated_backs = exchange(activated_backs, "fsdp")
    all_backs = gather(line_back, "rep", rep_size)
    activated_back = jnp.sum(activated_backs.reshape(fsdp_size, slots, width), axis=0)
    conditioning_gradient = activated_back.reshape(rows, slots, width) * silu_slope(cond_float)

    def table_kernel(*refs):
        activateds, backs = refs[:rep_size], refs[rep_size : 2 * rep_size]
        table, table_bias, bias, activated_stack, back_stack = refs[2 * rep_size :]
        line = fsdp_size * GROUP
        total = jnp.zeros((1, columns), F32)
        for j in range(rep_size):
            activated_stack[j * line : (j + 1) * line, :] = activateds[j][...]
            back_stack[j * line : (j + 1) * line, :] = backs[j][...]
            total = total + backs[j][...].astype(F32)[slots : slots + 1, :]
        bias[...] = total
        back = back_stack[...].astype(F32)
        in_group = lax.rem(lax.broadcasted_iota(jnp.int32, (rep_size * line, 1), 0), GROUP)
        table_bias[...] = jnp.sum(
            jnp.where(in_group < slots, back, 0.0), axis=0, keepdims=True
        )
        table[...] = dot_lt(back_stack[...], activated_stack[...])

    table_gradient, table_bias_gradient, bias_gradients = call(
        order,
        table_kernel,
        "table_gradient",
        [],
        all_activated + all_backs,
        [((columns, width), F32), ((1, columns), F32), ((1, columns), F32)],
        3.0,
        scratch=[
            ((rep_size * fsdp_size * GROUP, width), BF),
            ((rep_size * fsdp_size * GROUP, columns), BF),
        ],
        limit=24,
    )

    def feed_blocks_kernel(r_ref, *refs):
        gate_out, up_out, down_out, stack = refs[rep_size:]
        for j in range(rep_size):
            stack[j] = refs[j][...].astype(F32)
        for k in range(rep_size):
            here = r_ref[0] ^ k
            for j in range(fsdp_size):
                target = slice(j * shard_ff + k * piece, j * shard_ff + (k + 1) * piece)
                first = block_ff + j * piece
                gate_out[:, target] = stack[here, :, j * piece : (j + 1) * piece]
                up_out[:, target] = stack[here, :, first : first + piece]
            for a, lanes, c, packed_lanes in units:
                to_row = k * piece + a
                down_out[to_row : to_row + unit_rows, lanes] = stack[
                    here, c : c + unit_rows, packed_lanes
                ]

    gate_gradient, up_gradient, down_gradient = call(
        order,
        feed_blocks_kernel,
        "feed_blocks",
        [r_index],
        feed_sums,
        [((shard_width, fsdp_size * shard_ff), F32)] * 2 + [((shard_ff, width), F32)],
        5.0,
        scratch=[((rep_size, shard_width, 3 * block_ff), F32)],
        limit=24,
    )

    def attention_blocks_kernel(r_ref, *refs):
        projection_out, output_out, stack = refs[rep_size:]
        for j in range(rep_size):
            stack[j] = refs[j][...].astype(F32)
        for k in range(rep_size):
            here = r_ref[0] ^ k
            for t in range(3):
                first = t * width + k * block
                projection_out[:, first : first + block] = stack[
                    here, :, t * block : (t + 1) * block
                ]
            output_out[:, k * block : (k + 1) * block] = stack[here, :, 3 * block :]

    projection_gradient, output_gradient = call(
        order,
        attention_blocks_kernel,
        "attention_blocks",
        [r_index],
        gather(attention_sum, "rep", rep_size),
        [((shard_width, 3 * width), F32), ((shard_width, width), F32)],
        3.0,
        scratch=[((rep_size, shard_width, 4 * block), F32)],
        limit=24,
    )
    return (
        block_output[None],
        tokens_gradient[None],
        conditioning_gradient,
        table_gradient.T,
        table_bias_gradient[0],
        projection_gradient,
        bias_gradients[0, :shard_bias],
        output_gradient,
        bias_gradients[0, shard_bias : shard_bias + shard_out_bias],
        gate_gradient,
        up_gradient,
        down_gradient,
    )


def solution(mesh):
    sizes = dict(mesh.shape)

    def body(*arrays):
        return on_device(sizes["rep"], sizes["fsdp"], *arrays)

    rows = ("rep", "fsdp")
    in_specs = (
        P(rows, None, None),
        P(rows, None, None),
        P(rows, None),
        P(rows, None),
        P(rows, None),
        P(rows, None),
        P(None, "fsdp"),
        P("fsdp"),
        P("fsdp", None),
        P("fsdp"),
        P("fsdp", None),
        P("fsdp"),
        P("fsdp", None),
        P("fsdp", None),
        P("fsdp", None),
        P(rows, None, None),
    )
    out_specs = (
        P(rows, None, None),
        P(rows, None, None),
        P(rows, None, None),
        P(None, "fsdp"),
        P("fsdp"),
        P("fsdp", None),
        P("fsdp"),
        P("fsdp", None),
        P("fsdp"),
        P("fsdp", None),
        P("fsdp", None),
        P("fsdp", None),
    )
    return jax.shard_map(
        body, mesh=mesh, in_specs=in_specs, out_specs=out_specs, check_vma=False
    )
```

```python
import math

import jax
import jax.numpy as jnp
import numpy as np
from jax import lax
from jax.experimental import pallas as pl
from jax.experimental.pallas import tpu as pltpu
from jax.sharding import PartitionSpec as P

HEADS = 16
BF = jnp.bfloat16
F32 = jnp.float32
LANES = 128
CHUNK = 32
GROUP = 8


def wait_for(value, *others):
    return lax.optimization_barrier((value, others))[0]


def swap_with(value, axis, size, bit):
    return lax.ppermute(value, axis, [(i, i ^ bit) for i in range(size)])


def gather(value, axis, size):
    return [value] + [swap_with(value, axis, size, j) for j in range(1, size)]


def send(values, axis, size):
    return [values[0]] + [swap_with(values[j], axis, size, j) for j in range(1, size)]


def exchange(value, axis):
    return lax.all_to_all(value, axis, 0, 0, tiled=True)


def whole_block(array):
    zeros = (0,) * len(array.shape)
    return pl.BlockSpec(array.shape, lambda i: zeros, pipeline_mode=pl.Buffered(1))


def call(order, body, name, scalars, arrays, outs, micros, scratch=(), limit=48, near=()):
    shapes = [pltpu.HBM(shape, dtype) for shape, dtype in outs]
    if order:
        first, _ = lax.optimization_barrier((arrays[0], order.pop()))
        arrays = [first] + list(arrays[1:])
    arrays = [
        array if n in near else pltpu.with_memory_space_constraint(array, pltpu.HBM)
        for n, array in enumerate(arrays)
    ]
    results = pl.pallas_call(
        body,
        name=name,
        grid=(1,),
        out_shape=shapes,
        in_specs=[pl.BlockSpec(memory_space=pltpu.SMEM)] * len(scalars)
        + [whole_block(array) for array in arrays],
        out_specs=[whole_block(shape) for shape in shapes],
        scratch_shapes=[pltpu.VMEM(shape, dtype) for shape, dtype in scratch],
        compiler_params=pltpu.CompilerParams(vmem_limit_bytes=limit << 20),
        cost_estimate=pl.CostEstimate(
            flops=int(micros * 3e9), bytes_accessed=int(micros * 9e6), transcendentals=0
        ),
    )(*scalars, *arrays)
    order.append(results[0])
    return results


def part_shapes(size, tokens, width):
    return [((tokens, width), F32)] + [((tokens, width), BF)] * (size - 1)


def store_parts(parts, refs):
    refs[0][...] = parts[0]
    for j in range(1, len(refs)):
        refs[j][...] = parts[j].astype(BF)


def dot(left, right):
    return jnp.dot(left, right, preferred_element_type=F32)


def dot_rt(left, right):
    return lax.dot_general(left, right, (((1,), (1,)), ((), ())), preferred_element_type=F32)


def dot_lt(left, right):
    return lax.dot_general(left, right, (((0,), (0,)), ((), ())), preferred_element_type=F32)


def pick(modulation, slot_of, first, width):
    total = jnp.zeros((slot_of.shape[0], width), F32)
    for k in range(modulation.shape[0]):
        total = jnp.where(slot_of == k, modulation[k : k + 1, first : first + width], total)
    return total


def normalize_keep(values):
    centered = values - jnp.mean(values, axis=-1, keepdims=True)
    variance = jnp.mean(centered * centered, axis=-1, keepdims=True)
    inverse = lax.rsqrt(variance + 1e-06)
    return centered * inverse, inverse


def normalize_back(normed, inverse, upstream):
    return inverse * (
        upstream
        - jnp.mean(upstream, axis=-1, keepdims=True)
        - normed * jnp.mean(upstream * normed, axis=-1, keepdims=True)
    )


def add_slots(sums, base, count, slot_of, values):
    rows, width = values.shape
    for k in range(count):
        chosen = jnp.where(slot_of == k, values, 0.0)
        sums[base + k] += jnp.sum(chosen.reshape(rows // 8, 8, width), axis=0)


def chunks(tokens, step):
    def body(i, carry):
        step(pl.ds(pl.multiple_of(i * CHUNK, CHUNK), CHUNK))
        return carry

    lax.fori_loop(0, tokens // CHUNK, body, 0)


def silu_slope(values):
    sigmoid = jax.nn.sigmoid(values)
    return sigmoid * (1.0 + values * (1.0 - sigmoid))


def on_device(
    rep_size,
    fsdp_size,
    tokens,
    conditioning,
    segment_ids,
    heights,
    widths,
    pad_mask,
    modulation_weight,
    modulation_bias,
    projection_weight,
    projection_bias,
    output_weight,
    output_bias,
    gate_weight,
    up_weight,
    down_weight,
    cotangent,
):
    rows, count, width = tokens.shape
    assert rows == 1
    slots = conditioning.shape[1]
    head_width = width // HEADS
    local_heads = HEADS // rep_size
    block = width // rep_size
    padded = -(-block // LANES) * LANES
    score_scale = 1.0 / math.sqrt(head_width)
    shard_ff = down_weight.shape[0]
    piece = shard_ff // rep_size
    block_ff = fsdp_size * piece
    shard_width = projection_weight.shape[0]
    columns = modulation_weight.shape[1]
    flat = rep_size * count
    others = rep_size - 1
    r = lax.axis_index("rep")
    r_index = r.reshape(1).astype(jnp.int32)
    tokens, cotangent = tokens[0], cotangent[0]
    order = []

    def qkv_shard_kernel(r_ref, projection, out):
        for k in range(rep_size):

            @pl.when(r_ref[0] == k)
            def _():
                for t in range(3):
                    first = t * width + k * block
                    out[:, t * block : (t + 1) * block] = projection[:, first : first + block]

    (qkv_shard,) = call(
        order,
        qkv_shard_kernel,
        "qkv_shard",
        [r_index],
        [projection_weight],
        [((shard_width, 3 * block), BF)],
        1.5,
        limit=16,
    )

    slot_ids = jnp.arange(slots, dtype=jnp.int32)
    member_ints = (segment_ids[:, :, None] == slot_ids).astype(jnp.int32)
    before_ints = (slot_ids < segment_ids[:, :, None]).astype(jnp.int32)
    starts = jnp.sum(before_ints * (heights * widths)[:, None, :], axis=2)
    offsets = jnp.arange(count, dtype=jnp.int32)[None, :] - starts
    row_width = jnp.sum(member_ints * widths[:, None, :], axis=2)
    places = jnp.concatenate(
        [segment_ids, offsets // row_width, offsets % row_width, pad_mask], axis=1
    ).astype(BF)
    places = jnp.pad(places, ((0, GROUP - 1), (0, width - 4 * count)))
    token_rows = gather(jnp.concatenate([tokens, places], axis=0), "rep", rep_size)
    cotangent_rows = gather(wait_for(cotangent, token_rows), "rep", rep_size)

    cond_float = conditioning.astype(F32)
    activated = jax.nn.silu(cond_float).astype(BF).reshape(slots, width)
    shard_bias, shard_out_bias = projection_bias.shape[0], output_bias.shape[0]
    bias_row = jnp.pad(
        jnp.concatenate([projection_bias, output_bias]), (0, width - shard_bias - shard_out_bias)
    )[None]
    group_rows = jnp.concatenate(
        [activated, bias_row, jnp.zeros((GROUP - slots - 1, width), BF)], axis=0
    )
    line_rows = lax.all_gather(group_rows, "fsdp", axis=0, tiled=True)

    def modulate_kernel(r_ref, *refs):
        groups, weight, bias = refs[:3]
        out, activated_out, bias_out, out_bias, stack, whole = refs[3:]
        stack[...] = groups[...].astype(F32).reshape(fsdp_size, GROUP, width)
        in_group = lax.rem(lax.broadcasted_iota(jnp.int32, (fsdp_size * GROUP, 1), 0), GROUP)
        rows_low = jnp.where(in_group < slots, groups[...].astype(F32), 0.0).astype(BF)
        activated_out[...] = rows_low
        out[...] = dot_rt(rows_low, weight[...]) + bias[...]
        for k in range(fsdp_size):
            row = stack[k, slots : slots + 1, :]
            whole[:, k * shard_bias : (k + 1) * shard_bias] = row[:, :shard_bias]
            at = slice(k * shard_out_bias, (k + 1) * shard_out_bias)
            out_bias[:, at] = row[:, shard_bias : shard_bias + shard_out_bias]
        bias_out[...] = jnp.zeros_like(bias_out)
        for k in range(rep_size):

            @pl.when(r_ref[0] == k)
            def _():
                for t in range(3):
                    first = t * width + k * block
                    bias_out[:, t * padded : t * padded + block] = whole[:, first : first + block]

    line_modulation, line_activated, own_bias, output_bias_all = call(
        order,
        modulate_kernel,
        "modulate",
        [r_index],
        [line_rows, modulation_weight.T, modulation_bias.astype(F32)[None]],
        [
            ((fsdp_size * GROUP, columns), F32),
            ((fsdp_size * GROUP, width), BF),
            ((1, 3 * padded), F32),
            ((1, width), F32),
        ],
        2.0,
        scratch=[((fsdp_size, GROUP, width), F32), ((1, 3 * width), F32)],
        limit=24,
    )
    own_modulation = lax.all_to_all(line_modulation, "fsdp", 0, 0, tiled=True)

    unit_rows, unit_lanes = math.gcd(piece, shard_width), math.gcd(width, block_ff)
    units = []
    for u in range((piece // unit_rows) * (width // unit_lanes)):
        (a, b), (c, d) = divmod(u, width // unit_lanes), divmod(u, block_ff // unit_lanes)
        units.append(
            (
                a * unit_rows,
                slice(b * unit_lanes, (b + 1) * unit_lanes),
                c * unit_rows,
                slice(2 * block_ff + d * unit_lanes, 2 * block_ff + (d + 1) * unit_lanes),
            )
        )

    def feed_shard_kernel(r_ref, gate, up, down, out):
        for k in range(rep_size):

            @pl.when(r_ref[0] == k)
            def _():
                for j in range(fsdp_size):
                    source = slice(j * shard_ff + k * piece, j * shard_ff + (k + 1) * piece)
                    out[:, j * piece : (j + 1) * piece] = gate[:, source]
                    first = block_ff + j * piece
                    out[:, first : first + piece] = up[:, source]
                for a, lanes, c, packed_lanes in units:
                    out[c : c + unit_rows, packed_lanes] = down[
                        k * piece + a : k * piece + a + unit_rows, lanes
                    ]

    (feed_shard,) = call(
        order,
        feed_shard_kernel,
        "feed_shard",
        [r_index],
        [gate_weight, up_weight, down_weight],
        [((shard_width, 3 * block_ff), BF)],
        1.5,
        limit=16,
    )
    qkv_block = lax.all_gather(qkv_shard, "fsdp", axis=0, tiled=True)
    out_full = lax.all_gather(wait_for(output_weight, qkv_shard), "fsdp", axis=0, tiled=True)
    feed_block = lax.all_gather(feed_shard, "fsdp", axis=0, tiled=True)

    def norm_rows_kernel(*refs):
        out, columns_out, rows_out = refs[rep_size:]
        for j in range(rep_size):
            ref = refs[j]

            def step(at, ref=ref, j=j):
                normed, _ = normalize_keep(ref[at, :].astype(F32))
                out[pl.ds(j * count + at.start, CHUNK), :] = normed

            chunks(count, step)
            line = ref[count:, :].astype(F32)
            for q in range(4):
                rows_out[j, q : q + 1, :] = line[:1, q * count : (q + 1) * count]
            rows_out[j, 4:, :] = jnp.zeros((4, count), F32)
            columns_out[j] = rows_out[j].T

    normed_rows, place_columns, place_rows = call(
        order,
        norm_rows_kernel,
        "first_norm",
        [],
        token_rows,
        [((flat, width), F32), ((rep_size, count, 8), F32), ((rep_size, 8, count), F32)],
        6.0,
        limit=24,
        near=range(1, rep_size),
    )
    pair_count = head_width // 4
    most_rows, most_columns = count // 4, 32
    lane = np.arange(padded)
    in_head = lane % head_width
    lane_frequency = 10000.0 ** (-(in_head % pair_count) / pair_count)
    of_row = (lane < block) & (in_head < 2 * pair_count)
    of_column = (lane < block) & (in_head >= 2 * pair_count)
    sign = np.where((in_head // pair_count) % 2 == 1, 1.0, -1.0)
    row_angle = np.arange(most_rows)[:, None] * lane_frequency
    column_angle = np.arange(most_columns)[:, None] * lane_frequency
    tables = np.concatenate(
        [
            np.concatenate(
                [
                    np.where(of_row, np.cos(row_angle), 0.0),
                    np.where(of_column, np.cos(column_angle), 0.0),
                ]
            ),
            np.concatenate(
                [
                    np.where(of_row, sign * np.sin(row_angle), 0.0),
                    np.where(of_column, sign * np.sin(column_angle), 0.0),
                ]
            ),
        ],
        axis=1,
    ).astype(np.float32)
    pieces, left = [], tables
    for _ in range(3):
        pieces.append(left.astype(jnp.bfloat16))
        left = left - pieces[-1].astype(np.float32)
    tables = jnp.asarray(np.stack(pieces))

    def rotary(tables_ref, places):
        numbers = lax.broadcasted_iota(jnp.int32, (count, most_rows + most_columns), 1).astype(F32)
        is_row = (numbers < most_rows) & (numbers == places[:, 1:2])
        is_column = (numbers >= most_rows) & (numbers - most_rows == places[:, 2:3])
        chosen = jnp.where(is_row | is_column, 1.0, 0.0).astype(BF)
        both = dot(chosen, tables_ref[2]) + dot(chosen, tables_ref[1]) + dot(chosen, tables_ref[0])
        return both[:, :padded], both[:, padded:]

    def modulation_kernel(arrived, modulation, sent):
        for k in range(fsdp_size):
            at = slice(k * columns, (k + 1) * columns)
            modulation[:, at] = arrived[k * GROUP : k * GROUP + slots, :]
        sent[:, : 2 * width] = modulation[:, : 2 * width]
        sent[:, 2 * width :] = modulation[:, 5 * width :]

    modulation, sent_modulation = call(
        order,
        modulation_kernel,
        "modulation",
        [],
        [wait_for(own_modulation, normed_rows)],
        [((slots, 6 * width), F32), ((slots, 3 * width), F32)],
        1.0,
        limit=8,
    )
    modulation_rows = gather(sent_modulation, "rep", rep_size)

    def head_mask(h):
        lanes = lax.broadcasted_iota(jnp.int32, (1, padded), 1)
        inside = (lanes >= h * head_width) & (lanes < (h + 1) * head_width)
        return jnp.where(inside, 1.0, 0.0).astype(BF)

    def probabilities(query_head, key, same):
        scores = jnp.where(same, dot_rt(query_head, key) * score_scale, -1e30)
        exponent = jnp.exp(scores - jnp.max(scores, axis=-1, keepdims=True))
        return exponent / jnp.sum(exponent, axis=-1, keepdims=True)

    def turn(values, cosine_row, sine_row, sense):
        before = pltpu.roll(values, pair_count, 1)
        after = pltpu.roll(values, padded - pair_count, 1)
        lanes = lax.broadcasted_iota(jnp.int32, (1, padded), 1)
        second = lax.rem(lanes, 2 * pair_count) >= pair_count
        return values * cosine_row + jnp.where(second, before, after) * (sense * sine_row)

    def attention_kernel(r_ref, *refs):
        modulations = refs[:rep_size]
        normed, weight, bias, tables_ref, column_ref, row_ref = refs[rep_size : rep_size + 6]
        hidden_all, wide, query_out, key_out, value_out, attended_out, modulation_stack = refs[
            rep_size + 6 :
        ]
        for j in range(rep_size):
            modulation_stack[j] = modulations[j][:, : 2 * width]
        for t in range(3):
            wide[:, t * padded : t * padded + block] = weight[:, t * block : (t + 1) * block]
            if padded > block:
                wide[:, t * padded + block : (t + 1) * padded] = jnp.zeros(
                    (width, padded - block), BF
                )

        def row(j, carry):
            first = pl.multiple_of(j * count, count)

            def step(at):
                here = pl.ds(pl.multiple_of(first + at.start, CHUNK), CHUNK)
                slot_of = column_ref[j, at, 0:1]
                scale = pick(modulation_stack[j], slot_of, width, width)
                shift = pick(modulation_stack[j], slot_of, 0, width)
                hidden_all[here, :] = (normed[here, :] * (1.0 + scale) + shift).astype(BF)

            chunks(count, step)
            projected = dot(hidden_all[pl.ds(first, count), :], wide[...]) + bias[...]
            cos_row, sin_row = rotary(tables_ref, column_ref[j])
            query = turn(projected[:, :padded], cos_row, sin_row, 1.0).astype(BF)
            key = turn(projected[:, padded : 2 * padded], cos_row, sin_row, 1.0).astype(BF)
            value = projected[:, 2 * padded :].astype(BF)
            query_out[j], key_out[j], value_out[j] = query, key, value
            same = column_ref[j, :, 0:1] == row_ref[j, 0:1, :]
            total = jnp.zeros((count, padded), F32)
            for h in range(local_heads):
                mask = head_mask(h)
                probs = probabilities(query * mask, key, same)
                total = total + dot(probs.astype(BF), value * mask)
            owner = pl.ds(pl.multiple_of((r_ref[0] ^ j) * count, count), count)
            attended_out[owner, :] = total[:, :block].astype(BF)
            return carry

        lax.fori_loop(0, rep_size, row, 0)

    hidden_one_all, wide_weight, query_all, key_all, value_all, attended_heads = call(
        order,
        attention_kernel,
        "attention",
        [r_index],
        modulation_rows
        + [normed_rows, qkv_block, own_bias, tables, place_columns, place_rows],
        [((flat, width), BF), ((width, 3 * padded), BF)]
        + [((rep_size, count, padded), BF)] * 3
        + [((flat, block), BF)],
        22.0,
        scratch=[((rep_size, slots, 2 * width), F32)],
        limit=44,
        near=range(1, rep_size),
    )
    own_heads = exchange(attended_heads, "rep")

    def feed_back_kernel(*refs):
        cotangents, modulations = refs[:rep_size], refs[rep_size : 2 * rep_size]
        columns_ref, out = refs[2 * rep_size :]
        for j in range(rep_size):

            def step(at, j=j):
                masked = cotangents[j][at, :].astype(F32) * columns_ref[j, at, 3:4]
                gate = pick(modulations[j], columns_ref[j, at, 0:1], 2 * width, width)
                out[pl.ds(j * count + at.start, CHUNK), :] = (gate * masked).astype(BF)

            chunks(count, step)

    (feed_back_all,) = call(
        order,
        feed_back_kernel,
        "feed_back",
        [],
        cotangent_rows + modulation_rows + [place_columns],
        [((flat, width), BF)],
        4.0,
        limit=24,
        near=(*range(1, rep_size), *range(rep_size + 1, 2 * rep_size)),
    )

    def middle_kernel(
        heads, weight, bias, tokens_ref, modulation, places, branch, normed_out, inverse_out,
        hidden, attended,
    ):
        for k in range(rep_size):
            attended[:, k * block : (k + 1) * block] = heads[k * count : (k + 1) * count, :]
        branch[...] = dot(attended[...], weight[...]) + bias[...]

        def step(here):
            slot_of = places[0, here, 0:1]
            gate = pick(modulation, slot_of, 2 * width, width)
            middle = tokens_ref[here, :].astype(F32) + gate * branch[here, :]
            normed, inverse = normalize_keep(middle)
            normed_out[here, :] = normed
            inverse_out[here, :] = inverse
            scale = pick(modulation, slot_of, 4 * width, width)
            hidden[here, :] = (
                normed * (1.0 + scale) + pick(modulation, slot_of, 3 * width, width)
            ).astype(BF)

        chunks(count, step)

    branch, normed_two, inverse_two, hidden_two, attended = call(
        order,
        middle_kernel,
        "second_norm",
        [],
        [own_heads, out_full, output_bias_all, tokens, modulation, place_columns],
        [((count, width), F32), ((count, width), F32), ((count, 1), F32)]
        + [((count, width), BF)] * 2,
        7.0,
        limit=24,
    )
    hidden_two_rows = gather(hidden_two, "rep", rep_size)
    all_activated = gather(wait_for(line_activated, hidden_two_rows), "rep", rep_size)
    attended_rows = gather(wait_for(attended, hidden_two_rows), "rep", rep_size)

    step_ff = 256 if block_ff % 256 == 0 else 128

    def feed_kernel(*refs):
        back_all, weight = refs[rep_size : rep_size + 2]
        outs = refs[rep_size + 2 :]
        hidden_all, three, both_back, down = outs[:4]
        parts_out, parts = outs[4:-1], outs[-1]
        for j in range(rep_size):
            hidden_all[j * count : (j + 1) * count, :] = refs[j][...]
        for j in range(fsdp_size):
            for a, lanes, c, packed_lanes in units:
                from_row, to_row = j * shard_width + c, j * piece + a
                down[to_row : to_row + unit_rows, lanes] = weight[
                    from_row : from_row + unit_rows, packed_lanes
                ]

        def row(j, carry):
            here = pl.ds(pl.multiple_of(j * count, count), count)
            hidden, back = hidden_all[here, :], back_all[here, :]
            for c in range(block_ff // step_ff):
                at = slice(c * step_ff, (c + 1) * step_ff)
                up_at = slice(block_ff + c * step_ff, block_ff + (c + 1) * step_ff)
                gate = dot(hidden, weight[:, at])
                up = dot(hidden, weight[:, up_at])
                hidden_back = dot_rt(back, down[at, :])
                sigmoid = jax.nn.sigmoid(gate)
                silu = gate * sigmoid
                three[here, at] = (silu * up).astype(BF)
                slope = sigmoid * (1.0 + gate * (1.0 - sigmoid))
                both_back[here, at] = (hidden_back * up * slope).astype(BF)
                both_back[here, up_at] = (hidden_back * silu).astype(BF)
            parts[j] = dot_rt(both_back[here, :], weight[:, : 2 * block_ff])
            return carry

        lax.fori_loop(0, rep_size, row, 0)
        store_parts(parts, parts_out)

    hidden_two_all, hidden_three, both_back, down_block, *back_parts = call(
        order,
        feed_kernel,
        "feed_forward",
        [],
        hidden_two_rows + [feed_back_all, feed_block],
        [
            ((flat, width), BF),
            ((flat, block_ff), BF),
            ((flat, 2 * block_ff), BF),
            ((block_ff, width), BF),
        ]
        + part_shapes(rep_size, count, width),
        20.0,
        scratch=[((rep_size, count, width), F32)],
        limit=44,
        near=range(1, rep_size),
    )
    back_addends = send(back_parts, "rep", rep_size)

    def sent_gradient(value):
        return lax.psum_scatter(value, "fsdp", scatter_dimension=0, tiled=True)

    def feed_gradient_kernel(hidden_all, back_all, three, both_back, out):
        step_width = width // 3
        for m in range(3):
            at = slice(m * step_width, (m + 1) * step_width)
            out[at, : 2 * block_ff] = dot_lt(hidden_all[:, at], both_back[...]).astype(BF)
        together = max(1, fsdp_size // 2)
        for first in range(0, fsdp_size, together):
            gradient = dot_lt(
                three[:, first * piece : (first + together) * piece], back_all[...]
            ).astype(BF)
            for j in range(together):
                for a, lanes, c, packed_lanes in units:
                    to_row = (first + j) * shard_width + c
                    out[to_row : to_row + unit_rows, packed_lanes] = gradient[
                        j * piece + a : j * piece + a + unit_rows, lanes
                    ]

    (feed_gradient,) = call(
        order,
        feed_gradient_kernel,
        "feed_gradient",
        [],
        [wait_for(hidden_two_all, all_activated), feed_back_all, hidden_three, both_back],
        [((width, 3 * block_ff), BF)],
        9.0,
        limit=36,
    )
    feed_sum = sent_gradient(feed_gradient)

    def middle_back_kernel(*refs):
        addends = refs[:rep_size]
        cotangent_ref, places, modulation, normed_ref, inverse_ref, branch_ref, weight = refs[
            rep_size : rep_size + 7
        ]
        middle_back, branch_back, sums_out, bias_out, heads_out, sums = refs[
            rep_size + 7 :
        ]
        sums[...] = jnp.zeros_like(sums)

        def step(here):
            slot_of = places[0, here, 0:1]
            upstream = addends[0][here, :]
            for ref in addends[1:]:
                upstream = upstream + ref[here, :].astype(F32)
            normed = normed_ref[here, :]
            masked = cotangent_ref[here, :].astype(F32) * places[0, here, 3:4]
            scale = pick(modulation, slot_of, 4 * width, width)
            back = masked + normalize_back(normed, inverse_ref[here, :], upstream * (1.0 + scale))
            middle_back[here, :] = back
            gate = pick(modulation, slot_of, 2 * width, width)
            low = (back * gate).astype(BF)
            branch_back[here, :] = low
            add_slots(sums, 0, slots, slot_of, back * branch_ref[here, :])
            add_slots(sums, slots, slots, slot_of, upstream)
            add_slots(sums, 2 * slots, slots, slot_of, upstream * normed)
            sums[3 * slots] += jnp.sum(low.astype(F32).reshape(CHUNK // 8, 8, width), axis=0)

        chunks(count, step)
        total = jnp.sum(sums[...], axis=1)
        sums_out[...] = total[: 3 * slots]
        bias_out[...] = total[3 * slots :]
        heads = dot_rt(branch_back[...], weight[...])
        for k in range(rep_size):
            to, at = slice(k * count, (k + 1) * count), slice(k * block, (k + 1) * block)
            heads_out[to, :] = heads[:, at].astype(BF)

    middle_back, branch_back, middle_sums, output_bias_sum, sent_heads = call(
        order,
        middle_back_kernel,
        "second_norm_back",
        [],
        back_addends
        + [cotangent, place_columns, modulation, normed_two, inverse_two, branch, out_full],
        [
            ((count, width), F32),
            ((count, width), BF),
            ((3 * slots, width), F32),
            ((1, width), F32),
            ((flat, block), BF),
        ],
        6.0,
        scratch=[((3 * slots + 1, 8, width), F32)],
        limit=28,
        near=range(1, rep_size),
    )
    heads_back = exchange(sent_heads, "rep")

    group_tokens = count // rep_size

    def feed_out_kernel(r_ref, three, down, branch_back_ref, *outs):
        for j in range(rep_size):
            rows_here = slice(j * count, (j + 1) * count)
            outs[j][:count, :] = dot(three[rows_here, :], down[...]).astype(outs[j].dtype)
            for k in range(rep_size):

                @pl.when((r_ref[0] ^ j) == k)
                def _(j=j, k=k):
                    for g in range(rep_size):
                        rows_here = slice(g * group_tokens, (g + 1) * group_tokens)
                        outs[j][count:, g * block : (g + 1) * block] = branch_back_ref[
                            rows_here, k * block : (k + 1) * block
                        ].astype(outs[j].dtype)

    feed_parts = call(
        order,
        feed_out_kernel,
        "feed_out",
        [r_index],
        [wait_for(hidden_three, attended_rows), down_block, branch_back],
        [((count + group_tokens, width), F32)] + [((count + group_tokens, width), BF)] * others,
        4.0,
        limit=24,
    )
    feed_addends = send(wait_for(list(feed_parts), heads_back), "rep", rep_size)

    def attention_back_kernel(r_ref, *refs):
        heads, query_ref, key_ref, value_ref, wide, tables_ref = refs[:6]
        column_ref, row_ref, projected_back, bias_out = refs[6:10]
        parts_out = refs[10:-2]
        parts, head_stack = refs[-2:]
        if padded > block:
            head_stack[:, :, block:] = jnp.zeros((rep_size, count, padded - block), BF)
        for j in range(rep_size):
            owner = pl.ds(pl.multiple_of((r_ref[0] ^ j) * count, count), count)
            head_stack[j, :, :block] = heads[owner, :]
        bias_out[...] = jnp.zeros_like(bias_out)

        def row(j, carry):
            here = pl.ds(pl.multiple_of(j * count, count), count)
            query, key, value, back = query_ref[j], key_ref[j], value_ref[j], head_stack[j]
            same = column_ref[j, :, 0:1] == row_ref[j, 0:1, :]
            query_back = jnp.zeros((count, padded), F32)
            key_back = jnp.zeros((count, padded), F32)
            value_back = jnp.zeros((count, padded), F32)
            for h in range(local_heads):
                mask = head_mask(h)
                query_head, back_head = query * mask, back * mask
                probs = probabilities(query_head, key, same)
                probs_back = dot_rt(back_head, value)
                scores_back = (
                    probs
                    * (probs_back - jnp.sum(probs * probs_back, axis=-1, keepdims=True))
                ).astype(BF)
                value_back = value_back + dot_lt(probs.astype(BF), back_head)
                query_back = query_back + dot(scores_back, key * mask)
                key_back = key_back + dot_lt(scores_back, query_head)
            cos_row, sin_row = rotary(tables_ref, column_ref[j])
            query_back = turn(query_back * score_scale, cos_row, sin_row, -1.0)
            key_back = turn(key_back * score_scale, cos_row, sin_row, -1.0)
            low = [value.astype(BF) for value in (query_back, key_back, value_back)]
            for t in range(3):
                projected_back[here, t * block : (t + 1) * block] = low[t][:, :block]
                bias_out[:, t * padded : (t + 1) * padded] += jnp.sum(
                    low[t].astype(F32), axis=0, keepdims=True
                )
            parts[j] = dot_rt(jnp.concatenate(low, axis=1), wide[...])
            return carry

        lax.fori_loop(0, rep_size, row, 0)
        store_parts(parts, parts_out)

    projected_back, projection_bias_sum, *one_parts = call(
        order,
        attention_back_kernel,
        "attention_back",
        [r_index],
        [heads_back, query_all, key_all, value_all, wide_weight, tables]
        + [place_columns, place_rows],
        [((flat, 3 * block), BF), ((1, 3 * padded), F32)] + part_shapes(rep_size, count, width),
        23.0,
        scratch=[((rep_size, count, width), F32), ((rep_size, count, padded), BF)],
        limit=44,
    )
    one_addends = send(one_parts, "rep", rep_size)

    def attention_gradient_kernel(*refs):
        hidden_all, back = refs[:2]
        heads, backs = refs[2 : 2 + rep_size], refs[2 + rep_size : 2 + 2 * rep_size]
        out, head_stack, back_stack = refs[2 + 2 * rep_size :]
        for j in range(rep_size):
            head_stack[j * count : (j + 1) * count, :] = heads[j][...]
            for g in range(rep_size):
                first = j * count + g * group_tokens
                back_stack[first : first + group_tokens, :] = backs[j][
                    count:, g * block : (g + 1) * block
                ].astype(BF)
        step_width = width // 3
        for m in range(3):
            at = slice(m * step_width, (m + 1) * step_width)
            out[at, : 3 * block] = dot_lt(hidden_all[:, at], back[...]).astype(BF)
            out[at, 3 * block :] = dot_lt(head_stack[:, at], back_stack[...]).astype(BF)

    (attention_gradient,) = call(
        order,
        attention_gradient_kernel,
        "attention_gradient",
        [],
        [hidden_one_all, projected_back] + attended_rows + feed_addends,
        [((width, 4 * block), BF)],
        5.0,
        scratch=[((flat, width), BF), ((flat, block), BF)],
        limit=32,
        near=(*range(3, 2 + rep_size), *range(3 + rep_size, 2 + 2 * rep_size)),
    )
    attention_sum = sent_gradient(attention_gradient)

    def output_kernel(*refs):
        feeds = refs[:rep_size]
        tokens_ref, branch_ref, cotangent_ref, places, modulation = refs[rep_size : rep_size + 5]
        block_out, sums_out, sums = refs[rep_size + 5 :]
        sums[...] = jnp.zeros_like(sums)

        def step(here):
            slot_of = places[0, here, 0:1]
            feed = feeds[0][here, :]
            for ref in feeds[1:]:
                feed = feed + ref[here, :].astype(F32)
            gate_one = pick(modulation, slot_of, 2 * width, width)
            middle = tokens_ref[here, :].astype(F32) + gate_one * branch_ref[here, :]
            gate_two = pick(modulation, slot_of, 5 * width, width)
            block_out[here, :] = (middle + gate_two * feed).astype(BF)
            masked = cotangent_ref[here, :].astype(F32) * places[0, here, 3:4]
            add_slots(sums, 0, slots, slot_of, masked * feed)

        chunks(count, step)
        sums_out[...] = jnp.sum(sums[...], axis=1)

    block_output, gate_two_sums = call(
        order,
        output_kernel,
        "layer_output",
        [],
        feed_addends + [tokens, branch, cotangent, place_columns, modulation],
        [((count, width), BF), ((slots, width), F32)],
        0.1,
        scratch=[((slots, 8, width), F32)],
        limit=16,
        near=range(1, rep_size),
    )

    def first_back_kernel(r_ref, *refs):
        addends = refs[:rep_size]
        tokens_ref, back_ref, modulation, places, middle_ref, gate_two_ref, bias, out_bias = refs[
            rep_size : rep_size + 8
        ]
        gradient, back_blocks, sums, whole, whole_bias, stack = refs[rep_size + 8 :]
        sums[...] = jnp.zeros_like(sums)

        def step(here):
            slot_of = places[0, here, 0:1]
            upstream = addends[0][here, :]
            for ref in addends[1:]:
                upstream = upstream + ref[here, :].astype(F32)
            normed, inverse = normalize_keep(tokens_ref[here, :].astype(F32))
            scale = pick(modulation, slot_of, width, width)
            gradient[here, :] = back_ref[here, :] + normalize_back(
                normed, inverse, upstream * (1.0 + scale)
            )
            add_slots(sums, 0, slots, slot_of, upstream)
            add_slots(sums, slots, slots, slot_of, upstream * normed)

        chunks(count, step)
        total = jnp.sum(sums[...], axis=1)
        whole[:, :width] = total[:slots]
        whole[:, width : 2 * width] = total[slots:]
        for t in range(3):
            at = slice((2 + t) * width, (3 + t) * width)
            whole[:, at] = middle_ref[t * slots : (t + 1) * slots, :]
        whole[:, 5 * width :] = gate_two_ref[...]
        whole_bias[...] = jnp.zeros_like(whole_bias)
        for k in range(rep_size):

            @pl.when(r_ref[0] == k)
            def _():
                for t in range(3):
                    first = t * width + k * block
                    whole_bias[:, first : first + block] = bias[:, t * padded : t * padded + block]

        stack[...] = jnp.zeros_like(stack)
        for k in range(fsdp_size):
            stack[k, :slots, :] = whole[:, k * columns : (k + 1) * columns]
            at = slice(k * shard_bias, (k + 1) * shard_bias)
            stack[k, slots : slots + 1, :shard_bias] = whole_bias[:, at]
            at = slice(k * shard_out_bias, (k + 1) * shard_out_bias)
            lanes = slice(shard_bias, shard_bias + shard_out_bias)
            stack[k, slots : slots + 1, lanes] = out_bias[:, at]
        back_blocks[...] = stack[...].reshape(fsdp_size * GROUP, columns).astype(BF)

    tokens_gradient, back_blocks = call(
        order,
        first_back_kernel,
        "first_norm_back",
        [r_index],
        one_addends
        + [tokens, middle_back, modulation, place_columns, middle_sums, gate_two_sums]
        + [projection_bias_sum, output_bias_sum],
        [((count, width), F32), ((fsdp_size * GROUP, columns), BF)],
        20.0,
        scratch=[
            ((2 * slots, 8, width), F32),
            ((slots, 6 * width), F32),
            ((1, 3 * width), F32),
            ((fsdp_size, GROUP, columns), F32),
        ],
        limit=20,
        near=range(1, rep_size),
    )

    line_backs = exchange(back_blocks, "fsdp")
    feed_sums = gather(wait_for(feed_sum, one_addends), "rep", rep_size)

    def conditioning_kernel(groups, weight, out, line_out):
        stack = groups[...].astype(F32)
        bias = jnp.sum(stack.reshape(fsdp_size, GROUP, columns), axis=0)[slots : slots + 1]
        row_ids = lax.broadcasted_iota(jnp.int32, (fsdp_size * GROUP, 1), 0)
        rows_back = jnp.where(lax.rem(row_ids, GROUP) < slots, stack, 0.0)
        line_out[...] = jnp.where(row_ids == slots, bias, rows_back).astype(BF)
        result = dot(rows_back.astype(BF), weight[...])
        for k in range(fsdp_size):
            out[k * slots : (k + 1) * slots, :] = result[k * GROUP : k * GROUP + slots, :]

    activated_backs, line_back = call(
        order,
        conditioning_kernel,
        "conditioning_back",
        [],
        [wait_for(line_backs, feed_sums), modulation_weight.T],
        [((fsdp_size * slots, width), F32), ((fsdp_size * GROUP, columns), BF)],
        10.0,
        limit=24,
    )
    activated_backs = exchange(activated_backs, "fsdp")
    all_backs = gather(line_back, "rep", rep_size)
    activated_back = jnp.sum(activated_backs.reshape(fsdp_size, slots, width), axis=0)
    conditioning_gradient = activated_back.reshape(rows, slots, width) * silu_slope(cond_float)

    def table_kernel(*refs):
        activateds, backs = refs[:rep_size], refs[rep_size : 2 * rep_size]
        table, table_bias, bias, activated_stack, back_stack = refs[2 * rep_size :]
        line = fsdp_size * GROUP
        total = jnp.zeros((1, columns), F32)
        for j in range(rep_size):
            activated_stack[j * line : (j + 1) * line, :] = activateds[j][...]
            back_stack[j * line : (j + 1) * line, :] = backs[j][...]
            total = total + backs[j][...].astype(F32)[slots : slots + 1, :]
        bias[...] = total
        back = back_stack[...].astype(F32)
        in_group = lax.rem(lax.broadcasted_iota(jnp.int32, (rep_size * line, 1), 0), GROUP)
        table_bias[...] = jnp.sum(
            jnp.where(in_group < slots, back, 0.0), axis=0, keepdims=True
        )
        table[...] = dot_lt(back_stack[...], activated_stack[...])

    table_gradient, table_bias_gradient, bias_gradients = call(
        order,
        table_kernel,
        "table_gradient",
        [],
        all_activated + all_backs,
        [((columns, width), F32), ((1, columns), F32), ((1, columns), F32)],
        10.0,
        scratch=[
            ((rep_size * fsdp_size * GROUP, width), BF),
            ((rep_size * fsdp_size * GROUP, columns), BF),
        ],
        limit=24,
        near=range(1, rep_size),
    )

    def feed_blocks_kernel(r_ref, *refs):
        gate_out, up_out, down_out, stack = refs[rep_size:]
        for j in range(rep_size):
            stack[j] = refs[j][...].astype(F32)
        for k in range(rep_size):
            here = r_ref[0] ^ k
            for j in range(fsdp_size):
                target = slice(j * shard_ff + k * piece, j * shard_ff + (k + 1) * piece)
                first = block_ff + j * piece
                gate_out[:, target] = stack[here, :, j * piece : (j + 1) * piece]
                up_out[:, target] = stack[here, :, first : first + piece]
            for a, lanes, c, packed_lanes in units:
                to_row = k * piece + a
                down_out[to_row : to_row + unit_rows, lanes] = stack[
                    here, c : c + unit_rows, packed_lanes
                ]

    gate_gradient, up_gradient, down_gradient = call(
        order,
        feed_blocks_kernel,
        "feed_blocks",
        [r_index],
        feed_sums,
        [((shard_width, fsdp_size * shard_ff), F32)] * 2 + [((shard_ff, width), F32)],
        10.0,
        scratch=[((rep_size, shard_width, 3 * block_ff), F32)],
        limit=24,
        near=range(1, rep_size),
    )

    def attention_blocks_kernel(r_ref, *refs):
        projection_out, output_out, stack = refs[rep_size:]
        for j in range(rep_size):
            stack[j] = refs[j][...].astype(F32)
        for k in range(rep_size):
            here = r_ref[0] ^ k
            for t in range(3):
                first = t * width + k * block
                projection_out[:, first : first + block] = stack[
                    here, :, t * block : (t + 1) * block
                ]
            output_out[:, k * block : (k + 1) * block] = stack[here, :, 3 * block :]

    projection_gradient, output_gradient = call(
        order,
        attention_blocks_kernel,
        "attention_blocks",
        [r_index],
        gather(attention_sum, "rep", rep_size),
        [((shard_width, 3 * width), F32), ((shard_width, width), F32)],
        3.0,
        scratch=[((rep_size, shard_width, 4 * block), F32)],
        limit=24,
        near=range(1, rep_size),
    )
    return (
        block_output[None],
        tokens_gradient[None],
        conditioning_gradient,
        table_gradient.T,
        table_bias_gradient[0],
        projection_gradient,
        bias_gradients[0, :shard_bias],
        output_gradient,
        bias_gradients[0, shard_bias : shard_bias + shard_out_bias],
        gate_gradient,
        up_gradient,
        down_gradient,
    )


def solution(mesh):
    sizes = dict(mesh.shape)

    def body(*arrays):
        return on_device(sizes["rep"], sizes["fsdp"], *arrays)

    rows = ("rep", "fsdp")
    in_specs = (
        P(rows, None, None),
        P(rows, None, None),
        P(rows, None),
        P(rows, None),
        P(rows, None),
        P(rows, None),
        P(None, "fsdp"),
        P("fsdp"),
        P("fsdp", None),
        P("fsdp"),
        P("fsdp", None),
        P("fsdp"),
        P("fsdp", None),
        P("fsdp", None),
        P("fsdp", None),
        P(rows, None, None),
    )
    out_specs = (
        P(rows, None, None),
        P(rows, None, None),
        P(rows, None, None),
        P(None, "fsdp"),
        P("fsdp"),
        P("fsdp", None),
        P("fsdp"),
        P("fsdp", None),
        P("fsdp"),
        P("fsdp", None),
        P("fsdp", None),
        P("fsdp", None),
    )
    return jax.shard_map(
        body, mesh=mesh, in_specs=in_specs, out_specs=out_specs, check_vma=False
    )
```

```python
import math

import jax
import jax.numpy as jnp
import numpy as np
from jax import lax
from jax.experimental import pallas as pl
from jax.experimental.pallas import tpu as pltpu
from jax.sharding import PartitionSpec as P

HEADS = 16
BF = jnp.bfloat16
F32 = jnp.float32
LANES = 128
CHUNK = 32
GROUP = 8


def wait_for(value, *others):
    return lax.optimization_barrier((value, others))[0]


def swap_with(value, axis, size, bit):
    return lax.ppermute(value, axis, [(i, i ^ bit) for i in range(size)])


def gather(value, axis, size):
    return [value] + [swap_with(value, axis, size, j) for j in range(1, size)]


def halves_gather(top, low, axis, size):
    if size != 4:
        return list(zip(gather(top, axis, size), gather(low, axis, size), strict=True))
    top_one, low_two = swap_with(top, axis, size, 1), swap_with(low, axis, size, 2)
    top_three, low_three = swap_with(top_one, axis, size, 2), swap_with(low_two, axis, size, 1)
    low_one, top_two = swap_with(low, axis, size, 1), swap_with(top, axis, size, 2)
    return [(top, low), (top_one, low_one), (top_two, low_two), (top_three, low_three)]


def send(values, axis, size):
    return [values[0]] + [swap_with(values[j], axis, size, j) for j in range(1, size)]


def exchange(value, axis):
    return lax.all_to_all(value, axis, 0, 0, tiled=True)


def whole_block(array):
    zeros = (0,) * len(array.shape)
    return pl.BlockSpec(array.shape, lambda i: zeros, pipeline_mode=pl.Buffered(1))


def call(order, body, name, scalars, arrays, outs, micros, scratch=(), limit=48, near=()):
    shapes = [pltpu.HBM(shape, dtype) for shape, dtype in outs]
    if order:
        first, _ = lax.optimization_barrier((arrays[0], order.pop()))
        arrays = [first] + list(arrays[1:])
    arrays = [
        array if n in near else pltpu.with_memory_space_constraint(array, pltpu.HBM)
        for n, array in enumerate(arrays)
    ]
    results = pl.pallas_call(
        body,
        name=name,
        grid=(1,),
        out_shape=shapes,
        in_specs=[pl.BlockSpec(memory_space=pltpu.SMEM)] * len(scalars)
        + [whole_block(array) for array in arrays],
        out_specs=[whole_block(shape) for shape in shapes],
        scratch_shapes=[pltpu.VMEM(shape, dtype) for shape, dtype in scratch],
        compiler_params=pltpu.CompilerParams(vmem_limit_bytes=limit << 20),
        cost_estimate=pl.CostEstimate(
            flops=int(micros * 1.000e+09), bytes_accessed=int(micros * 3.000e+06), transcendentals=0
        ),
    )(*scalars, *arrays)
    order.append(results[0])
    return results


def part_shapes(size, tokens, width):
    return [((tokens, width), F32)] + [((tokens, width), BF)] * (size - 1)


def store_parts(parts, refs):
    refs[0][...] = parts[0]
    for j in range(1, len(refs)):
        refs[j][...] = parts[j].astype(BF)


def dot(left, right):
    return jnp.dot(left, right, preferred_element_type=F32)


def dot_rt(left, right):
    return lax.dot_general(left, right, (((1,), (1,)), ((), ())), preferred_element_type=F32)


def dot_lt(left, right):
    return lax.dot_general(left, right, (((0,), (0,)), ((), ())), preferred_element_type=F32)


def pick(modulation, slot_of, first, width):
    total = jnp.zeros((slot_of.shape[0], width), F32)
    for k in range(modulation.shape[0]):
        total = jnp.where(slot_of == k, modulation[k : k + 1, first : first + width], total)
    return total


def normalize_keep(values):
    centered = values - jnp.mean(values, axis=-1, keepdims=True)
    variance = jnp.mean(centered * centered, axis=-1, keepdims=True)
    inverse = lax.rsqrt(variance + 1e-06)
    return centered * inverse, inverse


def normalize_back(normed, inverse, upstream):
    return inverse * (
        upstream
        - jnp.mean(upstream, axis=-1, keepdims=True)
        - normed * jnp.mean(upstream * normed, axis=-1, keepdims=True)
    )


def add_slots(sums, base, count, slot_of, values):
    rows, width = values.shape
    for k in range(count):
        chosen = jnp.where(slot_of == k, values, 0.0)
        sums[base + k] += jnp.sum(chosen.reshape(rows // 8, 8, width), axis=0)


def chunks(tokens, step):
    def body(i, carry):
        step(pl.ds(pl.multiple_of(i * CHUNK, CHUNK), CHUNK))
        return carry

    lax.fori_loop(0, tokens // CHUNK, body, 0, unroll=2)


def silu_slope(values):
    sigmoid = jax.nn.sigmoid(values)
    return sigmoid * (1.0 + values * (1.0 - sigmoid))


def on_device(
    rep_size,
    fsdp_size,
    tokens,
    conditioning,
    segment_ids,
    heights,
    widths,
    pad_mask,
    modulation_weight,
    modulation_bias,
    projection_weight,
    projection_bias,
    output_weight,
    output_bias,
    gate_weight,
    up_weight,
    down_weight,
    cotangent,
):
    rows, count, width = tokens.shape
    assert rows == 1
    slots = conditioning.shape[1]
    head_width = width // HEADS
    local_heads = HEADS // rep_size
    block = width // rep_size
    padded = -(-block // LANES) * LANES
    score_scale = 1.0 / math.sqrt(head_width)
    shard_ff = down_weight.shape[0]
    piece = shard_ff // rep_size
    block_ff = fsdp_size * piece
    shard_width = projection_weight.shape[0]
    columns = modulation_weight.shape[1]
    flat = rep_size * count
    half = count // 2
    others = rep_size - 1
    r = lax.axis_index("rep")
    r_index = r.reshape(1).astype(jnp.int32)
    tokens, cotangent = tokens[0], cotangent[0]
    order = []

    def qkv_shard_kernel(r_ref, projection, out):
        for k in range(rep_size):

            @pl.when(r_ref[0] == k)
            def _():
                for t in range(3):
                    first = t * width + k * block
                    out[:, t * block : (t + 1) * block] = projection[:, first : first + block]

    (qkv_shard,) = call(
        order,
        qkv_shard_kernel,
        "qkv_shard",
        [r_index],
        [projection_weight],
        [((shard_width, 3 * block), BF)],
        4.5,
        limit=16,
    )

    slot_ids = jnp.arange(slots, dtype=jnp.int32)
    member_ints = (segment_ids[:, :, None] == slot_ids).astype(jnp.int32)
    before_ints = (slot_ids < segment_ids[:, :, None]).astype(jnp.int32)
    starts = jnp.sum(before_ints * (heights * widths)[:, None, :], axis=2)
    offsets = jnp.arange(count, dtype=jnp.int32)[None, :] - starts
    row_width = jnp.sum(member_ints * widths[:, None, :], axis=2)
    places = jnp.concatenate(
        [segment_ids, offsets // row_width, offsets % row_width, pad_mask], axis=1
    ).astype(BF)
    places = jnp.pad(places, ((0, GROUP - 1), (0, width - 4 * count)))
    token_rows = gather(jnp.concatenate([tokens, places], axis=0), "rep", rep_size)
    cotangent_rows = gather(wait_for(cotangent, token_rows), "rep", rep_size)

    cond_float = conditioning.astype(F32)
    activated = jax.nn.silu(cond_float).astype(BF).reshape(slots, width)
    shard_bias, shard_out_bias = projection_bias.shape[0], output_bias.shape[0]
    bias_row = jnp.pad(
        jnp.concatenate([projection_bias, output_bias]), (0, width - shard_bias - shard_out_bias)
    )[None]
    group_rows = jnp.concatenate(
        [activated, bias_row, jnp.zeros((GROUP - slots - 1, width), BF)], axis=0
    )
    line_rows = lax.all_gather(group_rows, "fsdp", axis=0, tiled=True)

    def modulate_kernel(r_ref, *refs):
        groups, weight, bias = refs[:3]
        out, activated_out, bias_out, out_bias, stack, whole = refs[3:]
        stack[...] = groups[...].astype(F32).reshape(fsdp_size, GROUP, width)
        in_group = lax.rem(lax.broadcasted_iota(jnp.int32, (fsdp_size * GROUP, 1), 0), GROUP)
        rows_low = jnp.where(in_group < slots, groups[...].astype(F32), 0.0).astype(BF)
        activated_out[...] = rows_low
        out[...] = dot_rt(rows_low, weight[...]) + bias[...]
        for k in range(fsdp_size):
            row = stack[k, slots : slots + 1, :]
            whole[:, k * shard_bias : (k + 1) * shard_bias] = row[:, :shard_bias]
            at = slice(k * shard_out_bias, (k + 1) * shard_out_bias)
            out_bias[:, at] = row[:, shard_bias : shard_bias + shard_out_bias]
        bias_out[...] = jnp.zeros_like(bias_out)
        for k in range(rep_size):

            @pl.when(r_ref[0] == k)
            def _():
                for t in range(3):
                    first = t * width + k * block
                    bias_out[:, t * padded : t * padded + block] = whole[:, first : first + block]

    line_modulation, line_activated, own_bias, output_bias_all = call(
        order,
        modulate_kernel,
        "modulate",
        [r_index],
        [line_rows, modulation_weight.T, modulation_bias.astype(F32)[None]],
        [
            ((fsdp_size * GROUP, columns), F32),
            ((fsdp_size * GROUP, width), BF),
            ((1, 3 * padded), F32),
            ((1, width), F32),
        ],
        6.0,
        scratch=[((fsdp_size, GROUP, width), F32), ((1, 3 * width), F32)],
        limit=24,
    )
    own_modulation = lax.all_to_all(line_modulation, "fsdp", 0, 0, tiled=True)

    unit_rows, unit_lanes = math.gcd(piece, shard_width), math.gcd(width, block_ff)
    units = []
    for u in range((piece // unit_rows) * (width // unit_lanes)):
        (a, b), (c, d) = divmod(u, width // unit_lanes), divmod(u, block_ff // unit_lanes)
        units.append(
            (
                a * unit_rows,
                slice(b * unit_lanes, (b + 1) * unit_lanes),
                c * unit_rows,
                slice(2 * block_ff + d * unit_lanes, 2 * block_ff + (d + 1) * unit_lanes),
            )
        )

    def feed_shard_kernel(r_ref, gate, up, down, out):
        for k in range(rep_size):

            @pl.when(r_ref[0] == k)
            def _():
                for j in range(fsdp_size):
                    source = slice(j * shard_ff + k * piece, j * shard_ff + (k + 1) * piece)
                    out[:, j * piece : (j + 1) * piece] = gate[:, source]
                    first = block_ff + j * piece
                    out[:, first : first + piece] = up[:, source]
                for a, lanes, c, packed_lanes in units:
                    out[c : c + unit_rows, packed_lanes] = down[
                        k * piece + a : k * piece + a + unit_rows, lanes
                    ]

    (feed_shard,) = call(
        order,
        feed_shard_kernel,
        "feed_shard",
        [r_index],
        [gate_weight, up_weight, down_weight],
        [((shard_width, 3 * block_ff), BF)],
        4.5,
        limit=16,
    )
    qkv_block = lax.all_gather(qkv_shard, "fsdp", axis=0, tiled=True)
    out_full = lax.all_gather(wait_for(output_weight, qkv_shard), "fsdp", axis=0, tiled=True)
    feed_block = lax.all_gather(feed_shard, "fsdp", axis=0, tiled=True)

    def norm_rows_kernel(*refs):
        out, columns_out, rows_out = refs[rep_size:]
        for j in range(rep_size):
            ref = refs[j]

            def step(at, ref=ref, j=j):
                normed, _ = normalize_keep(ref[at, :].astype(F32))
                out[pl.ds(j * count + at.start, CHUNK), :] = normed

            chunks(count, step)
            line = ref[count:, :].astype(F32)
            for q in range(4):
                rows_out[j, q : q + 1, :] = line[:1, q * count : (q + 1) * count]
            rows_out[j, 4:, :] = jnp.zeros((4, count), F32)
            columns_out[j] = rows_out[j].T

    normed_rows, place_columns, place_rows = call(
        order,
        norm_rows_kernel,
        "first_norm",
        [],
        token_rows,
        [((flat, width), F32), ((rep_size, count, 8), F32), ((rep_size, 8, count), F32)],
        18.0,
        limit=24,
        near=range(1, rep_size),
    )
    pair_count = head_width // 4
    most_rows, most_columns = count // 4, 32
    lane = np.arange(padded)
    in_head = lane % head_width
    lane_frequency = 10000.0 ** (-(in_head % pair_count) / pair_count)
    of_row = (lane < block) & (in_head < 2 * pair_count)
    of_column = (lane < block) & (in_head >= 2 * pair_count)
    sign = np.where((in_head // pair_count) % 2 == 1, 1.0, -1.0)
    row_angle = np.arange(most_rows)[:, None] * lane_frequency
    column_angle = np.arange(most_columns)[:, None] * lane_frequency
    tables = np.concatenate(
        [
            np.concatenate(
                [
                    np.where(of_row, np.cos(row_angle), 0.0),
                    np.where(of_column, np.cos(column_angle), 0.0),
                ]
            ),
            np.concatenate(
                [
                    np.where(of_row, sign * np.sin(row_angle), 0.0),
                    np.where(of_column, sign * np.sin(column_angle), 0.0),
                ]
            ),
        ],
        axis=1,
    ).astype(np.float32)
    pieces, left = [], tables
    for _ in range(3):
        pieces.append(left.astype(jnp.bfloat16))
        left = left - pieces[-1].astype(np.float32)
    tables = jnp.asarray(np.stack(pieces))

    def rotary(tables_ref, places):
        numbers = lax.broadcasted_iota(jnp.int32, (count, most_rows + most_columns), 1).astype(F32)
        is_row = (numbers < most_rows) & (numbers == places[:, 1:2])
        is_column = (numbers >= most_rows) & (numbers - most_rows == places[:, 2:3])
        chosen = jnp.where(is_row | is_column, 1.0, 0.0).astype(BF)
        both = dot(chosen, tables_ref[2]) + dot(chosen, tables_ref[1]) + dot(chosen, tables_ref[0])
        return both[:, :padded], both[:, padded:]

    def modulation_kernel(arrived, modulation, sent):
        for k in range(fsdp_size):
            at = slice(k * columns, (k + 1) * columns)
            modulation[:, at] = arrived[k * GROUP : k * GROUP + slots, :]
        sent[:, : 2 * width] = modulation[:, : 2 * width]
        sent[:, 2 * width :] = modulation[:, 5 * width :]

    modulation, sent_modulation = call(
        order,
        modulation_kernel,
        "modulation",
        [],
        [wait_for(own_modulation, normed_rows)],
        [((slots, 6 * width), F32), ((slots, 3 * width), F32)],
        3.0,
        limit=8,
    )
    modulation_rows = gather(sent_modulation, "rep", rep_size)

    def head_mask(h):
        lanes = lax.broadcasted_iota(jnp.int32, (1, padded), 1)
        inside = (lanes >= h * head_width) & (lanes < (h + 1) * head_width)
        return jnp.where(inside, 1.0, 0.0).astype(BF)

    def probabilities(query_head, key, same):
        scores = jnp.where(same, dot_rt(query_head, key) * score_scale, -1e30)
        exponent = jnp.exp(scores - jnp.max(scores, axis=-1, keepdims=True))
        return exponent / jnp.sum(exponent, axis=-1, keepdims=True)

    def turn(values, cosine_row, sine_row, sense):
        before = pltpu.roll(values, pair_count, 1)
        after = pltpu.roll(values, padded - pair_count, 1)
        lanes = lax.broadcasted_iota(jnp.int32, (1, padded), 1)
        second = lax.rem(lanes, 2 * pair_count) >= pair_count
        return values * cosine_row + jnp.where(second, before, after) * (sense * sine_row)

    def attention_kernel(r_ref, *refs):
        modulations = refs[:rep_size]
        normed, weight, bias, tables_ref, column_ref, row_ref = refs[rep_size : rep_size + 6]
        hidden_all, wide, query_out, key_out, value_out, attended_out, modulation_stack = refs[
            rep_size + 6 :
        ]
        for j in range(rep_size):
            modulation_stack[j] = modulations[j][:, : 2 * width]
        for t in range(3):
            wide[:, t * padded : t * padded + block] = weight[:, t * block : (t + 1) * block]
            if padded > block:
                wide[:, t * padded + block : (t + 1) * padded] = jnp.zeros(
                    (width, padded - block), BF
                )

        def row(j, carry):
            first = pl.multiple_of(j * count, count)

            def step(at):
                here = pl.ds(pl.multiple_of(first + at.start, CHUNK), CHUNK)
                slot_of = column_ref[j, at, 0:1]
                scale = pick(modulation_stack[j], slot_of, width, width)
                shift = pick(modulation_stack[j], slot_of, 0, width)
                hidden_all[here, :] = (normed[here, :] * (1.0 + scale) + shift).astype(BF)

            chunks(count, step)
            projected = dot(hidden_all[pl.ds(first, count), :], wide[...]) + bias[...]
            cos_row, sin_row = rotary(tables_ref, column_ref[j])
            query = turn(projected[:, :padded], cos_row, sin_row, 1.0).astype(BF)
            key = turn(projected[:, padded : 2 * padded], cos_row, sin_row, 1.0).astype(BF)
            value = projected[:, 2 * padded :].astype(BF)
            query_out[j], key_out[j], value_out[j] = query, key, value
            same = column_ref[j, :, 0:1] == row_ref[j, 0:1, :]
            total = jnp.zeros((count, padded), F32)
            for h in range(local_heads):
                mask = head_mask(h)
                probs = probabilities(query * mask, key, same)
                total = total + dot(probs.astype(BF), value * mask)
            owner = pl.ds(pl.multiple_of((r_ref[0] ^ j) * count, count), count)
            attended_out[owner, :] = total[:, :block].astype(BF)
            return carry

        lax.fori_loop(0, rep_size, row, 0)

    hidden_one_all, wide_weight, query_all, key_all, value_all, attended_heads = call(
        order,
        attention_kernel,
        "attention",
        [r_index],
        modulation_rows
        + [normed_rows, qkv_block, own_bias, tables, place_columns, place_rows],
        [((flat, width), BF), ((width, 3 * padded), BF)]
        + [((rep_size, count, padded), BF)] * 3
        + [((flat, block), BF)],
        66.0,
        scratch=[((rep_size, slots, 2 * width), F32)],
        limit=44,
        near=range(1, rep_size),
    )
    own_heads = exchange(attended_heads, "rep")

    def feed_back_kernel(*refs):
        cotangents, modulations = refs[:rep_size], refs[rep_size : 2 * rep_size]
        columns_ref, out = refs[2 * rep_size :]
        for j in range(rep_size):

            def step(at, j=j):
                masked = cotangents[j][at, :].astype(F32) * columns_ref[j, at, 3:4]
                gate = pick(modulations[j], columns_ref[j, at, 0:1], 2 * width, width)
                out[pl.ds(j * count + at.start, CHUNK), :] = (gate * masked).astype(BF)

            chunks(count, step)

    (feed_back_all,) = call(
        order,
        feed_back_kernel,
        "feed_back",
        [],
        cotangent_rows + modulation_rows + [place_columns],
        [((flat, width), BF)],
        12.0,
        limit=24,
        near=(*range(1, rep_size), *range(rep_size + 1, 2 * rep_size)),
    )

    def middle_kernel(
        heads, weight, bias, tokens_ref, modulation, places, branch, normed_out, inverse_out,
        top, low, attended,
    ):
        for k in range(rep_size):
            attended[:, k * block : (k + 1) * block] = heads[k * count : (k + 1) * count, :]
        branch[...] = dot(attended[...], weight[...]) + bias[...]

        for p, hidden in enumerate((top, low)):

            def step(at, p=p, hidden=hidden):
                here = pl.ds(p * half + at.start, CHUNK)
                slot_of = places[0, here, 0:1]
                gate = pick(modulation, slot_of, 2 * width, width)
                middle = tokens_ref[here, :].astype(F32) + gate * branch[here, :]
                normed, inverse = normalize_keep(middle)
                normed_out[here, :] = normed
                inverse_out[here, :] = inverse
                scale = pick(modulation, slot_of, 4 * width, width)
                hidden[at, :] = (
                    normed * (1.0 + scale) + pick(modulation, slot_of, 3 * width, width)
                ).astype(BF)

            chunks(half, step)

    branch, normed_two, inverse_two, hidden_top, hidden_low, attended = call(
        order,
        middle_kernel,
        "second_norm",
        [],
        [own_heads, out_full, output_bias_all, tokens, modulation, place_columns],
        [((count, width), F32), ((count, width), F32), ((count, 1), F32)]
        + [((half, width), BF)] * 2
        + [((count, width), BF)],
        21.0,
        limit=24,
    )
    hidden_two_rows = halves_gather(hidden_top, hidden_low, "rep", rep_size)
    hidden_two_rows = [piece for row in hidden_two_rows for piece in row]
    all_activated = gather(wait_for(line_activated, hidden_two_rows), "rep", rep_size)

    step_ff = 256 if block_ff % 256 == 0 else 128

    def feed_kernel(*refs):
        back_all, weight = refs[2 * rep_size : 2 * rep_size + 2]
        outs = refs[2 * rep_size + 2 :]
        hidden_all, three, both_back, down = outs[:4]
        parts_out, parts = outs[4:-1], outs[-1]
        for n in range(2 * rep_size):
            hidden_all[n * half : (n + 1) * half, :] = refs[n][...]
        for j in range(fsdp_size):
            for a, lanes, c, packed_lanes in units:
                from_row, to_row = j * shard_width + c, j * piece + a
                down[to_row : to_row + unit_rows, lanes] = weight[
                    from_row : from_row + unit_rows, packed_lanes
                ]

        def row(j, carry):
            here = pl.ds(pl.multiple_of(j * count, count), count)
            hidden, back = hidden_all[here, :], back_all[here, :]
            for c in range(block_ff // step_ff):
                at = slice(c * step_ff, (c + 1) * step_ff)
                up_at = slice(block_ff + c * step_ff, block_ff + (c + 1) * step_ff)
                gate = dot(hidden, weight[:, at])
                up = dot(hidden, weight[:, up_at])
                hidden_back = dot_rt(back, down[at, :])
                sigmoid = jax.nn.sigmoid(gate)
                silu = gate * sigmoid
                three[here, at] = (silu * up).astype(BF)
                slope = sigmoid * (1.0 + gate * (1.0 - sigmoid))
                both_back[here, at] = (hidden_back * up * slope).astype(BF)
                both_back[here, up_at] = (hidden_back * silu).astype(BF)
            parts[j] = dot_rt(both_back[here, :], weight[:, : 2 * block_ff])
            return carry

        lax.fori_loop(0, rep_size, row, 0)
        store_parts(parts, parts_out)

    hidden_two_all, hidden_three, both_back, down_block, *back_parts = call(
        order,
        feed_kernel,
        "feed_forward",
        [],
        hidden_two_rows + [feed_back_all, feed_block],
        [
            ((flat, width), BF),
            ((flat, block_ff), BF),
            ((flat, 2 * block_ff), BF),
            ((block_ff, width), BF),
        ]
        + part_shapes(rep_size, count, width),
        60.0,
        scratch=[((rep_size, count, width), F32)],
        limit=44,
        near=range(2, 2 * rep_size),
    )
    back_addends = send(back_parts, "rep", rep_size)

    def sent_gradient(value):
        return lax.psum_scatter(value, "fsdp", scatter_dimension=0, tiled=True)

    def feed_gradient_kernel(hidden_all, back_all, three, both_back, out):
        step_width = width // 3
        for m in range(3):
            at = slice(m * step_width, (m + 1) * step_width)
            out[at, : 2 * block_ff] = dot_lt(hidden_all[:, at], both_back[...]).astype(BF)
        together = max(1, fsdp_size // 2)
        for first in range(0, fsdp_size, together):
            gradient = dot_lt(
                three[:, first * piece : (first + together) * piece], back_all[...]
            ).astype(BF)
            for j in range(together):
                for a, lanes, c, packed_lanes in units:
                    to_row = (first + j) * shard_width + c
                    out[to_row : to_row + unit_rows, packed_lanes] = gradient[
                        j * piece + a : j * piece + a + unit_rows, lanes
                    ]

    (feed_gradient,) = call(
        order,
        feed_gradient_kernel,
        "feed_gradient",
        [],
        [wait_for(hidden_two_all, all_activated), feed_back_all, hidden_three, both_back],
        [((width, 3 * block_ff), BF)],
        12.0,
        limit=36,
    )
    feed_sum = sent_gradient(feed_gradient)

    def middle_back_kernel(*refs):
        addends = refs[:rep_size]
        cotangent_ref, places, modulation, normed_ref, inverse_ref, branch_ref, weight = refs[
            rep_size : rep_size + 7
        ]
        middle_back, branch_back, sums_out, bias_out, heads_out, sums = refs[
            rep_size + 7 :
        ]
        sums[...] = jnp.zeros_like(sums)

        def step(here):
            slot_of = places[0, here, 0:1]
            upstream = addends[0][here, :]
            for ref in addends[1:]:
                upstream = upstream + ref[here, :].astype(F32)
            normed = normed_ref[here, :]
            masked = cotangent_ref[here, :].astype(F32) * places[0, here, 3:4]
            scale = pick(modulation, slot_of, 4 * width, width)
            back = masked + normalize_back(normed, inverse_ref[here, :], upstream * (1.0 + scale))
            middle_back[here, :] = back
            gate = pick(modulation, slot_of, 2 * width, width)
            low = (back * gate).astype(BF)
            branch_back[here, :] = low
            add_slots(sums, 0, slots, slot_of, back * branch_ref[here, :])
            add_slots(sums, slots, slots, slot_of, upstream)
            add_slots(sums, 2 * slots, slots, slot_of, upstream * normed)
            sums[3 * slots] += jnp.sum(low.astype(F32).reshape(CHUNK // 8, 8, width), axis=0)

        chunks(count, step)
        total = jnp.sum(sums[...], axis=1)
        sums_out[...] = total[: 3 * slots]
        bias_out[...] = total[3 * slots :]
        heads = dot_rt(branch_back[...], weight[...])
        for k in range(rep_size):
            to, at = slice(k * count, (k + 1) * count), slice(k * block, (k + 1) * block)
            heads_out[to, :] = heads[:, at].astype(BF)

    middle_back, branch_back, middle_sums, output_bias_sum, sent_heads = call(
        order,
        middle_back_kernel,
        "second_norm_back",
        [],
        back_addends
        + [cotangent, place_columns, modulation, normed_two, inverse_two, branch, out_full],
        [
            ((count, width), F32),
            ((count, width), BF),
            ((3 * slots, width), F32),
            ((1, width), F32),
            ((flat, block), BF),
        ],
        150.0,
        scratch=[((3 * slots + 1, 8, width), F32)],
        limit=28,
        near=range(1, rep_size),
    )
    heads_back = exchange(sent_heads, "rep")

    def output_gradient_kernel(attended_ref, back_ref, out):
        out[...] = dot_lt(attended_ref[...], back_ref[...]).astype(BF)

    (output_part,) = call(
        order,
        output_gradient_kernel,
        "output_gradient",
        [],
        [attended, branch_back],
        [((width, width), BF)],
        3.7,
        limit=24,
    )
    output_sum = sent_gradient(output_part)

    def feed_out_kernel(three, down, *outs):
        for j in range(rep_size):
            rows_here = slice(j * count, (j + 1) * count)
            outs[j][...] = dot(three[rows_here, :], down[...]).astype(outs[j].dtype)

    feed_parts = call(
        order,
        feed_out_kernel,
        "feed_out",
        [],
        [hidden_three, down_block],
        part_shapes(rep_size, count, width),
        5.0,
        limit=24,
    )
    feed_addends = send(wait_for(list(feed_parts), heads_back), "rep", rep_size)

    def attention_back_kernel(r_ref, *refs):
        heads, query_ref, key_ref, value_ref, wide, tables_ref = refs[:6]
        column_ref, row_ref, projected_back, bias_out = refs[6:10]
        parts_out = refs[10:-2]
        parts, head_stack = refs[-2:]
        if padded > block:
            head_stack[:, :, block:] = jnp.zeros((rep_size, count, padded - block), BF)
        for j in range(rep_size):
            owner = pl.ds(pl.multiple_of((r_ref[0] ^ j) * count, count), count)
            head_stack[j, :, :block] = heads[owner, :]
        bias_out[...] = jnp.zeros_like(bias_out)

        def row(j, carry):
            here = pl.ds(pl.multiple_of(j * count, count), count)
            query, key, value, back = query_ref[j], key_ref[j], value_ref[j], head_stack[j]
            same = column_ref[j, :, 0:1] == row_ref[j, 0:1, :]
            query_back = jnp.zeros((count, padded), F32)
            key_back = jnp.zeros((count, padded), F32)
            value_back = jnp.zeros((count, padded), F32)
            for h in range(local_heads):
                mask = head_mask(h)
                query_head, back_head = query * mask, back * mask
                probs = probabilities(query_head, key, same)
                probs_back = dot_rt(back_head, value)
                scores_back = (
                    probs
                    * (probs_back - jnp.sum(probs * probs_back, axis=-1, keepdims=True))
                ).astype(BF)
                value_back = value_back + dot_lt(probs.astype(BF), back_head)
                query_back = query_back + dot(scores_back, key * mask)
                key_back = key_back + dot_lt(scores_back, query_head)
            cos_row, sin_row = rotary(tables_ref, column_ref[j])
            query_back = turn(query_back * score_scale, cos_row, sin_row, -1.0)
            key_back = turn(key_back * score_scale, cos_row, sin_row, -1.0)
            low = [value.astype(BF) for value in (query_back, key_back, value_back)]
            for t in range(3):
                projected_back[here, t * block : (t + 1) * block] = low[t][:, :block]
                bias_out[:, t * padded : (t + 1) * padded] += jnp.sum(
                    low[t].astype(F32), axis=0, keepdims=True
                )
            parts[j] = dot_rt(jnp.concatenate(low, axis=1), wide[...])
            return carry

        lax.fori_loop(0, rep_size, row, 0)
        store_parts(parts, parts_out)

    projected_back, projection_bias_sum, *one_parts = call(
        order,
        attention_back_kernel,
        "attention_back",
        [r_index],
        [heads_back, query_all, key_all, value_all, wide_weight, tables]
        + [place_columns, place_rows],
        [((flat, 3 * block), BF), ((1, 3 * padded), F32)] + part_shapes(rep_size, count, width),
        90.0,
        scratch=[((rep_size, count, width), F32), ((rep_size, count, padded), BF)],
        limit=44,
    )
    one_addends = send(one_parts, "rep", rep_size)

    def attention_gradient_kernel(hidden_all, back, out):
        step_width = width // 3
        for m in range(3):
            at = slice(m * step_width, (m + 1) * step_width)
            out[at, :] = dot_lt(hidden_all[:, at], back[...]).astype(BF)

    (attention_gradient,) = call(
        order,
        attention_gradient_kernel,
        "attention_gradient",
        [],
        [wait_for(hidden_one_all, feed_addends), projected_back],
        [((width, 3 * block), BF)],
        6.4,
        limit=32,
    )
    attention_sum = sent_gradient(attention_gradient)

    def output_kernel(*refs):
        feeds = refs[:rep_size]
        tokens_ref, branch_ref, cotangent_ref, places, modulation = refs[rep_size : rep_size + 5]
        block_out, sums_out, sums = refs[rep_size + 5 :]
        sums[...] = jnp.zeros_like(sums)

        def step(here):
            slot_of = places[0, here, 0:1]
            feed = feeds[0][here, :]
            for ref in feeds[1:]:
                feed = feed + ref[here, :].astype(F32)
            gate_one = pick(modulation, slot_of, 2 * width, width)
            middle = tokens_ref[here, :].astype(F32) + gate_one * branch_ref[here, :]
            gate_two = pick(modulation, slot_of, 5 * width, width)
            block_out[here, :] = (middle + gate_two * feed).astype(BF)
            masked = cotangent_ref[here, :].astype(F32) * places[0, here, 3:4]
            add_slots(sums, 0, slots, slot_of, masked * feed)

        chunks(count, step)
        sums_out[...] = jnp.sum(sums[...], axis=1)

    block_output, gate_two_sums = call(
        order,
        output_kernel,
        "layer_output",
        [],
        feed_addends + [tokens, branch, cotangent, place_columns, modulation],
        [((count, width), BF), ((slots, width), F32)],
        4.5,
        scratch=[((slots, 8, width), F32)],
        limit=16,
        near=range(1, rep_size),
    )

    def first_back_kernel(r_ref, *refs):
        addends = refs[:rep_size]
        tokens_ref, back_ref, modulation, places, middle_ref, gate_two_ref, bias, out_bias = refs[
            rep_size : rep_size + 8
        ]
        gradient, back_blocks, sums, whole, whole_bias, stack = refs[rep_size + 8 :]
        sums[...] = jnp.zeros_like(sums)

        def step(here):
            slot_of = places[0, here, 0:1]
            upstream = addends[0][here, :]
            for ref in addends[1:]:
                upstream = upstream + ref[here, :].astype(F32)
            normed, inverse = normalize_keep(tokens_ref[here, :].astype(F32))
            scale = pick(modulation, slot_of, width, width)
            gradient[here, :] = back_ref[here, :] + normalize_back(
                normed, inverse, upstream * (1.0 + scale)
            )
            add_slots(sums, 0, slots, slot_of, upstream)
            add_slots(sums, slots, slots, slot_of, upstream * normed)

        chunks(count, step)
        total = jnp.sum(sums[...], axis=1)
        whole[:, :width] = total[:slots]
        whole[:, width : 2 * width] = total[slots:]
        for t in range(3):
            at = slice((2 + t) * width, (3 + t) * width)
            whole[:, at] = middle_ref[t * slots : (t + 1) * slots, :]
        whole[:, 5 * width :] = gate_two_ref[...]
        whole_bias[...] = jnp.zeros_like(whole_bias)
        for k in range(rep_size):

            @pl.when(r_ref[0] == k)
            def _():
                for t in range(3):
                    first = t * width + k * block
                    whole_bias[:, first : first + block] = bias[:, t * padded : t * padded + block]

        stack[...] = jnp.zeros_like(stack)
        for k in range(fsdp_size):
            stack[k, :slots, :] = whole[:, k * columns : (k + 1) * columns]
            at = slice(k * shard_bias, (k + 1) * shard_bias)
            stack[k, slots : slots + 1, :shard_bias] = whole_bias[:, at]
            at = slice(k * shard_out_bias, (k + 1) * shard_out_bias)
            lanes = slice(shard_bias, shard_bias + shard_out_bias)
            stack[k, slots : slots + 1, lanes] = out_bias[:, at]
        back_blocks[...] = stack[...].reshape(fsdp_size * GROUP, columns).astype(BF)

    tokens_gradient, back_blocks = call(
        order,
        first_back_kernel,
        "first_norm_back",
        [r_index],
        one_addends
        + [tokens, middle_back, modulation, place_columns, middle_sums, gate_two_sums]
        + [projection_bias_sum, output_bias_sum],
        [((count, width), F32), ((fsdp_size * GROUP, columns), BF)],
        25.0,
        scratch=[
            ((2 * slots, 8, width), F32),
            ((slots, 6 * width), F32),
            ((1, 3 * width), F32),
            ((fsdp_size, GROUP, columns), F32),
        ],
        limit=20,
        near=range(1, rep_size),
    )

    line_backs = exchange(back_blocks, "fsdp")
    feed_sums = gather(wait_for(feed_sum, one_addends), "rep", rep_size)

    output_gradient, came_outputs = wait_for(output_sum, feed_sum).astype(F32), []
    for bit in [1 << k for k in range(rep_size.bit_length() - 1)]:
        came_outputs.append(swap_with(output_gradient.astype(BF), "rep", rep_size, bit))
        output_gradient = output_gradient + came_outputs[-1].astype(F32)

    def conditioning_kernel(groups, weight, out, line_out):
        stack = groups[...].astype(F32)
        bias = jnp.sum(stack.reshape(fsdp_size, GROUP, columns), axis=0)[slots : slots + 1]
        row_ids = lax.broadcasted_iota(jnp.int32, (fsdp_size * GROUP, 1), 0)
        rows_back = jnp.where(lax.rem(row_ids, GROUP) < slots, stack, 0.0)
        line_out[...] = jnp.where(row_ids == slots, bias, rows_back).astype(BF)
        result = dot(rows_back.astype(BF), weight[...])
        for k in range(fsdp_size):
            out[k * slots : (k + 1) * slots, :] = result[k * GROUP : k * GROUP + slots, :]

    activated_backs, line_back = call(
        order,
        conditioning_kernel,
        "conditioning_back",
        [],
        [wait_for(line_backs, feed_sums[1:3], came_outputs[0]), modulation_weight.T],
        [((fsdp_size * slots, width), F32), ((fsdp_size * GROUP, columns), BF)],
        30.0,
        limit=24,
    )
    activated_backs = exchange(activated_backs, "fsdp")
    all_backs = gather(line_back, "rep", rep_size)
    activated_back = jnp.sum(activated_backs.reshape(fsdp_size, slots, width), axis=0)
    conditioning_gradient = activated_back.reshape(rows, slots, width) * silu_slope(cond_float)

    def feed_blocks_kernel(r_ref, *refs):
        gate_out, up_out, down_out, stack = refs[rep_size:]
        for j in range(rep_size):
            stack[j] = refs[j][...].astype(F32)
        for k in range(rep_size):
            here = r_ref[0] ^ k
            for j in range(fsdp_size):
                target = slice(j * shard_ff + k * piece, j * shard_ff + (k + 1) * piece)
                first = block_ff + j * piece
                gate_out[:, target] = stack[here, :, j * piece : (j + 1) * piece]
                up_out[:, target] = stack[here, :, first : first + piece]
            for a, lanes, c, packed_lanes in units:
                to_row = k * piece + a
                down_out[to_row : to_row + unit_rows, lanes] = stack[
                    here, c : c + unit_rows, packed_lanes
                ]

    gate_gradient, up_gradient, down_gradient = call(
        order,
        feed_blocks_kernel,
        "feed_blocks",
        [r_index],
        feed_sums,
        [((shard_width, fsdp_size * shard_ff), F32)] * 2 + [((shard_ff, width), F32)],
        5.2,
        scratch=[((rep_size, shard_width, 3 * block_ff), F32)],
        limit=24,
        near=range(1, rep_size),
    )

    def table_kernel(*refs):
        activateds, backs = refs[:rep_size], refs[rep_size : 2 * rep_size]
        table, table_bias, bias, out_bias, activated_stack, back_stack = refs[2 * rep_size :]
        line = fsdp_size * GROUP
        total = jnp.zeros((1, columns), F32)
        for j in range(rep_size):
            activated_stack[j * line : (j + 1) * line, :] = activateds[j][...]
            back_stack[j * line : (j + 1) * line, :] = backs[j][...]
            total = total + backs[j][...].astype(F32)[slots : slots + 1, :]
        bias[...] = total[:, :shard_bias]
        out_bias[...] = total[:, shard_bias : shard_bias + shard_out_bias]
        back = back_stack[...].astype(F32)
        in_group = lax.rem(lax.broadcasted_iota(jnp.int32, (rep_size * line, 1), 0), GROUP)
        table_bias[...] = jnp.sum(
            jnp.where(in_group < slots, back, 0.0), axis=0, keepdims=True
        )
        table[...] = dot_lt(back_stack[...], activated_stack[...])

    table_gradient, table_bias_gradient, bias_gradient, out_bias_gradient = call(
        order,
        table_kernel,
        "table_gradient",
        [],
        wait_for(all_activated, came_outputs) + all_backs,
        [((columns, width), F32), ((1, columns), F32)]
        + [((1, shard_bias), F32), ((1, shard_out_bias), F32)],
        4.0,
        scratch=[
            ((rep_size * fsdp_size * GROUP, width), BF),
            ((rep_size * fsdp_size * GROUP, columns), BF),
        ],
        limit=24,
        near=range(1, rep_size),
    )

    def attention_blocks_kernel(r_ref, *refs):
        projection_out, stack = refs[rep_size:]
        for j in range(rep_size):
            stack[j] = refs[j][...].astype(F32)
        for k in range(rep_size):
            here = r_ref[0] ^ k
            for t in range(3):
                first = t * width + k * block
                projection_out[:, first : first + block] = stack[
                    here, :, t * block : (t + 1) * block
                ]

    (projection_gradient,) = call(
        order,
        attention_blocks_kernel,
        "attention_blocks",
        [r_index],
        gather(wait_for(attention_sum, gate_gradient), "rep", rep_size),
        [((shard_width, 3 * width), F32)],
        3.0,
        scratch=[((rep_size, shard_width, 3 * block), F32)],
        limit=24,
        near=range(1, rep_size),
    )
    return (
        block_output[None],
        tokens_gradient[None],
        conditioning_gradient,
        table_gradient.T,
        table_bias_gradient[0],
        projection_gradient,
        bias_gradient[0],
        output_gradient,
        out_bias_gradient[0],
        gate_gradient,
        up_gradient,
        down_gradient,
    )


def solution(mesh):
    sizes = dict(mesh.shape)

    def body(*arrays):
        return on_device(sizes["rep"], sizes["fsdp"], *arrays)

    rows = ("rep", "fsdp")
    in_specs = (
        P(rows, None, None),
        P(rows, None, None),
        P(rows, None),
        P(rows, None),
        P(rows, None),
        P(rows, None),
        P(None, "fsdp"),
        P("fsdp"),
        P("fsdp", None),
        P("fsdp"),
        P("fsdp", None),
        P("fsdp"),
        P("fsdp", None),
        P("fsdp", None),
        P("fsdp", None),
        P(rows, None, None),
    )
    out_specs = (
        P(rows, None, None),
        P(rows, None, None),
        P(rows, None, None),
        P(None, "fsdp"),
        P("fsdp"),
        P("fsdp", None),
        P("fsdp"),
        P("fsdp", None),
        P("fsdp"),
        P("fsdp", None),
        P("fsdp", None),
        P("fsdp", None),
    )
    return jax.shard_map(
        body, mesh=mesh, in_specs=in_specs, out_specs=out_specs, check_vma=False
    )
```

```python
import math

import jax
import jax.numpy as jnp
import numpy as np
from jax import lax
from jax.experimental import pallas as pl
from jax.experimental.pallas import tpu as pltpu
from jax.sharding import PartitionSpec as P

HEADS = 16
BF = jnp.bfloat16
F32 = jnp.float32
LANES = 128
CHUNK = 32
GROUP = 8


def wait_for(value, *others):
    return lax.optimization_barrier((value, others))[0]


def swap_with(value, axis, size, bit):
    return lax.ppermute(value, axis, [(i, i ^ bit) for i in range(size)])


def gather(value, axis, size):
    return [value] + [swap_with(value, axis, size, j) for j in range(1, size)]


def halves_gather(top, low, axis, size):
    if size != 4:
        return list(zip(gather(top, axis, size), gather(low, axis, size), strict=True))
    top_one, low_two = swap_with(top, axis, size, 1), swap_with(low, axis, size, 2)
    top_three, low_three = swap_with(top_one, axis, size, 2), swap_with(low_two, axis, size, 1)
    low_one, top_two = swap_with(low, axis, size, 1), swap_with(top, axis, size, 2)
    return [(top, low), (top_one, low_one), (top_two, low_two), (top_three, low_three)]


def send(values, axis, size):
    return [values[0]] + [swap_with(values[j], axis, size, j) for j in range(1, size)]


def exchange(value, axis):
    return lax.all_to_all(value, axis, 0, 0, tiled=True)


def block_of(shape, by_step):
    if by_step:
        return pl.BlockSpec(shape, lambda i: (i,) + (0,) * (len(shape) - 1))
    zeros = (0,) * len(shape)
    return pl.BlockSpec(shape, lambda i: zeros, pipeline_mode=pl.Buffered(1))


def call(order, body, name, scalars, arrays, outs, micros, scratch=(), limit=48, near=(), steps=1):
    shapes = [pltpu.HBM(out[0], out[1]) for out in outs]
    out_specs = [block_of(out[-1], True) if len(out) > 2 else block_of(out[0], False) for out in outs]
    in_specs = [
        block_of(array[1], len(array) > 2) if isinstance(array, tuple) else block_of(array.shape, False)
        for array in arrays
    ]
    arrays = [array[0] if isinstance(array, tuple) else array for array in arrays]
    if order:
        first, _ = lax.optimization_barrier((arrays[0], order.pop()))
        arrays = [first] + list(arrays[1:])
    arrays = [
        array if n in near else pltpu.with_memory_space_constraint(array, pltpu.HBM)
        for n, array in enumerate(arrays)
    ]
    results = pl.pallas_call(
        body,
        name=name,
        grid=(steps,),
        out_shape=shapes,
        in_specs=[pl.BlockSpec(memory_space=pltpu.SMEM)] * len(scalars)
        + in_specs,
        out_specs=out_specs,
        scratch_shapes=[pltpu.VMEM(shape, dtype) for shape, dtype in scratch],
        compiler_params=pltpu.CompilerParams(vmem_limit_bytes=limit << 20),
        cost_estimate=pl.CostEstimate(
            flops=int(micros * 1.000e+09), bytes_accessed=int(micros * 3.000e+06), transcendentals=0
        ),
    )(*scalars, *arrays)
    order.append(results[0])
    return results


def part_shapes(size, tokens, width):
    return [((tokens, width), F32)] + [((tokens, width), BF)] * (size - 1)


def store_part(j, value, refs):
    for k, ref in enumerate(refs):

        @pl.when(j == k)
        def _(ref=ref):
            ref[...] = value.astype(ref.dtype)


def dot(left, right):
    return jnp.dot(left, right, preferred_element_type=F32)


def dot_rt(left, right):
    return lax.dot_general(left, right, (((1,), (1,)), ((), ())), preferred_element_type=F32)


def dot_lt(left, right):
    return lax.dot_general(left, right, (((0,), (0,)), ((), ())), preferred_element_type=F32)


def pick(modulation, slot_of, first, width):
    total = jnp.zeros((slot_of.shape[0], width), F32)
    for k in range(modulation.shape[0]):
        total = jnp.where(slot_of == k, modulation[k : k + 1, first : first + width], total)
    return total


def normalize_keep(values):
    centered = values - jnp.mean(values, axis=-1, keepdims=True)
    variance = jnp.mean(centered * centered, axis=-1, keepdims=True)
    inverse = lax.rsqrt(variance + 1e-06)
    return centered * inverse, inverse


def normalize_back(normed, inverse, upstream):
    return inverse * (
        upstream
        - jnp.mean(upstream, axis=-1, keepdims=True)
        - normed * jnp.mean(upstream * normed, axis=-1, keepdims=True)
    )


def add_slots(sums, base, count, slot_of, values):
    rows, width = values.shape
    for k in range(count):
        chosen = jnp.where(slot_of == k, values, 0.0)
        sums[base + k] += jnp.sum(chosen.reshape(rows // 8, 8, width), axis=0)


def chunks(tokens, step, unroll=2):
    def body(i, carry):
        step(pl.ds(pl.multiple_of(i * CHUNK, CHUNK), CHUNK))
        return carry

    lax.fori_loop(0, tokens // CHUNK, body, 0, unroll=unroll)


def silu_slope(values):
    sigmoid = jax.nn.sigmoid(values)
    return sigmoid * (1.0 + values * (1.0 - sigmoid))


def on_device(
    rep_size,
    fsdp_size,
    tokens,
    conditioning,
    segment_ids,
    heights,
    widths,
    pad_mask,
    modulation_weight,
    modulation_bias,
    projection_weight,
    projection_bias,
    output_weight,
    output_bias,
    gate_weight,
    up_weight,
    down_weight,
    cotangent,
):
    rows, count, width = tokens.shape
    assert rows == 1
    slots = conditioning.shape[1]
    head_width = width // HEADS
    local_heads = HEADS // rep_size
    block = width // rep_size
    padded = -(-block // LANES) * LANES
    score_scale = 1.0 / math.sqrt(head_width)
    shard_ff = down_weight.shape[0]
    piece = shard_ff // rep_size
    block_ff = fsdp_size * piece
    shard_width = projection_weight.shape[0]
    columns = modulation_weight.shape[1]
    flat = rep_size * count
    half = count // 2
    group_tokens = count // rep_size
    others = rep_size - 1
    r = lax.axis_index("rep")
    r_index = r.reshape(1).astype(jnp.int32)
    tokens, cotangent = tokens[0], cotangent[0]
    order = []

    def qkv_shard_kernel(r_ref, projection, output, out):
        out[:, :width] = output[...]
        for k in range(rep_size):

            @pl.when(r_ref[0] == k)
            def _():
                for t in range(3):
                    first, to = t * width + k * block, width + t * block
                    out[:, to : to + block] = projection[:, first : first + block]

    (qkv_shard,) = call(
        order,
        qkv_shard_kernel,
        "qkv_shard",
        [r_index],
        [projection_weight, output_weight],
        [((shard_width, width + 3 * block), BF)],
        4.5,
        limit=16,
    )

    slot_ids = jnp.arange(slots, dtype=jnp.int32)
    member_ints = (segment_ids[:, :, None] == slot_ids).astype(jnp.int32)
    before_ints = (slot_ids < segment_ids[:, :, None]).astype(jnp.int32)
    starts = jnp.sum(before_ints * (heights * widths)[:, None, :], axis=2)
    offsets = jnp.arange(count, dtype=jnp.int32)[None, :] - starts
    row_width = jnp.sum(member_ints * widths[:, None, :], axis=2)
    places = jnp.concatenate(
        [segment_ids, offsets // row_width, offsets % row_width, pad_mask], axis=1
    ).astype(BF)
    places = jnp.pad(places, ((0, GROUP - 1), (0, width - 4 * count)))
    token_rows = gather(jnp.concatenate([tokens, places], axis=0), "rep", rep_size)

    cond_float = conditioning.astype(F32)
    activated = jax.nn.silu(cond_float).astype(BF).reshape(slots, width)
    shard_bias, shard_out_bias = projection_bias.shape[0], output_bias.shape[0]
    bias_row = jnp.pad(
        jnp.concatenate([projection_bias, output_bias]), (0, width - shard_bias - shard_out_bias)
    )[None]
    group_rows = jnp.concatenate(
        [activated, bias_row, jnp.zeros((GROUP - slots - 1, width), BF)], axis=0
    )
    line_rows = lax.all_gather(group_rows, "fsdp", axis=0, tiled=True)

    def modulate_kernel(r_ref, *refs):
        groups, weight, bias = refs[:3]
        out, activated_out, bias_out, out_bias, stack, whole = refs[3:]
        stack[...] = groups[...].astype(F32).reshape(fsdp_size, GROUP, width)
        in_group = lax.rem(lax.broadcasted_iota(jnp.int32, (fsdp_size * GROUP, 1), 0), GROUP)
        rows_low = jnp.where(in_group < slots, groups[...].astype(F32), 0.0).astype(BF)
        activated_out[...] = rows_low
        out[...] = dot_rt(rows_low, weight[...]) + bias[...]
        for k in range(fsdp_size):
            row = stack[k, slots : slots + 1, :]
            whole[:, k * shard_bias : (k + 1) * shard_bias] = row[:, :shard_bias]
            at = slice(k * shard_out_bias, (k + 1) * shard_out_bias)
            out_bias[:, at] = row[:, shard_bias : shard_bias + shard_out_bias]
        bias_out[...] = jnp.zeros_like(bias_out)
        for k in range(rep_size):

            @pl.when(r_ref[0] == k)
            def _():
                for t in range(3):
                    first = t * width + k * block
                    bias_out[:, t * padded : t * padded + block] = whole[:, first : first + block]

    line_modulation, line_activated, own_bias, output_bias_all = call(
        order,
        modulate_kernel,
        "modulate",
        [r_index],
        [line_rows, modulation_weight.T, modulation_bias.astype(F32)[None]],
        [
            ((fsdp_size * GROUP, columns), F32),
            ((fsdp_size * GROUP, width), BF),
            ((1, 3 * padded), F32),
            ((1, width), F32),
        ],
        6.0,
        scratch=[((fsdp_size, GROUP, width), F32), ((1, 3 * width), F32)],
        limit=24,
    )
    own_modulation = lax.all_to_all(line_modulation, "fsdp", 0, 0, tiled=True)

    unit_rows, unit_lanes = math.gcd(piece, shard_width), math.gcd(width, block_ff)
    units = []
    for u in range((piece // unit_rows) * (width // unit_lanes)):
        (a, b), (c, d) = divmod(u, width // unit_lanes), divmod(u, block_ff // unit_lanes)
        units.append(
            (
                a * unit_rows,
                slice(b * unit_lanes, (b + 1) * unit_lanes),
                c * unit_rows,
                slice(2 * block_ff + d * unit_lanes, 2 * block_ff + (d + 1) * unit_lanes),
            )
        )

    def feed_shard_kernel(r_ref, gate, up, down, out):
        for k in range(rep_size):

            @pl.when(r_ref[0] == k)
            def _():
                for j in range(fsdp_size):
                    source = slice(j * shard_ff + k * piece, j * shard_ff + (k + 1) * piece)
                    out[:, j * piece : (j + 1) * piece] = gate[:, source]
                    first = block_ff + j * piece
                    out[:, first : first + piece] = up[:, source]
                for a, lanes, c, packed_lanes in units:
                    out[c : c + unit_rows, packed_lanes] = down[
                        k * piece + a : k * piece + a + unit_rows, lanes
                    ]

    (feed_shard,) = call(
        order,
        feed_shard_kernel,
        "feed_shard",
        [r_index],
        [gate_weight, up_weight, down_weight],
        [((shard_width, 3 * block_ff), BF)],
        4.5,
        limit=16,
    )
    qkv_block = lax.all_gather(qkv_shard, "fsdp", axis=0, tiled=True)
    feed_block = lax.all_gather(feed_shard, "fsdp", axis=0, tiled=True)

    def norm_rows_kernel(*refs):
        out, columns_out, rows_out = refs[rep_size:]
        for j in range(rep_size):
            ref = refs[j]

            def step(at, ref=ref, j=j):
                normed, _ = normalize_keep(ref[at, :].astype(F32))
                out[pl.ds(j * count + at.start, CHUNK), :] = normed

            chunks(count, step)
            line = ref[count:, :].astype(F32)
            for q in range(4):
                rows_out[j, q : q + 1, :] = line[:1, q * count : (q + 1) * count]
            rows_out[j, 4:, :] = jnp.zeros((4, count), F32)
            columns_out[j] = rows_out[j].T

    normed_rows, place_columns, place_rows = call(
        order,
        norm_rows_kernel,
        "first_norm",
        [],
        token_rows,
        [((flat, width), F32), ((rep_size, count, 8), F32), ((rep_size, 8, count), F32)],
        18.0,
        limit=24,
        near=range(1, rep_size),
    )
    pair_count = head_width // 4
    most_rows, most_columns = count // 4, 32
    lane = np.arange(padded)
    in_head = lane % head_width
    lane_frequency = 10000.0 ** (-(in_head % pair_count) / pair_count)
    of_row = (lane < block) & (in_head < 2 * pair_count)
    of_column = (lane < block) & (in_head >= 2 * pair_count)
    sign = np.where((in_head // pair_count) % 2 == 1, 1.0, -1.0)
    row_angle = np.arange(most_rows)[:, None] * lane_frequency
    column_angle = np.arange(most_columns)[:, None] * lane_frequency
    tables = np.concatenate(
        [
            np.concatenate(
                [
                    np.where(of_row, np.cos(row_angle), 0.0),
                    np.where(of_column, np.cos(column_angle), 0.0),
                ]
            ),
            np.concatenate(
                [
                    np.where(of_row, sign * np.sin(row_angle), 0.0),
                    np.where(of_column, sign * np.sin(column_angle), 0.0),
                ]
            ),
        ],
        axis=1,
    ).astype(np.float32)
    pieces, left = [], tables
    for _ in range(3):
        pieces.append(left.astype(jnp.bfloat16))
        left = left - pieces[-1].astype(np.float32)
    tables = jnp.asarray(np.stack(pieces))

    def rotary(tables_ref, places):
        numbers = lax.broadcasted_iota(jnp.int32, (count, most_rows + most_columns), 1).astype(F32)
        is_row = (numbers < most_rows) & (numbers == places[:, 1:2])
        is_column = (numbers >= most_rows) & (numbers - most_rows == places[:, 2:3])
        chosen = jnp.where(is_row | is_column, 1.0, 0.0).astype(BF)
        both = dot(chosen, tables_ref[2]) + dot(chosen, tables_ref[1]) + dot(chosen, tables_ref[0])
        return both[:, :padded], both[:, padded:]

    def modulation_kernel(arrived, modulation, sent):
        for k in range(fsdp_size):
            at = slice(k * columns, (k + 1) * columns)
            modulation[:, at] = arrived[k * GROUP : k * GROUP + slots, :]
        sent[:, : 2 * width] = modulation[:, : 2 * width]
        sent[:, 2 * width :] = modulation[:, 5 * width :]

    modulation, sent_modulation = call(
        order,
        modulation_kernel,
        "modulation",
        [],
        [wait_for(own_modulation, normed_rows)],
        [((slots, 6 * width), F32), ((slots, 3 * width), F32)],
        3.0,
        limit=8,
    )
    modulation_rows = gather(sent_modulation, "rep", rep_size)
    cotangent_rows = gather(wait_for(cotangent, modulation_rows), "rep", rep_size)

    def head_mask(h):
        lanes = lax.broadcasted_iota(jnp.int32, (1, padded), 1)
        inside = (lanes >= h * head_width) & (lanes < (h + 1) * head_width)
        return jnp.where(inside, 1.0, 0.0).astype(BF)

    def probabilities(query_head, key, same):
        scores = jnp.where(same, dot_rt(query_head, key) * score_scale, -1e30)
        exponent = jnp.exp(scores - jnp.max(scores, axis=-1, keepdims=True))
        return exponent / jnp.sum(exponent, axis=-1, keepdims=True)

    def turn(values, cosine_row, sine_row, sense):
        before = pltpu.roll(values, pair_count, 1)
        after = pltpu.roll(values, padded - pair_count, 1)
        lanes = lax.broadcasted_iota(jnp.int32, (1, padded), 1)
        second = lax.rem(lanes, 2 * pair_count) >= pair_count
        return values * cosine_row + jnp.where(second, before, after) * (sense * sine_row)

    def attention_kernel(r_ref, *refs):
        modulations = refs[:rep_size]
        normed, weight, bias, tables_ref, column_ref, row_ref = refs[rep_size : rep_size + 6]
        hidden_all, wide, query_out, key_out, value_out, attended_out, modulation_stack = refs[
            rep_size + 6 :
        ]
        for j in range(rep_size):
            modulation_stack[j] = modulations[j][:, : 2 * width]
        for t in range(3):
            first = width + t * block
            wide[:, t * padded : t * padded + block] = weight[:, first : first + block]
            if padded > block:
                wide[:, t * padded + block : (t + 1) * padded] = jnp.zeros(
                    (width, padded - block), BF
                )

        def row(j, carry):
            first = pl.multiple_of(j * count, count)

            def step(at):
                here = pl.ds(pl.multiple_of(first + at.start, CHUNK), CHUNK)
                slot_of = column_ref[j, at, 0:1]
                scale = pick(modulation_stack[j], slot_of, width, width)
                shift = pick(modulation_stack[j], slot_of, 0, width)
                hidden_all[here, :] = (normed[here, :] * (1.0 + scale) + shift).astype(BF)

            chunks(count, step)
            projected = dot(hidden_all[pl.ds(first, count), :], wide[...]) + bias[...]
            cos_row, sin_row = rotary(tables_ref, column_ref[j])
            query = turn(projected[:, :padded], cos_row, sin_row, 1.0).astype(BF)
            key = turn(projected[:, padded : 2 * padded], cos_row, sin_row, 1.0).astype(BF)
            value = projected[:, 2 * padded :].astype(BF)
            query_out[j], key_out[j], value_out[j] = query, key, value
            same = column_ref[j, :, 0:1] == row_ref[j, 0:1, :]
            total = jnp.zeros((count, padded), F32)
            for h in range(local_heads):
                mask = head_mask(h)
                probs = probabilities(query * mask, key, same)
                total = total + dot(probs.astype(BF), value * mask)
            owner = pl.ds(pl.multiple_of((r_ref[0] ^ j) * group_tokens, 16), group_tokens)
            low = total[:, :block].astype(BF)
            for g in range(rep_size):
                attended_out[owner, g * block : (g + 1) * block] = low[
                    g * group_tokens : (g + 1) * group_tokens, :
                ]
            return carry

        lax.fori_loop(0, rep_size, row, 0)

    hidden_one_all, wide_weight, query_all, key_all, value_all, attended_heads = call(
        order,
        attention_kernel,
        "attention",
        [r_index],
        modulation_rows
        + [normed_rows, qkv_block, own_bias, tables, place_columns, place_rows],
        [((flat, width), BF), ((width, 3 * padded), BF)]
        + [((rep_size, count, padded), BF)] * 3
        + [((count, width), BF)],
        66.0,
        scratch=[((rep_size, slots, 2 * width), F32)],
        limit=44,
        near=range(1, rep_size),
    )
    own_heads = exchange(attended_heads, "rep")

    def feed_back_kernel(*refs):
        cotangents, modulations = refs[:rep_size], refs[rep_size : 2 * rep_size]
        columns_ref, out = refs[2 * rep_size :]
        for j in range(rep_size):

            def step(at, j=j):
                masked = cotangents[j][at, :].astype(F32) * columns_ref[j, at, 3:4]
                gate = pick(modulations[j], columns_ref[j, at, 0:1], 2 * width, width)
                out[pl.ds(j * count + at.start, CHUNK), :] = (gate * masked).astype(BF)

            chunks(count, step)

    (feed_back_all,) = call(
        order,
        feed_back_kernel,
        "feed_back",
        [],
        cotangent_rows + modulation_rows + [place_columns],
        [((flat, width), BF)],
        12.0,
        limit=24,
        near=(*range(1, rep_size), *range(rep_size + 1, 2 * rep_size)),
    )

    def middle_kernel(
        heads, weight, bias, tokens_ref, modulation, places, branch, normed_out, inverse_out,
        top, low, attended,
    ):
        for k in range(rep_size):
            for g in range(rep_size):
                attended[
                    g * group_tokens : (g + 1) * group_tokens, k * block : (k + 1) * block
                ] = heads[k * group_tokens : (k + 1) * group_tokens, g * block : (g + 1) * block]
        branch[...] = dot(attended[...], weight[...]) + bias[...]

        for p, hidden in enumerate((top, low)):

            def step(at, p=p, hidden=hidden):
                here = pl.ds(p * half + at.start, CHUNK)
                slot_of = places[0, here, 0:1]
                gate = pick(modulation, slot_of, 2 * width, width)
                middle = tokens_ref[here, :].astype(F32) + gate * branch[here, :]
                normed, inverse = normalize_keep(middle)
                normed_out[here, :] = normed
                inverse_out[here, :] = inverse
                scale = pick(modulation, slot_of, 4 * width, width)
                hidden[at, :] = (
                    normed * (1.0 + scale) + pick(modulation, slot_of, 3 * width, width)
                ).astype(BF)

            chunks(half, step)

    branch, normed_two, inverse_two, hidden_top, hidden_low, attended = call(
        order,
        middle_kernel,
        "second_norm",
        [],
        [own_heads, (qkv_block, (width, width)), output_bias_all, tokens, modulation, place_columns],
        [((count, width), F32), ((count, width), F32), ((count, 1), F32)]
        + [((half, width), BF)] * 2
        + [((count, width), BF)],
        21.0,
        limit=24,
    )
    hidden_two_rows = halves_gather(hidden_top, hidden_low, "rep", rep_size)
    hidden_two_rows = [piece for row in hidden_two_rows for piece in row]


    step_ff = 256 if block_ff % 256 == 0 else 128
    taken = count

    def feed_kernel(*refs):
        back, weight = refs[2 * rep_size : 2 * rep_size + 2]
        hidden_out, three, both_back, down = refs[2 * rep_size + 2 : 2 * rep_size + 6]
        parts_out, hidden_all = refs[2 * rep_size + 6 : -1], refs[-1]
        j = pl.program_id(0)

        @pl.when(j == 0)
        def _():
            for n in range(2 * rep_size):
                hidden_all[n * half : (n + 1) * half, :] = refs[n][...]
            for k in range(fsdp_size):
                for a, lanes, c, packed_lanes in units:
                    from_row, to_row = k * shard_width + c, k * piece + a
                    down[to_row : to_row + unit_rows, lanes] = weight[
                        from_row : from_row + unit_rows, packed_lanes
                    ]

        hidden = hidden_all[pl.ds(pl.multiple_of(j * taken, taken), taken), :]
        hidden_out[...] = hidden
        for c in range(block_ff // step_ff):
            at = slice(c * step_ff, (c + 1) * step_ff)
            up_at = slice(block_ff + c * step_ff, block_ff + (c + 1) * step_ff)
            gate = dot(hidden, weight[:, at])
            up = dot(hidden, weight[:, up_at])
            hidden_back = dot_rt(back[...], down[at, :])
            sigmoid = jax.nn.sigmoid(gate)
            silu = gate * sigmoid
            three[:, at] = (silu * up).astype(BF)
            slope = sigmoid * (1.0 + gate * (1.0 - sigmoid))
            both_back[:, at] = (hidden_back * up * slope).astype(BF)
            both_back[:, up_at] = (hidden_back * silu).astype(BF)
        back_hidden = dot_rt(both_back[...], weight[:, : 2 * block_ff])
        for q in range(taken // count):
            part_rows = back_hidden[q * count : (q + 1) * count, :]
            store_part(j * (taken // count) + q, part_rows, parts_out)

    hidden_two_all, hidden_three, both_back, down_block, *back_parts = call(
        order,
        feed_kernel,
        "feed_forward",
        [],
        hidden_two_rows + [(feed_back_all, (taken, width), True), feed_block],
        [
            ((flat, width), BF, (taken, width)),
            ((flat, block_ff), BF, (taken, block_ff)),
            ((flat, 2 * block_ff), BF, (taken, 2 * block_ff)),
            ((block_ff, width), BF),
        ]
        + part_shapes(rep_size, count, width),
        60.0,
        scratch=[((flat, width), BF)],
        limit=44,
        near=range(2, 2 * rep_size),
        steps=flat // taken,
    )
    back_addends = send(back_parts, "rep", rep_size)

    def sent_gradient(value):
        return lax.psum_scatter(value, "fsdp", scatter_dimension=0, tiled=True)

    def feed_gradient_kernel(hidden_all, back_all, three, both_back, out):
        step_width = width // 3
        for m in range(3):
            at = slice(m * step_width, (m + 1) * step_width)
            out[at, : 2 * block_ff] = dot_lt(hidden_all[:, at], both_back[...]).astype(BF)
        together = max(1, fsdp_size // 2)
        for first in range(0, fsdp_size, together):
            gradient = dot_lt(
                three[:, first * piece : (first + together) * piece], back_all[...]
            ).astype(BF)
            for j in range(together):
                for a, lanes, c, packed_lanes in units:
                    to_row = (first + j) * shard_width + c
                    out[to_row : to_row + unit_rows, packed_lanes] = gradient[
                        j * piece + a : j * piece + a + unit_rows, lanes
                    ]

    (feed_gradient,) = call(
        order,
        feed_gradient_kernel,
        "feed_gradient",
        [],
        [hidden_two_all, feed_back_all, hidden_three, both_back],
        [((width, 3 * block_ff), BF)],
        12.0,
        limit=36,
    )
    feed_sum = sent_gradient(feed_gradient)

    def middle_back_kernel(*refs):
        addends = refs[:rep_size]
        cotangent_ref, places, modulation, normed_ref, inverse_ref, branch_ref, weight = refs[
            rep_size : rep_size + 7
        ]
        middle_back, branch_back, sums_out, bias_out, heads_out, sums = refs[
            rep_size + 7 :
        ]
        sums[...] = jnp.zeros_like(sums)

        def step(here):
            slot_of = places[0, here, 0:1]
            upstream = addends[0][here, :]
            for ref in addends[1:]:
                upstream = upstream + ref[here, :].astype(F32)
            normed = normed_ref[here, :]
            masked = cotangent_ref[here, :].astype(F32) * places[0, here, 3:4]
            scale = pick(modulation, slot_of, 4 * width, width)
            back = masked + normalize_back(normed, inverse_ref[here, :], upstream * (1.0 + scale))
            middle_back[here, :] = back
            gate = pick(modulation, slot_of, 2 * width, width)
            low = (back * gate).astype(BF)
            branch_back[here, :] = low
            add_slots(sums, 0, slots, slot_of, back * branch_ref[here, :])
            add_slots(sums, slots, slots, slot_of, upstream)
            add_slots(sums, 2 * slots, slots, slot_of, upstream * normed)
            sums[3 * slots] += jnp.sum(low.astype(F32).reshape(CHUNK // 8, 8, width), axis=0)

        chunks(count, step, 1)
        total = jnp.sum(sums[...], axis=1)
        sums_out[...] = total[: 3 * slots]
        bias_out[...] = total[3 * slots :]
        heads = dot_rt(branch_back[...], weight[...])
        for k in range(rep_size):
            to, at = slice(k * group_tokens, (k + 1) * group_tokens), slice(k * block, (k + 1) * block)
            for g in range(rep_size):
                heads_out[to, g * block : (g + 1) * block] = heads[
                    g * group_tokens : (g + 1) * group_tokens, at
                ].astype(BF)

    middle_back, branch_back, middle_sums, output_bias_sum, sent_heads = call(
        order,
        middle_back_kernel,
        "second_norm_back",
        [],
        back_addends
        + [cotangent, place_columns, modulation, normed_two, inverse_two]
        + [branch, (qkv_block, (width, width))],
        [
            ((count, width), F32),
            ((count, width), BF),
            ((3 * slots, width), F32),
            ((1, width), F32),
            ((count, width), BF),
        ],
        150.0,
        scratch=[((3 * slots + 1, 8, width), F32)],
        limit=28,
        near=range(1, rep_size),
    )
    heads_back = exchange(sent_heads, "rep")

    def feed_out_kernel(three, down, *outs):
        for j in range(rep_size):
            rows_here = slice(j * count, (j + 1) * count)
            outs[j][...] = dot(three[rows_here, :], down[...]).astype(outs[j].dtype)

    feed_parts = call(
        order,
        feed_out_kernel,
        "feed_out",
        [],
        [hidden_three, down_block],
        part_shapes(rep_size, count, width),
        5.0,
        limit=24,
    )
    feed_addends = send(list(feed_parts), "rep", rep_size)

    def attention_back_kernel(r_ref, *refs):
        heads, query_ref, key_ref, value_ref, wide, tables_ref = refs[:6]
        column_ref, row_ref, projected_back, bias_out = refs[6:10]
        parts_out, head_stack = refs[10:-1], refs[-1]
        if padded > block:
            head_stack[:, :, block:] = jnp.zeros((rep_size, count, padded - block), BF)
        for j in range(rep_size):
            owner = pl.ds(pl.multiple_of((r_ref[0] ^ j) * group_tokens, 16), group_tokens)
            for g in range(rep_size):
                head_stack[j, g * group_tokens : (g + 1) * group_tokens, :block] = heads[
                    owner, g * block : (g + 1) * block
                ]
        bias_out[...] = jnp.zeros_like(bias_out)

        def row(j, carry):
            here = pl.ds(pl.multiple_of(j * count, count), count)
            query, key, value, back = query_ref[j], key_ref[j], value_ref[j], head_stack[j]
            same = column_ref[j, :, 0:1] == row_ref[j, 0:1, :]
            query_back = jnp.zeros((count, padded), F32)
            key_back = jnp.zeros((count, padded), F32)
            value_back = jnp.zeros((count, padded), F32)
            for h in range(local_heads):
                mask = head_mask(h)
                query_head, back_head = query * mask, back * mask
                probs = probabilities(query_head, key, same)
                probs_back = dot_rt(back_head, value)
                scores_back = (
                    probs
                    * (probs_back - jnp.sum(probs * probs_back, axis=-1, keepdims=True))
                ).astype(BF)
                value_back = value_back + dot_lt(probs.astype(BF), back_head)
                query_back = query_back + dot(scores_back, key * mask)
                key_back = key_back + dot_lt(scores_back, query_head)
            cos_row, sin_row = rotary(tables_ref, column_ref[j])
            query_back = turn(query_back * score_scale, cos_row, sin_row, -1.0)
            key_back = turn(key_back * score_scale, cos_row, sin_row, -1.0)
            low = [value.astype(BF) for value in (query_back, key_back, value_back)]
            for t in range(3):
                projected_back[here, t * block : (t + 1) * block] = low[t][:, :block]
                bias_out[:, t * padded : (t + 1) * padded] += jnp.sum(
                    low[t].astype(F32), axis=0, keepdims=True
                )
            store_part(j, dot_rt(jnp.concatenate(low, axis=1), wide[...]), parts_out)
            return carry

        lax.fori_loop(0, rep_size, row, 0)

    projected_back, projection_bias_sum, *one_parts = call(
        order,
        attention_back_kernel,
        "attention_back",
        [r_index],
        [heads_back, query_all, key_all, value_all, wide_weight, tables]
        + [place_columns, place_rows],
        [((flat, 3 * block), BF), ((1, 3 * padded), F32)] + part_shapes(rep_size, count, width),
        90.0,
        scratch=[((rep_size, count, padded), BF)],
        limit=44,
    )
    one_addends = send(one_parts, "rep", rep_size)

    def attention_gradient_kernel(attended_ref, own_back, hidden_all, back, out):
        step_width = width // 3
        for m in range(3):
            at = slice(m * step_width, (m + 1) * step_width)
            out[at, :width] = dot_lt(attended_ref[:, at], own_back[...]).astype(BF)
            out[at, width:] = dot_lt(hidden_all[:, at], back[...]).astype(BF)

    (attention_gradient,) = call(
        order,
        attention_gradient_kernel,
        "attention_gradient",
        [],
        [wait_for(attended, feed_addends), branch_back, hidden_one_all, projected_back],
        [((width, width + 3 * block), BF)],
        6.4,
        limit=32,
    )
    attention_sum = sent_gradient(attention_gradient)

    def output_kernel(*refs):
        feeds = refs[:rep_size]
        tokens_ref, branch_ref, cotangent_ref, places, modulation = refs[rep_size : rep_size + 5]
        block_out, sums_out, sums = refs[rep_size + 5 :]
        sums[...] = jnp.zeros_like(sums)

        def step(here):
            slot_of = places[0, here, 0:1]
            feed = feeds[0][here, :]
            for ref in feeds[1:]:
                feed = feed + ref[here, :].astype(F32)
            gate_one = pick(modulation, slot_of, 2 * width, width)
            middle = tokens_ref[here, :].astype(F32) + gate_one * branch_ref[here, :]
            gate_two = pick(modulation, slot_of, 5 * width, width)
            block_out[here, :] = (middle + gate_two * feed).astype(BF)
            masked = cotangent_ref[here, :].astype(F32) * places[0, here, 3:4]
            add_slots(sums, 0, slots, slot_of, masked * feed)

        chunks(count, step, 1)
        sums_out[...] = jnp.sum(sums[...], axis=1)

    block_output, gate_two_sums = call(
        order,
        output_kernel,
        "layer_output",
        [],
        feed_addends + [tokens, branch, cotangent, place_columns, modulation],
        [((count, width), BF), ((slots, width), F32)],
        30.0,
        scratch=[((slots, 8, width), F32)],
        limit=16,
        near=range(1, rep_size),
    )

    def first_back_kernel(r_ref, *refs):
        addends = refs[:rep_size]
        tokens_ref, back_ref, modulation, places, middle_ref, gate_two_ref, bias, out_bias = refs[
            rep_size : rep_size + 8
        ]
        gradient, back_blocks, sums, whole, whole_bias, stack = refs[rep_size + 8 :]
        sums[...] = jnp.zeros_like(sums)

        def step(here):
            slot_of = places[0, here, 0:1]
            upstream = addends[0][here, :]
            for ref in addends[1:]:
                upstream = upstream + ref[here, :].astype(F32)
            normed, inverse = normalize_keep(tokens_ref[here, :].astype(F32))
            scale = pick(modulation, slot_of, width, width)
            gradient[here, :] = back_ref[here, :] + normalize_back(
                normed, inverse, upstream * (1.0 + scale)
            )
            add_slots(sums, 0, slots, slot_of, upstream)
            add_slots(sums, slots, slots, slot_of, upstream * normed)

        chunks(count, step)
        total = jnp.sum(sums[...], axis=1)
        whole[:, :width] = total[:slots]
        whole[:, width : 2 * width] = total[slots:]
        for t in range(3):
            at = slice((2 + t) * width, (3 + t) * width)
            whole[:, at] = middle_ref[t * slots : (t + 1) * slots, :]
        whole[:, 5 * width :] = gate_two_ref[...]
        whole_bias[...] = jnp.zeros_like(whole_bias)
        for k in range(rep_size):

            @pl.when(r_ref[0] == k)
            def _():
                for t in range(3):
                    first = t * width + k * block
                    whole_bias[:, first : first + block] = bias[:, t * padded : t * padded + block]

        stack[...] = jnp.zeros_like(stack)
        for k in range(fsdp_size):
            stack[k, :slots, :] = whole[:, k * columns : (k + 1) * columns]
            at = slice(k * shard_bias, (k + 1) * shard_bias)
            stack[k, slots : slots + 1, :shard_bias] = whole_bias[:, at]
            at = slice(k * shard_out_bias, (k + 1) * shard_out_bias)
            lanes = slice(shard_bias, shard_bias + shard_out_bias)
            stack[k, slots : slots + 1, lanes] = out_bias[:, at]
        back_blocks[...] = stack[...].reshape(fsdp_size * GROUP, columns).astype(BF)

    tokens_gradient, back_blocks = call(
        order,
        first_back_kernel,
        "first_norm_back",
        [r_index],
        one_addends
        + [tokens, middle_back, modulation, place_columns, middle_sums, gate_two_sums]
        + [projection_bias_sum, output_bias_sum],
        [((count, width), F32), ((fsdp_size * GROUP, columns), BF)],
        30.0,
        scratch=[
            ((2 * slots, 8, width), F32),
            ((slots, 6 * width), F32),
            ((1, 3 * width), F32),
            ((fsdp_size, GROUP, columns), F32),
        ],
        limit=20,
        near=range(1, rep_size),
    )

    line_backs = exchange(back_blocks, "fsdp")
    feed_sums = gather(wait_for(feed_sum, one_addends), "rep", rep_size)

    def conditioning_kernel(groups, activated_ref, weight, out, line_out):
        stack = groups[...].astype(F32)
        bias = jnp.sum(stack.reshape(fsdp_size, GROUP, columns), axis=0)[slots : slots + 1]
        row_ids = lax.broadcasted_iota(jnp.int32, (fsdp_size * GROUP, 1), 0)
        rows_back = jnp.where(lax.rem(row_ids, GROUP) < slots, stack, 0.0)
        line_out[:, :width] = activated_ref[...]
        line_out[:, width:] = jnp.where(row_ids == slots, bias, rows_back).astype(BF)
        result = dot(rows_back.astype(BF), weight[...])
        for k in range(fsdp_size):
            out[k * slots : (k + 1) * slots, :] = result[k * GROUP : k * GROUP + slots, :]

    activated_backs, line_back = call(
        order,
        conditioning_kernel,
        "conditioning_back",
        [],
        [wait_for(line_backs, feed_sums[1:3]), line_activated, modulation_weight.T],
        [((fsdp_size * slots, width), F32), ((fsdp_size * GROUP, width + columns), BF)],
        40.0,
        limit=24,
    )
    activated_backs = exchange(activated_backs, "fsdp")
    all_lines = gather(line_back, "rep", rep_size)

    def feed_blocks_kernel(r_ref, *refs):
        gate_out, up_out, down_out, stack = refs[rep_size:]
        for j in range(rep_size):
            stack[j] = refs[j][...].astype(F32)
        for k in range(rep_size):
            here = r_ref[0] ^ k
            for j in range(fsdp_size):
                target = slice(j * shard_ff + k * piece, j * shard_ff + (k + 1) * piece)
                first = block_ff + j * piece
                gate_out[:, target] = stack[here, :, j * piece : (j + 1) * piece]
                up_out[:, target] = stack[here, :, first : first + piece]
            for a, lanes, c, packed_lanes in units:
                to_row = k * piece + a
                down_out[to_row : to_row + unit_rows, lanes] = stack[
                    here, c : c + unit_rows, packed_lanes
                ]

    gate_gradient, up_gradient, down_gradient = call(
        order,
        feed_blocks_kernel,
        "feed_blocks",
        [r_index],
        feed_sums,
        [((shard_width, fsdp_size * shard_ff), F32)] * 2 + [((shard_ff, width), F32)],
        5.2,
        scratch=[((rep_size, shard_width, 3 * block_ff), F32)],
        limit=24,
        near=range(1, rep_size),
    )

    def table_kernel(*refs):
        lines, (condition, activated_back) = refs[:rep_size], refs[rep_size : rep_size + 2]
        table, table_bias, bias, out_bias, gradient, activated_stack, back_stack = refs[
            rep_size + 2 :
        ]
        upstream = jnp.sum(activated_back[...].reshape(fsdp_size, slots, width), axis=0)
        gradient[...] = upstream * silu_slope(condition[...].astype(F32))
        line = fsdp_size * GROUP
        total = jnp.zeros((1, columns), F32)
        for j in range(rep_size):
            back = lines[j][:, width:]
            activated_stack[j * line : (j + 1) * line, :] = lines[j][:, :width]
            back_stack[j * line : (j + 1) * line, :] = back
            total = total + back.astype(F32)[slots : slots + 1, :]
        bias[...] = total[:, :shard_bias]
        out_bias[...] = total[:, shard_bias : shard_bias + shard_out_bias]
        back = back_stack[...].astype(F32)
        in_group = lax.rem(lax.broadcasted_iota(jnp.int32, (rep_size * line, 1), 0), GROUP)
        table_bias[...] = jnp.sum(
            jnp.where(in_group < slots, back, 0.0), axis=0, keepdims=True
        )
        table[...] = dot_lt(back_stack[...], activated_stack[...])

    table_gradient, table_bias_gradient, bias_gradient, out_bias_gradient, activated_gradient = call(
        order,
        table_kernel,
        "table_gradient",
        [],
        all_lines + [conditioning[0], activated_backs],
        [((columns, width), F32), ((1, columns), F32)]
        + [((1, shard_bias), F32), ((1, shard_out_bias), F32), ((slots, width), F32)],
        4.0,
        scratch=[
            ((rep_size * fsdp_size * GROUP, width), BF),
            ((rep_size * fsdp_size * GROUP, columns), BF),
        ],
        limit=24,
        near=range(1, rep_size),
    )

    attention_late = wait_for(attention_sum, table_gradient)
    output_gradient = attention_late[:, :width].astype(F32)
    projection_sums = gather(attention_late[:, width:], "rep", rep_size)
    for bit in [1 << k for k in range(rep_size.bit_length() - 1)]:
        came = swap_with(output_gradient.astype(BF), "rep", rep_size, bit)
        came = wait_for(came, projection_sums[2 % rep_size]) if bit == 1 else came
        output_gradient = output_gradient + came.astype(F32)

    def projection_blocks_kernel(r_ref, *refs):
        out, stack = refs[rep_size:]
        for j in range(rep_size):
            stack[j] = refs[j][...].astype(F32)
        for k in range(rep_size):
            here = r_ref[0] ^ k
            for t in range(3):
                first = t * width + k * block
                out[:, first : first + block] = stack[here, :, t * block : (t + 1) * block]

    (projection_gradient,) = call(
        order,
        projection_blocks_kernel,
        "projection_blocks",
        [r_index],
        projection_sums,
        [((shard_width, 3 * width), F32)],
        3.0,
        scratch=[((rep_size, shard_width, 3 * block), F32)],
        limit=24,
        near=range(1, rep_size),
    )
    return (
        block_output[None],
        tokens_gradient[None],
        activated_gradient[None],
        table_gradient.T,
        table_bias_gradient[0],
        projection_gradient,
        bias_gradient[0],
        output_gradient,
        out_bias_gradient[0],
        gate_gradient,
        up_gradient,
        down_gradient,
    )


def solution(mesh):
    sizes = dict(mesh.shape)

    def body(*arrays):
        return on_device(sizes["rep"], sizes["fsdp"], *arrays)

    rows = ("rep", "fsdp")
    in_specs = (
        P(rows, None, None),
        P(rows, None, None),
        P(rows, None),
        P(rows, None),
        P(rows, None),
        P(rows, None),
        P(None, "fsdp"),
        P("fsdp"),
        P("fsdp", None),
        P("fsdp"),
        P("fsdp", None),
        P("fsdp"),
        P("fsdp", None),
        P("fsdp", None),
        P("fsdp", None),
        P(rows, None, None),
    )
    out_specs = (
        P(rows, None, None),
        P(rows, None, None),
        P(rows, None, None),
        P(None, "fsdp"),
        P("fsdp"),
        P("fsdp", None),
        P("fsdp"),
        P("fsdp", None),
        P("fsdp"),
        P("fsdp", None),
        P("fsdp", None),
        P("fsdp", None),
    )
    return jax.shard_map(
        body, mesh=mesh, in_specs=in_specs, out_specs=out_specs, check_vma=False
    )
```

```python
import math

import jax
import jax.numpy as jnp
import numpy as np
from jax import lax
from jax.experimental import pallas as pl
from jax.experimental.pallas import tpu as pltpu
from jax.sharding import PartitionSpec as P

HEADS = 16
BF = jnp.bfloat16
F32 = jnp.float32
LANES = 128
CHUNK = 32
GROUP = 8


def wait_for(value, *others):
    return lax.optimization_barrier((value, others))[0]


def swap_with(value, axis, size, bit):
    return lax.ppermute(value, axis, [(i, i ^ bit) for i in range(size)])


def gather(value, axis, size):
    return [value] + [swap_with(value, axis, size, j) for j in range(1, size)]


def halves_gather(top, low, axis, size):
    if size != 4:
        return list(zip(gather(top, axis, size), gather(low, axis, size), strict=True))
    top_one, low_two = swap_with(top, axis, size, 1), swap_with(low, axis, size, 2)
    top_three, low_three = swap_with(top_one, axis, size, 2), swap_with(low_two, axis, size, 1)
    low_one, top_two = swap_with(low, axis, size, 1), swap_with(top, axis, size, 2)
    return [(top, low), (top_one, low_one), (top_two, low_two), (top_three, low_three)]


def send(values, axis, size):
    return [values[0]] + [swap_with(values[j], axis, size, j) for j in range(1, size)]


def exchange(value, axis):
    return lax.all_to_all(value, axis, 0, 0, tiled=True)


def block_of(shape, by_step, offset=0):
    if by_step:
        return pl.BlockSpec(shape, lambda i: (i + offset,) + (0,) * (len(shape) - 1))
    zeros = (0,) * len(shape)
    return pl.BlockSpec(shape, lambda i: zeros, pipeline_mode=pl.Buffered(1))


def call(order, body, name, scalars, arrays, outs, micros, scratch=(), limit=48, near=(), steps=1):
    shapes = [pltpu.HBM(out[0], out[1]) for out in outs]
    out_specs = [block_of(out[-1], True) if len(out) > 2 else block_of(out[0], False) for out in outs]
    in_specs = [
        block_of(array[1], len(array) > 2, *array[3:])
        if isinstance(array, tuple)
        else block_of(array.shape, False)
        for array in arrays
    ]
    arrays = [array[0] if isinstance(array, tuple) else array for array in arrays]
    if order:
        first, _ = lax.optimization_barrier((arrays[0], order.pop()))
        arrays = [first] + list(arrays[1:])
    arrays = [
        array if n in near else pltpu.with_memory_space_constraint(array, pltpu.HBM)
        for n, array in enumerate(arrays)
    ]
    results = pl.pallas_call(
        body,
        name=name,
        grid=(steps,),
        out_shape=shapes,
        in_specs=[pl.BlockSpec(memory_space=pltpu.SMEM)] * len(scalars)
        + in_specs,
        out_specs=out_specs,
        scratch_shapes=[pltpu.VMEM(shape, dtype) for shape, dtype in scratch],
        compiler_params=pltpu.CompilerParams(vmem_limit_bytes=limit << 20),
        cost_estimate=pl.CostEstimate(
            flops=int(micros * 1.000e+09), bytes_accessed=int(micros * 3.000e+06), transcendentals=0
        ),
    )(*scalars, *arrays)
    order.append(results[0])
    return results


def part_shapes(size, tokens, width):
    return [((tokens, width), F32)] + [((tokens, width), BF)] * (size - 1)


def store_part(j, value, refs):
    for k, ref in enumerate(refs):

        @pl.when(j == k)
        def _(ref=ref):
            ref[...] = value.astype(ref.dtype)


def dot(left, right):
    return jnp.dot(left, right, preferred_element_type=F32)


def dot_rt(left, right):
    return lax.dot_general(left, right, (((1,), (1,)), ((), ())), preferred_element_type=F32)


def dot_lt(left, right):
    return lax.dot_general(left, right, (((0,), (0,)), ((), ())), preferred_element_type=F32)


def pick(modulation, slot_of, first, width):
    total = jnp.zeros((slot_of.shape[0], width), F32)
    for k in range(modulation.shape[0]):
        total = jnp.where(slot_of == k, modulation[k : k + 1, first : first + width], total)
    return total


def normalize_keep(values):
    centered = values - jnp.mean(values, axis=-1, keepdims=True)
    variance = jnp.mean(centered * centered, axis=-1, keepdims=True)
    inverse = lax.rsqrt(variance + 1e-06)
    return centered * inverse, inverse


def normalize_back(normed, inverse, upstream):
    return inverse * (
        upstream
        - jnp.mean(upstream, axis=-1, keepdims=True)
        - normed * jnp.mean(upstream * normed, axis=-1, keepdims=True)
    )


def add_slots(sums, base, count, slot_of, values):
    rows, width = values.shape
    for k in range(count):
        chosen = jnp.where(slot_of == k, values, 0.0)
        sums[base + k] += jnp.sum(chosen.reshape(rows // 8, 8, width), axis=0)


def chunks(tokens, step, unroll=2):
    def body(i, carry):
        step(pl.ds(pl.multiple_of(i * CHUNK, CHUNK), CHUNK))
        return carry

    lax.fori_loop(0, tokens // CHUNK, body, 0, unroll=unroll)


def silu_slope(values):
    sigmoid = jax.nn.sigmoid(values)
    return sigmoid * (1.0 + values * (1.0 - sigmoid))


def on_device(
    rep_size,
    fsdp_size,
    tokens,
    conditioning,
    segment_ids,
    heights,
    widths,
    pad_mask,
    modulation_weight,
    modulation_bias,
    projection_weight,
    projection_bias,
    output_weight,
    output_bias,
    gate_weight,
    up_weight,
    down_weight,
    cotangent,
):
    rows, count, width = tokens.shape
    assert rows == 1
    slots = conditioning.shape[1]
    head_width = width // HEADS
    local_heads = HEADS // rep_size
    block = width // rep_size
    padded = -(-block // LANES) * LANES
    score_scale = 1.0 / math.sqrt(head_width)
    shard_ff = down_weight.shape[0]
    piece = shard_ff // rep_size
    block_ff = fsdp_size * piece
    shard_width = projection_weight.shape[0]
    columns = modulation_weight.shape[1]
    flat = rep_size * count
    half = count // 2
    group_tokens = count // rep_size
    others = rep_size - 1
    r = lax.axis_index("rep")
    r_index = r.reshape(1).astype(jnp.int32)
    tokens, cotangent = tokens[0], cotangent[0]
    order = []

    def qkv_shard_kernel(r_ref, projection, output, out):
        out[:, :width] = output[...]
        for k in range(rep_size):

            @pl.when(r_ref[0] == k)
            def _():
                for t in range(3):
                    first, to = t * width + k * block, width + t * block
                    out[:, to : to + block] = projection[:, first : first + block]

    (qkv_shard,) = call(
        order,
        qkv_shard_kernel,
        "qkv_shard",
        [r_index],
        [projection_weight, output_weight],
        [((shard_width, width + 3 * block), BF)],
        4.5,
        limit=16,
    )

    slot_ids = jnp.arange(slots, dtype=jnp.int32)
    member_ints = (segment_ids[:, :, None] == slot_ids).astype(jnp.int32)
    before_ints = (slot_ids < segment_ids[:, :, None]).astype(jnp.int32)
    starts = jnp.sum(before_ints * (heights * widths)[:, None, :], axis=2)
    offsets = jnp.arange(count, dtype=jnp.int32)[None, :] - starts
    row_width = jnp.sum(member_ints * widths[:, None, :], axis=2)
    places = jnp.concatenate(
        [segment_ids, offsets // row_width, offsets % row_width, pad_mask], axis=1
    ).astype(BF)
    places = jnp.pad(places, ((0, GROUP - 1), (0, width - 4 * count)))
    token_rows = gather(jnp.concatenate([tokens, places], axis=0), "rep", rep_size)

    cond_float = conditioning.astype(F32)
    activated = jax.nn.silu(cond_float).astype(BF).reshape(slots, width)
    shard_bias, shard_out_bias = projection_bias.shape[0], output_bias.shape[0]
    bias_row = jnp.pad(
        jnp.concatenate([projection_bias, output_bias]), (0, width - shard_bias - shard_out_bias)
    )[None]
    group_rows = jnp.concatenate(
        [activated, bias_row, jnp.zeros((GROUP - slots - 1, width), BF)], axis=0
    )
    line_rows = lax.all_gather(group_rows, "fsdp", axis=0, tiled=True)

    def modulate_kernel(r_ref, *refs):
        groups, weight, bias = refs[:3]
        out, activated_out, bias_out, out_bias, stack, whole = refs[3:]
        stack[...] = groups[...].astype(F32).reshape(fsdp_size, GROUP, width)
        in_group = lax.rem(lax.broadcasted_iota(jnp.int32, (fsdp_size * GROUP, 1), 0), GROUP)
        rows_low = jnp.where(in_group < slots, groups[...].astype(F32), 0.0).astype(BF)
        activated_out[...] = rows_low
        out[...] = dot_rt(rows_low, weight[...]) + bias[...]
        for k in range(fsdp_size):
            row = stack[k, slots : slots + 1, :]
            whole[:, k * shard_bias : (k + 1) * shard_bias] = row[:, :shard_bias]
            at = slice(k * shard_out_bias, (k + 1) * shard_out_bias)
            out_bias[:, at] = row[:, shard_bias : shard_bias + shard_out_bias]
        bias_out[...] = jnp.zeros_like(bias_out)
        for k in range(rep_size):

            @pl.when(r_ref[0] == k)
            def _():
                for t in range(3):
                    first = t * width + k * block
                    bias_out[:, t * padded : t * padded + block] = whole[:, first : first + block]

    line_modulation, line_activated, own_bias, output_bias_all = call(
        order,
        modulate_kernel,
        "modulate",
        [r_index],
        [line_rows, modulation_weight.T, modulation_bias.astype(F32)[None]],
        [
            ((fsdp_size * GROUP, columns), F32),
            ((fsdp_size * GROUP, width), BF),
            ((1, 3 * padded), F32),
            ((1, width), F32),
        ],
        6.0,
        scratch=[((fsdp_size, GROUP, width), F32), ((1, 3 * width), F32)],
        limit=24,
    )
    own_modulation = lax.all_to_all(line_modulation, "fsdp", 0, 0, tiled=True)

    unit_rows, unit_lanes = math.gcd(piece, shard_width), math.gcd(width, block_ff)
    units = []
    for u in range((piece // unit_rows) * (width // unit_lanes)):
        (a, b), (c, d) = divmod(u, width // unit_lanes), divmod(u, block_ff // unit_lanes)
        units.append(
            (
                a * unit_rows,
                slice(b * unit_lanes, (b + 1) * unit_lanes),
                c * unit_rows,
                slice(2 * block_ff + d * unit_lanes, 2 * block_ff + (d + 1) * unit_lanes),
            )
        )

    def feed_shard_kernel(r_ref, gate, up, down, out):
        for k in range(rep_size):

            @pl.when(r_ref[0] == k)
            def _():
                for j in range(fsdp_size):
                    source = slice(j * shard_ff + k * piece, j * shard_ff + (k + 1) * piece)
                    out[:, j * piece : (j + 1) * piece] = gate[:, source]
                    first = block_ff + j * piece
                    out[:, first : first + piece] = up[:, source]
                for a, lanes, c, packed_lanes in units:
                    out[c : c + unit_rows, packed_lanes] = down[
                        k * piece + a : k * piece + a + unit_rows, lanes
                    ]

    (feed_shard,) = call(
        order,
        feed_shard_kernel,
        "feed_shard",
        [r_index],
        [gate_weight, up_weight, down_weight],
        [((shard_width, 3 * block_ff), BF)],
        4.5,
        limit=16,
    )
    qkv_block = lax.all_gather(qkv_shard, "fsdp", axis=0, tiled=True)
    feed_block = lax.all_gather(feed_shard, "fsdp", axis=0, tiled=True)

    def norm_rows_kernel(*refs):
        out, columns_out, rows_out = refs[rep_size:]
        for j in range(rep_size):
            ref = refs[j]

            def step(at, ref=ref, j=j):
                normed, _ = normalize_keep(ref[at, :].astype(F32))
                out[pl.ds(j * count + at.start, CHUNK), :] = normed

            chunks(count, step)
            line = ref[count:, :].astype(F32)
            for q in range(4):
                rows_out[j, q : q + 1, :] = line[:1, q * count : (q + 1) * count]
            rows_out[j, 4:, :] = jnp.zeros((4, count), F32)
            columns_out[j] = rows_out[j].T

    normed_rows, place_columns, place_rows = call(
        order,
        norm_rows_kernel,
        "first_norm",
        [],
        token_rows,
        [((flat, width), F32), ((rep_size, count, 8), F32), ((rep_size, 8, count), F32)],
        18.0,
        limit=24,
        near=range(1, rep_size),
    )
    pair_count = head_width // 4
    most_rows, most_columns = count // 4, 32
    lane = np.arange(padded)
    in_head = lane % head_width
    lane_frequency = 10000.0 ** (-(in_head % pair_count) / pair_count)
    of_row = (lane < block) & (in_head < 2 * pair_count)
    of_column = (lane < block) & (in_head >= 2 * pair_count)
    sign = np.where((in_head // pair_count) % 2 == 1, 1.0, -1.0)
    row_angle = np.arange(most_rows)[:, None] * lane_frequency
    column_angle = np.arange(most_columns)[:, None] * lane_frequency
    tables = np.concatenate(
        [
            np.concatenate(
                [
                    np.where(of_row, np.cos(row_angle), 0.0),
                    np.where(of_column, np.cos(column_angle), 0.0),
                ]
            ),
            np.concatenate(
                [
                    np.where(of_row, sign * np.sin(row_angle), 0.0),
                    np.where(of_column, sign * np.sin(column_angle), 0.0),
                ]
            ),
        ],
        axis=1,
    ).astype(np.float32)
    pieces, left = [], tables
    for _ in range(3):
        pieces.append(left.astype(jnp.bfloat16))
        left = left - pieces[-1].astype(np.float32)
    tables = jnp.asarray(np.stack(pieces))

    def rotary(tables_ref, places):
        numbers = lax.broadcasted_iota(jnp.int32, (count, most_rows + most_columns), 1).astype(F32)
        is_row = (numbers < most_rows) & (numbers == places[:, 1:2])
        is_column = (numbers >= most_rows) & (numbers - most_rows == places[:, 2:3])
        chosen = jnp.where(is_row | is_column, 1.0, 0.0).astype(BF)
        both = dot(chosen, tables_ref[2]) + dot(chosen, tables_ref[1]) + dot(chosen, tables_ref[0])
        return both[:, :padded], both[:, padded:]

    def modulation_kernel(arrived, modulation, sent):
        for k in range(fsdp_size):
            at = slice(k * columns, (k + 1) * columns)
            modulation[:, at] = arrived[k * GROUP : k * GROUP + slots, :]
        sent[:, : 2 * width] = modulation[:, : 2 * width]
        sent[:, 2 * width :] = modulation[:, 5 * width :]

    modulation, sent_modulation = call(
        order,
        modulation_kernel,
        "modulation",
        [],
        [wait_for(own_modulation, normed_rows)],
        [((slots, 6 * width), F32), ((slots, 3 * width), F32)],
        3.0,
        limit=8,
    )
    modulation_rows = gather(sent_modulation, "rep", rep_size)
    cotangent_rows = gather(wait_for(cotangent, modulation_rows), "rep", rep_size)

    def head_mask(h):
        lanes = lax.broadcasted_iota(jnp.int32, (1, padded), 1)
        inside = (lanes >= h * head_width) & (lanes < (h + 1) * head_width)
        return jnp.where(inside, 1.0, 0.0).astype(BF)

    def probabilities(query_head, key, same):
        scores = jnp.where(same, dot_rt(query_head, key) * score_scale, -1e30)
        exponent = jnp.exp(scores - jnp.max(scores, axis=-1, keepdims=True))
        return exponent / jnp.sum(exponent, axis=-1, keepdims=True)

    def turn(values, cosine_row, sine_row, sense):
        before = pltpu.roll(values, pair_count, 1)
        after = pltpu.roll(values, padded - pair_count, 1)
        lanes = lax.broadcasted_iota(jnp.int32, (1, padded), 1)
        second = lax.rem(lanes, 2 * pair_count) >= pair_count
        return values * cosine_row + jnp.where(second, before, after) * (sense * sine_row)

    def attention_kernel(r_ref, *refs):
        modulations = refs[:rep_size]
        normed, weight, bias, tables_ref, column_ref, row_ref = refs[rep_size : rep_size + 6]
        hidden_all, wide, query_out, key_out, value_out, attended_out, modulation_stack = refs[
            rep_size + 6 :
        ]
        for j in range(rep_size):
            modulation_stack[j] = modulations[j][:, : 2 * width]
        for t in range(3):
            first = width + t * block
            wide[:, t * padded : t * padded + block] = weight[:, first : first + block]
            if padded > block:
                wide[:, t * padded + block : (t + 1) * padded] = jnp.zeros(
                    (width, padded - block), BF
                )

        def row(j, carry):
            first = pl.multiple_of(j * count, count)

            def step(at):
                here = pl.ds(pl.multiple_of(first + at.start, CHUNK), CHUNK)
                slot_of = column_ref[j, at, 0:1]
                scale = pick(modulation_stack[j], slot_of, width, width)
                shift = pick(modulation_stack[j], slot_of, 0, width)
                hidden_all[here, :] = (normed[here, :] * (1.0 + scale) + shift).astype(BF)

            chunks(count, step)
            projected = dot(hidden_all[pl.ds(first, count), :], wide[...]) + bias[...]
            cos_row, sin_row = rotary(tables_ref, column_ref[j])
            query = turn(projected[:, :padded], cos_row, sin_row, 1.0).astype(BF)
            key = turn(projected[:, padded : 2 * padded], cos_row, sin_row, 1.0).astype(BF)
            value = projected[:, 2 * padded :].astype(BF)
            query_out[j], key_out[j], value_out[j] = query, key, value
            same = column_ref[j, :, 0:1] == row_ref[j, 0:1, :]
            total = jnp.zeros((count, padded), F32)
            for h in range(local_heads):
                mask = head_mask(h)
                probs = probabilities(query * mask, key, same)
                total = total + dot(probs.astype(BF), value * mask)
            owner = pl.ds(pl.multiple_of((r_ref[0] ^ j) * group_tokens, 16), group_tokens)
            low = total[:, :block].astype(BF)
            for g in range(rep_size):
                attended_out[owner, g * block : (g + 1) * block] = low[
                    g * group_tokens : (g + 1) * group_tokens, :
                ]
            return carry

        lax.fori_loop(0, rep_size, row, 0)

    hidden_one_all, wide_weight, query_all, key_all, value_all, attended_heads = call(
        order,
        attention_kernel,
        "attention",
        [r_index],
        modulation_rows
        + [normed_rows, qkv_block, own_bias, tables, place_columns, place_rows],
        [((flat, width), BF), ((width, 3 * padded), BF)]
        + [((rep_size, count, padded), BF)] * 3
        + [((count, width), BF)],
        66.0,
        scratch=[((rep_size, slots, 2 * width), F32)],
        limit=44,
        near=range(1, rep_size),
    )
    own_heads = exchange(attended_heads, "rep")

    def feed_back_kernel(*refs):
        cotangents, modulations = refs[:rep_size], refs[rep_size : 2 * rep_size]
        columns_ref, out = refs[2 * rep_size :]
        for j in range(rep_size):

            def step(at, j=j):
                masked = cotangents[j][at, :].astype(F32) * columns_ref[j, at, 3:4]
                gate = pick(modulations[j], columns_ref[j, at, 0:1], 2 * width, width)
                out[pl.ds(j * count + at.start, CHUNK), :] = (gate * masked).astype(BF)

            chunks(count, step)

    (feed_back_all,) = call(
        order,
        feed_back_kernel,
        "feed_back",
        [],
        cotangent_rows + modulation_rows + [place_columns],
        [((flat, width), BF)],
        12.0,
        limit=24,
        near=(*range(1, rep_size), *range(rep_size + 1, 2 * rep_size)),
    )

    def middle_kernel(
        heads, weight, bias, tokens_ref, modulation, places, branch, normed_out, inverse_out,
        top, low, attended,
    ):
        for k in range(rep_size):
            for g in range(rep_size):
                attended[
                    g * group_tokens : (g + 1) * group_tokens, k * block : (k + 1) * block
                ] = heads[k * group_tokens : (k + 1) * group_tokens, g * block : (g + 1) * block]
        branch[...] = dot(attended[...], weight[...]) + bias[...]

        for p, hidden in enumerate((top, low)):

            def step(at, p=p, hidden=hidden):
                here = pl.ds(p * half + at.start, CHUNK)
                slot_of = places[0, here, 0:1]
                gate = pick(modulation, slot_of, 2 * width, width)
                middle = tokens_ref[here, :].astype(F32) + gate * branch[here, :]
                normed, inverse = normalize_keep(middle)
                normed_out[here, :] = normed
                inverse_out[here, :] = inverse
                scale = pick(modulation, slot_of, 4 * width, width)
                hidden[at, :] = (
                    normed * (1.0 + scale) + pick(modulation, slot_of, 3 * width, width)
                ).astype(BF)

            chunks(half, step)

    branch, normed_two, inverse_two, hidden_top, hidden_low, attended = call(
        order,
        middle_kernel,
        "second_norm",
        [],
        [own_heads, (qkv_block, (width, width)), output_bias_all, tokens, modulation, place_columns],
        [((count, width), F32), ((count, width), F32), ((count, 1), F32)]
        + [((half, width), BF)] * 2
        + [((count, width), BF)],
        21.0,
        limit=24,
    )
    hidden_two_rows = halves_gather(hidden_top, hidden_low, "rep", rep_size)
    hidden_two_rows = [piece for row in hidden_two_rows for piece in row]


    step_ff = 256 if block_ff % 256 == 0 else 128
    taken = count

    def feed_kernel(unpack, rows_here, *refs):
        back, weight = refs[2 * rows_here : 2 * rows_here + 2]
        refs_here = refs[2 * rows_here + 2 :]
        if unpack:
            hidden_out, three, both_back, down = refs_here[:4]
        else:
            down, hidden_out, three, both_back = refs_here[:4]
        parts_out, hidden_all = refs_here[4:-1], refs_here[-1]
        j = pl.program_id(0)

        @pl.when(j == 0)
        def _():
            for n in range(2 * rows_here):
                hidden_all[n * half : (n + 1) * half, :] = refs[n][...]
            if not unpack:
                return
            for k in range(fsdp_size):
                for a, lanes, c, packed_lanes in units:
                    from_row, to_row = k * shard_width + c, k * piece + a
                    down[to_row : to_row + unit_rows, lanes] = weight[
                        from_row : from_row + unit_rows, packed_lanes
                    ]

        hidden = hidden_all[pl.ds(pl.multiple_of(j * count, count), count), :]
        hidden_out[...] = hidden
        for c in range(block_ff // step_ff):
            at = slice(c * step_ff, (c + 1) * step_ff)
            up_at = slice(block_ff + c * step_ff, block_ff + (c + 1) * step_ff)
            gate = dot(hidden, weight[:, at])
            up = dot(hidden, weight[:, up_at])
            hidden_back = dot_rt(back[...], down[at, :])
            sigmoid = jax.nn.sigmoid(gate)
            silu = gate * sigmoid
            three[:, at] = (silu * up).astype(BF)
            slope = sigmoid * (1.0 + gate * (1.0 - sigmoid))
            both_back[:, at] = (hidden_back * up * slope).astype(BF)
            both_back[:, up_at] = (hidden_back * silu).astype(BF)
        store_part(j, dot_rt(both_back[...], weight[:, : 2 * block_ff]), parts_out)

    near_rows = rep_size - 1
    far_rows = rep_size - near_rows
    row_outs = [((width,), BF), ((block_ff,), BF), ((2 * block_ff,), BF)]

    def rows_out(row_count):
        return [((row_count * count,) + w, d, (count,) + w) for w, d in row_outs]

    far_hidden, far_three, far_both, down_block, *far_parts = call(
        order,
        lambda *refs: feed_kernel(True, far_rows, *refs),
        "feed_far",
        [],
        hidden_two_rows[2 * near_rows :]
        + [(feed_back_all, (count, width), True, near_rows), feed_block],
        rows_out(far_rows) + [((block_ff, width), BF)] + [((count, width), BF)] * far_rows,
        15.0,
        scratch=[((far_rows * count, width), BF)],
        limit=40,
        near=range(2 * far_rows),
        steps=far_rows,
    )
    near_hidden, near_three, near_both, *near_parts = call(
        order,
        lambda *refs: feed_kernel(False, near_rows, *refs),
        "feed_near",
        [],
        hidden_two_rows[: 2 * near_rows]
        + [(feed_back_all, (count, width), True, 0), feed_block, down_block],
        rows_out(near_rows) + part_shapes(near_rows, count, width),
        45.0,
        scratch=[((near_rows * count, width), BF)],
        limit=40,
        near=range(2, 2 * near_rows),
        steps=near_rows,
    )
    back_parts = near_parts + far_parts
    back_addends = send(back_parts, "rep", rep_size)

    def sent_gradient(value):
        return lax.psum_scatter(value, "fsdp", scatter_dimension=0, tiled=True)

    def feed_gradient_kernel(
        hidden, far_hidden, back_all, three, far_three, both, far_both, out
    ):
        step_width, split = width // 3, near_rows * count
        for m in range(3):
            at = slice(m * step_width, (m + 1) * step_width)
            gradient = dot_lt(hidden[:, at], both[...]) + dot_lt(far_hidden[:, at], far_both[...])
            out[at, : 2 * block_ff] = gradient.astype(BF)
        together = max(1, fsdp_size // 2)
        for first in range(0, fsdp_size, together):
            at = slice(first * piece, (first + together) * piece)
            gradient = dot_lt(three[:, at], back_all[:split, :]) + dot_lt(
                far_three[:, at], back_all[split:, :]
            )
            gradient = gradient.astype(BF)
            for j in range(together):
                for a, lanes, c, packed_lanes in units:
                    to_row = (first + j) * shard_width + c
                    out[to_row : to_row + unit_rows, packed_lanes] = gradient[
                        j * piece + a : j * piece + a + unit_rows, lanes
                    ]

    (feed_gradient,) = call(
        order,
        feed_gradient_kernel,
        "feed_gradient",
        [],
        [wait_for(near_hidden, back_addends[near_rows:])]
        + [far_hidden, feed_back_all, near_three, far_three, near_both, far_both],
        [((width, 3 * block_ff), BF)],
        12.0,
        limit=36,
    )
    feed_sum = sent_gradient(feed_gradient)

    def middle_back_kernel(*refs):
        addends = refs[:rep_size]
        cotangent_ref, places, modulation, normed_ref, inverse_ref, branch_ref, weight = refs[
            rep_size : rep_size + 7
        ]
        middle_back, branch_back, sums_out, bias_out, heads_out, sums = refs[
            rep_size + 7 :
        ]
        sums[...] = jnp.zeros_like(sums)

        def step(here):
            slot_of = places[0, here, 0:1]
            upstream = addends[0][here, :]
            for ref in addends[1:]:
                upstream = upstream + ref[here, :].astype(F32)
            normed = normed_ref[here, :]
            masked = cotangent_ref[here, :].astype(F32) * places[0, here, 3:4]
            scale = pick(modulation, slot_of, 4 * width, width)
            back = masked + normalize_back(normed, inverse_ref[here, :], upstream * (1.0 + scale))
            middle_back[here, :] = back
            gate = pick(modulation, slot_of, 2 * width, width)
            low = (back * gate).astype(BF)
            branch_back[here, :] = low
            add_slots(sums, 0, slots, slot_of, back * branch_ref[here, :])
            add_slots(sums, slots, slots, slot_of, upstream)
            add_slots(sums, 2 * slots, slots, slot_of, upstream * normed)
            sums[3 * slots] += jnp.sum(low.astype(F32).reshape(CHUNK // 8, 8, width), axis=0)

        chunks(count, step, 1)
        total = jnp.sum(sums[...], axis=1)
        sums_out[...] = total[: 3 * slots]
        bias_out[...] = total[3 * slots :]
        heads = dot_rt(branch_back[...], weight[...])
        for k in range(rep_size):
            to, at = slice(k * group_tokens, (k + 1) * group_tokens), slice(k * block, (k + 1) * block)
            for g in range(rep_size):
                heads_out[to, g * block : (g + 1) * block] = heads[
                    g * group_tokens : (g + 1) * group_tokens, at
                ].astype(BF)

    middle_back, branch_back, middle_sums, output_bias_sum, sent_heads = call(
        order,
        middle_back_kernel,
        "second_norm_back",
        [],
        back_addends
        + [cotangent, place_columns, modulation, normed_two, inverse_two]
        + [branch, (qkv_block, (width, width))],
        [
            ((count, width), F32),
            ((count, width), BF),
            ((3 * slots, width), F32),
            ((1, width), F32),
            ((count, width), BF),
        ],
        150.0,
        scratch=[((3 * slots + 1, 8, width), F32)],
        limit=28,
        near=range(1, rep_size),
    )
    heads_back = exchange(sent_heads, "rep")

    def feed_out_kernel(three, far_three, down, *outs):
        for j in range(rep_size):
            source, k = (three, j) if j < near_rows else (far_three, j - near_rows)
            rows_here = slice(k * count, (k + 1) * count)
            outs[j][...] = dot(source[rows_here, :], down[...]).astype(outs[j].dtype)

    feed_parts = call(
        order,
        feed_out_kernel,
        "feed_out",
        [],
        [near_three, far_three, down_block],
        part_shapes(rep_size, count, width),
        5.0,
        limit=24,
    )
    feed_addends = send(list(feed_parts), "rep", rep_size)

    def attention_back_kernel(r_ref, *refs):
        heads, query_ref, key_ref, value_ref, wide, tables_ref = refs[:6]
        column_ref, row_ref, projected_back, bias_out = refs[6:10]
        parts_out, head_stack = refs[10:-1], refs[-1]
        if padded > block:
            head_stack[:, :, block:] = jnp.zeros((rep_size, count, padded - block), BF)
        for j in range(rep_size):
            owner = pl.ds(pl.multiple_of((r_ref[0] ^ j) * group_tokens, 16), group_tokens)
            for g in range(rep_size):
                head_stack[j, g * group_tokens : (g + 1) * group_tokens, :block] = heads[
                    owner, g * block : (g + 1) * block
                ]
        bias_out[...] = jnp.zeros_like(bias_out)

        def row(j, carry):
            here = pl.ds(pl.multiple_of(j * count, count), count)
            query, key, value, back = query_ref[j], key_ref[j], value_ref[j], head_stack[j]
            same = column_ref[j, :, 0:1] == row_ref[j, 0:1, :]
            query_back = jnp.zeros((count, padded), F32)
            key_back = jnp.zeros((count, padded), F32)
            value_back = jnp.zeros((count, padded), F32)
            for h in range(local_heads):
                mask = head_mask(h)
                query_head, back_head = query * mask, back * mask
                probs = probabilities(query_head, key, same)
                probs_back = dot_rt(back_head, value)
                scores_back = (
                    probs
                    * (probs_back - jnp.sum(probs * probs_back, axis=-1, keepdims=True))
                ).astype(BF)
                value_back = value_back + dot_lt(probs.astype(BF), back_head)
                query_back = query_back + dot(scores_back, key * mask)
                key_back = key_back + dot_lt(scores_back, query_head)
            cos_row, sin_row = rotary(tables_ref, column_ref[j])
            query_back = turn(query_back * score_scale, cos_row, sin_row, -1.0)
            key_back = turn(key_back * score_scale, cos_row, sin_row, -1.0)
            low = [value.astype(BF) for value in (query_back, key_back, value_back)]
            for t in range(3):
                projected_back[here, t * block : (t + 1) * block] = low[t][:, :block]
                bias_out[:, t * padded : (t + 1) * padded] += jnp.sum(
                    low[t].astype(F32), axis=0, keepdims=True
                )
            store_part(j, dot_rt(jnp.concatenate(low, axis=1), wide[...]), parts_out)
            return carry

        lax.fori_loop(0, rep_size, row, 0)

    projected_back, projection_bias_sum, *one_parts = call(
        order,
        attention_back_kernel,
        "attention_back",
        [r_index],
        [heads_back, query_all, key_all, value_all, wide_weight, tables]
        + [place_columns, place_rows],
        [((flat, 3 * block), BF), ((1, 3 * padded), F32)] + part_shapes(rep_size, count, width),
        90.0,
        scratch=[((rep_size, count, padded), BF)],
        limit=44,
    )
    one_addends = send(one_parts, "rep", rep_size)

    def attention_gradient_kernel(attended_ref, own_back, hidden_all, back, out):
        step_width = width // 3
        for m in range(3):
            at = slice(m * step_width, (m + 1) * step_width)
            out[at, :width] = dot_lt(attended_ref[:, at], own_back[...]).astype(BF)
            out[at, width:] = dot_lt(hidden_all[:, at], back[...]).astype(BF)

    (attention_gradient,) = call(
        order,
        attention_gradient_kernel,
        "attention_gradient",
        [],
        [wait_for(attended, feed_addends), branch_back, hidden_one_all, projected_back],
        [((width, width + 3 * block), BF)],
        6.4,
        limit=32,
    )
    attention_sum = sent_gradient(attention_gradient)

    def output_kernel(*refs):
        feeds = refs[:rep_size]
        tokens_ref, branch_ref, cotangent_ref, places, modulation = refs[rep_size : rep_size + 5]
        block_out, sums_out, sums = refs[rep_size + 5 :]
        sums[...] = jnp.zeros_like(sums)

        def step(here):
            slot_of = places[0, here, 0:1]
            feed = feeds[0][here, :]
            for ref in feeds[1:]:
                feed = feed + ref[here, :].astype(F32)
            gate_one = pick(modulation, slot_of, 2 * width, width)
            middle = tokens_ref[here, :].astype(F32) + gate_one * branch_ref[here, :]
            gate_two = pick(modulation, slot_of, 5 * width, width)
            block_out[here, :] = (middle + gate_two * feed).astype(BF)
            masked = cotangent_ref[here, :].astype(F32) * places[0, here, 3:4]
            add_slots(sums, 0, slots, slot_of, masked * feed)

        chunks(count, step, 1)
        sums_out[...] = jnp.sum(sums[...], axis=1)

    block_output, gate_two_sums = call(
        order,
        output_kernel,
        "layer_output",
        [],
        feed_addends + [tokens, branch, cotangent, place_columns, modulation],
        [((count, width), BF), ((slots, width), F32)],
        30.0,
        scratch=[((slots, 8, width), F32)],
        limit=16,
        near=range(1, rep_size),
    )

    def first_back_kernel(r_ref, *refs):
        addends = refs[:rep_size]
        tokens_ref, back_ref, modulation, places, middle_ref, gate_two_ref, bias, out_bias = refs[
            rep_size : rep_size + 8
        ]
        gradient, back_blocks, sums, whole, whole_bias, stack = refs[rep_size + 8 :]
        sums[...] = jnp.zeros_like(sums)

        def step(here):
            slot_of = places[0, here, 0:1]
            upstream = addends[0][here, :]
            for ref in addends[1:]:
                upstream = upstream + ref[here, :].astype(F32)
            normed, inverse = normalize_keep(tokens_ref[here, :].astype(F32))
            scale = pick(modulation, slot_of, width, width)
            gradient[here, :] = back_ref[here, :] + normalize_back(
                normed, inverse, upstream * (1.0 + scale)
            )
            add_slots(sums, 0, slots, slot_of, upstream)
            add_slots(sums, slots, slots, slot_of, upstream * normed)

        chunks(count, step)
        total = jnp.sum(sums[...], axis=1)
        whole[:, :width] = total[:slots]
        whole[:, width : 2 * width] = total[slots:]
        for t in range(3):
            at = slice((2 + t) * width, (3 + t) * width)
            whole[:, at] = middle_ref[t * slots : (t + 1) * slots, :]
        whole[:, 5 * width :] = gate_two_ref[...]
        whole_bias[...] = jnp.zeros_like(whole_bias)
        for k in range(rep_size):

            @pl.when(r_ref[0] == k)
            def _():
                for t in range(3):
                    first = t * width + k * block
                    whole_bias[:, first : first + block] = bias[:, t * padded : t * padded + block]

        stack[...] = jnp.zeros_like(stack)
        for k in range(fsdp_size):
            stack[k, :slots, :] = whole[:, k * columns : (k + 1) * columns]
            at = slice(k * shard_bias, (k + 1) * shard_bias)
            stack[k, slots : slots + 1, :shard_bias] = whole_bias[:, at]
            at = slice(k * shard_out_bias, (k + 1) * shard_out_bias)
            lanes = slice(shard_bias, shard_bias + shard_out_bias)
            stack[k, slots : slots + 1, lanes] = out_bias[:, at]
        back_blocks[...] = stack[...].reshape(fsdp_size * GROUP, columns).astype(BF)

    tokens_gradient, back_blocks = call(
        order,
        first_back_kernel,
        "first_norm_back",
        [r_index],
        one_addends
        + [tokens, middle_back, modulation, place_columns, middle_sums, gate_two_sums]
        + [projection_bias_sum, output_bias_sum],
        [((count, width), F32), ((fsdp_size * GROUP, columns), BF)],
        30.0,
        scratch=[
            ((2 * slots, 8, width), F32),
            ((slots, 6 * width), F32),
            ((1, 3 * width), F32),
            ((fsdp_size, GROUP, columns), F32),
        ],
        limit=20,
        near=range(1, rep_size),
    )

    line_backs = exchange(back_blocks, "fsdp")
    feed_sums = gather(wait_for(feed_sum, one_addends), "rep", rep_size)

    def conditioning_kernel(groups, activated_ref, weight, out, line_out):
        stack = groups[...].astype(F32)
        bias = jnp.sum(stack.reshape(fsdp_size, GROUP, columns), axis=0)[slots : slots + 1]
        row_ids = lax.broadcasted_iota(jnp.int32, (fsdp_size * GROUP, 1), 0)
        rows_back = jnp.where(lax.rem(row_ids, GROUP) < slots, stack, 0.0)
        line_out[:, :width] = activated_ref[...]
        line_out[:, width:] = jnp.where(row_ids == slots, bias, rows_back).astype(BF)
        result = dot(rows_back.astype(BF), weight[...])
        for k in range(fsdp_size):
            out[k * slots : (k + 1) * slots, :] = result[k * GROUP : k * GROUP + slots, :]

    activated_backs, line_back = call(
        order,
        conditioning_kernel,
        "conditioning_back",
        [],
        [wait_for(line_backs, feed_sums[1:3]), line_activated, modulation_weight.T],
        [((fsdp_size * slots, width), F32), ((fsdp_size * GROUP, width + columns), BF)],
        40.0,
        limit=24,
    )
    activated_backs = exchange(activated_backs, "fsdp")
    all_lines = gather(line_back, "rep", rep_size)

    def feed_blocks_kernel(r_ref, *refs):
        gate_out, up_out, down_out, stack = refs[rep_size:]
        for j in range(rep_size):
            stack[j] = refs[j][...].astype(F32)
        for k in range(rep_size):
            here = r_ref[0] ^ k
            for j in range(fsdp_size):
                target = slice(j * shard_ff + k * piece, j * shard_ff + (k + 1) * piece)
                first = block_ff + j * piece
                gate_out[:, target] = stack[here, :, j * piece : (j + 1) * piece]
                up_out[:, target] = stack[here, :, first : first + piece]
            for a, lanes, c, packed_lanes in units:
                to_row = k * piece + a
                down_out[to_row : to_row + unit_rows, lanes] = stack[
                    here, c : c + unit_rows, packed_lanes
                ]

    gate_gradient, up_gradient, down_gradient = call(
        order,
        feed_blocks_kernel,
        "feed_blocks",
        [r_index],
        feed_sums,
        [((shard_width, fsdp_size * shard_ff), F32)] * 2 + [((shard_ff, width), F32)],
        5.2,
        scratch=[((rep_size, shard_width, 3 * block_ff), F32)],
        limit=24,
        near=range(1, rep_size),
    )

    def table_kernel(*refs):
        lines, (condition, activated_back) = refs[:rep_size], refs[rep_size : rep_size + 2]
        table, table_bias, bias, out_bias, gradient, activated_stack, back_stack = refs[
            rep_size + 2 :
        ]
        upstream = jnp.sum(activated_back[...].reshape(fsdp_size, slots, width), axis=0)
        gradient[...] = upstream * silu_slope(condition[...].astype(F32))
        line = fsdp_size * GROUP
        total = jnp.zeros((1, columns), F32)
        for j in range(rep_size):
            back = lines[j][:, width:]
            activated_stack[j * line : (j + 1) * line, :] = lines[j][:, :width]
            back_stack[j * line : (j + 1) * line, :] = back
            total = total + back.astype(F32)[slots : slots + 1, :]
        bias[...] = total[:, :shard_bias]
        out_bias[...] = total[:, shard_bias : shard_bias + shard_out_bias]
        back = back_stack[...].astype(F32)
        in_group = lax.rem(lax.broadcasted_iota(jnp.int32, (rep_size * line, 1), 0), GROUP)
        table_bias[...] = jnp.sum(
            jnp.where(in_group < slots, back, 0.0), axis=0, keepdims=True
        )
        table[...] = dot_lt(back_stack[...], activated_stack[...])

    table_gradient, table_bias_gradient, bias_gradient, out_bias_gradient, activated_gradient = call(
        order,
        table_kernel,
        "table_gradient",
        [],
        all_lines + [conditioning[0], activated_backs],
        [((columns, width), F32), ((1, columns), F32)]
        + [((1, shard_bias), F32), ((1, shard_out_bias), F32), ((slots, width), F32)],
        4.0,
        scratch=[
            ((rep_size * fsdp_size * GROUP, width), BF),
            ((rep_size * fsdp_size * GROUP, columns), BF),
        ],
        limit=24,
        near=range(1, rep_size),
    )

    attention_late = wait_for(attention_sum, table_gradient)
    output_gradient = attention_late[:, :width].astype(F32)
    projection_sums = gather(attention_late[:, width:], "rep", rep_size)
    for bit in [1 << k for k in range(rep_size.bit_length() - 1)]:
        came = swap_with(output_gradient.astype(BF), "rep", rep_size, bit)
        came = wait_for(came, projection_sums[2 % rep_size]) if bit == 1 else came
        output_gradient = output_gradient + came.astype(F32)

    def projection_blocks_kernel(r_ref, *refs):
        out, stack = refs[rep_size:]
        for j in range(rep_size):
            stack[j] = refs[j][...].astype(F32)
        for k in range(rep_size):
            here = r_ref[0] ^ k
            for t in range(3):
                first = t * width + k * block
                out[:, first : first + block] = stack[here, :, t * block : (t + 1) * block]

    (projection_gradient,) = call(
        order,
        projection_blocks_kernel,
        "projection_blocks",
        [r_index],
        projection_sums,
        [((shard_width, 3 * width), F32)],
        3.0,
        scratch=[((rep_size, shard_width, 3 * block), F32)],
        limit=24,
        near=range(1, rep_size),
    )
    return (
        block_output[None],
        tokens_gradient[None],
        activated_gradient[None],
        table_gradient.T,
        table_bias_gradient[0],
        projection_gradient,
        bias_gradient[0],
        output_gradient,
        out_bias_gradient[0],
        gate_gradient,
        up_gradient,
        down_gradient,
    )


def solution(mesh):
    sizes = dict(mesh.shape)

    def body(*arrays):
        return on_device(sizes["rep"], sizes["fsdp"], *arrays)

    rows = ("rep", "fsdp")
    in_specs = (
        P(rows, None, None),
        P(rows, None, None),
        P(rows, None),
        P(rows, None),
        P(rows, None),
        P(rows, None),
        P(None, "fsdp"),
        P("fsdp"),
        P("fsdp", None),
        P("fsdp"),
        P("fsdp", None),
        P("fsdp"),
        P("fsdp", None),
        P("fsdp", None),
        P("fsdp", None),
        P(rows, None, None),
    )
    out_specs = (
        P(rows, None, None),
        P(rows, None, None),
        P(rows, None, None),
        P(None, "fsdp"),
        P("fsdp"),
        P("fsdp", None),
        P("fsdp"),
        P("fsdp", None),
        P("fsdp"),
        P("fsdp", None),
        P("fsdp", None),
        P("fsdp", None),
    )
    return jax.shard_map(
        body, mesh=mesh, in_specs=in_specs, out_specs=out_specs, check_vma=False
    )
```

```python
import math

import jax
import jax.numpy as jnp
import numpy as np
from jax import lax
from jax.experimental import pallas as pl
from jax.experimental.pallas import tpu as pltpu
from jax.sharding import PartitionSpec as P

HEADS = 16
BF = jnp.bfloat16
F32 = jnp.float32
LANES = 128
CHUNK = 32
GROUP = 8


def wait_for(value, *others):
    return lax.optimization_barrier((value, others))[0]


def swap_with(value, axis, size, bit):
    return lax.ppermute(value, axis, [(i, i ^ bit) for i in range(size)])


def gather(value, axis, size):
    return [value] + [swap_with(value, axis, size, j) for j in range(1, size)]


def halves_gather(top, low, axis, size):
    if size != 4:
        return list(zip(gather(top, axis, size), gather(low, axis, size), strict=True))
    top_one, low_two = swap_with(top, axis, size, 1), swap_with(low, axis, size, 2)
    top_three, low_three = swap_with(top_one, axis, size, 2), swap_with(low_two, axis, size, 1)
    low_one, top_two = swap_with(low, axis, size, 1), swap_with(top, axis, size, 2)
    return [(top, low), (top_one, low_one), (top_two, low_two), (top_three, low_three)]


def send(values, axis, size):
    return [values[0]] + [swap_with(values[j], axis, size, j) for j in range(1, size)]


def exchange(value, axis):
    return lax.all_to_all(value, axis, 0, 0, tiled=True)


def block_of(shape, by_step, offset=0):
    if by_step:
        return pl.BlockSpec(shape, lambda i: (i + offset,) + (0,) * (len(shape) - 1))
    zeros = (0,) * len(shape)
    return pl.BlockSpec(shape, lambda i: zeros, pipeline_mode=pl.Buffered(1))


def call(order, body, name, scalars, arrays, outs, micros, scratch=(), limit=48, near=(), steps=1, free=()):
    shapes = [
        jax.ShapeDtypeStruct(*out[:2]) if n in free else pltpu.HBM(*out[:2])
        for n, out in enumerate(outs)
    ]
    out_specs = [block_of(out[-1], True) if len(out) > 2 else block_of(out[0], False) for out in outs]
    in_specs = [
        block_of(array[1], len(array) > 2, *array[3:])
        if isinstance(array, tuple)
        else block_of(array.shape, False)
        for array in arrays
    ]
    arrays = [array[0] if isinstance(array, tuple) else array for array in arrays]
    if order:
        first, _ = lax.optimization_barrier((arrays[0], order.pop()))
        arrays = [first] + list(arrays[1:])
    arrays = [
        array if n in near else pltpu.with_memory_space_constraint(array, pltpu.HBM)
        for n, array in enumerate(arrays)
    ]
    results = pl.pallas_call(
        body,
        name=name,
        grid=(steps,),
        out_shape=shapes,
        in_specs=[pl.BlockSpec(memory_space=pltpu.SMEM)] * len(scalars)
        + in_specs,
        out_specs=out_specs,
        scratch_shapes=[pltpu.VMEM(shape, dtype) for shape, dtype in scratch],
        compiler_params=pltpu.CompilerParams(vmem_limit_bytes=limit << 20),
        cost_estimate=pl.CostEstimate(
            flops=int(micros * 1.000e+09), bytes_accessed=int(micros * 3.000e+06), transcendentals=0
        ),
    )(*scalars, *arrays)
    order.append(results[0])
    return results


def part_shapes(size, tokens, width):
    return [((tokens, width), F32)] + [((tokens, width), BF)] * (size - 1)


def store_part(j, value, refs):
    for k, ref in enumerate(refs):

        @pl.when(j == k)
        def _(ref=ref):
            ref[...] = value.astype(ref.dtype)


def dot(left, right):
    return jnp.dot(left, right, preferred_element_type=F32)


def dot_rt(left, right):
    return lax.dot_general(left, right, (((1,), (1,)), ((), ())), preferred_element_type=F32)


def dot_lt(left, right):
    return lax.dot_general(left, right, (((0,), (0,)), ((), ())), preferred_element_type=F32)


def pick(modulation, slot_of, first, width):
    total = jnp.zeros((slot_of.shape[0], width), F32)
    for k in range(modulation.shape[0]):
        total = jnp.where(slot_of == k, modulation[k : k + 1, first : first + width], total)
    return total


def normalize_keep(values):
    centered = values - jnp.mean(values, axis=-1, keepdims=True)
    variance = jnp.mean(centered * centered, axis=-1, keepdims=True)
    inverse = lax.rsqrt(variance + 1e-06)
    return centered * inverse, inverse


def normalize_back(normed, inverse, upstream):
    return inverse * (
        upstream
        - jnp.mean(upstream, axis=-1, keepdims=True)
        - normed * jnp.mean(upstream * normed, axis=-1, keepdims=True)
    )


def add_slots(sums, base, count, slot_of, values):
    rows, width = values.shape
    for k in range(count):
        chosen = jnp.where(slot_of == k, values, 0.0)
        sums[base + k] += jnp.sum(chosen.reshape(rows // 8, 8, width), axis=0)


def chunks(tokens, step, unroll=2):
    def body(i, carry):
        step(pl.ds(pl.multiple_of(i * CHUNK, CHUNK), CHUNK))
        return carry

    lax.fori_loop(0, tokens // CHUNK, body, 0, unroll=unroll)


def silu_slope(values):
    sigmoid = jax.nn.sigmoid(values)
    return sigmoid * (1.0 + values * (1.0 - sigmoid))


def on_device(
    rep_size,
    fsdp_size,
    tokens,
    conditioning,
    segment_ids,
    heights,
    widths,
    pad_mask,
    modulation_weight,
    modulation_bias,
    projection_weight,
    projection_bias,
    output_weight,
    output_bias,
    gate_weight,
    up_weight,
    down_weight,
    cotangent,
):
    rows, count, width = tokens.shape
    assert rows == 1
    slots = conditioning.shape[1]
    head_width = width // HEADS
    local_heads = HEADS // rep_size
    block = width // rep_size
    padded = -(-block // LANES) * LANES
    score_scale = 1.0 / math.sqrt(head_width)
    shard_ff = down_weight.shape[0]
    piece = shard_ff // rep_size
    block_ff = fsdp_size * piece
    shard_width = projection_weight.shape[0]
    columns = modulation_weight.shape[1]
    flat = rep_size * count
    half = count // 2
    group_tokens = count // rep_size
    others = rep_size - 1
    r = lax.axis_index("rep")
    r_index = r.reshape(1).astype(jnp.int32)
    tokens, cotangent = tokens[0], cotangent[0]
    order = []

    def qkv_shard_kernel(r_ref, projection, output, out):
        out[:, :width] = output[...]
        for k in range(rep_size):

            @pl.when(r_ref[0] == k)
            def _():
                for t in range(3):
                    first, to = t * width + k * block, width + t * block
                    out[:, to : to + block] = projection[:, first : first + block]

    (qkv_shard,) = call(
        order,
        qkv_shard_kernel,
        "qkv_shard",
        [r_index],
        [projection_weight, output_weight],
        [((shard_width, width + 3 * block), BF)],
        4.5,
        limit=16,
    )

    slot_ids = jnp.arange(slots, dtype=jnp.int32)
    member_ints = (segment_ids[:, :, None] == slot_ids).astype(jnp.int32)
    before_ints = (slot_ids < segment_ids[:, :, None]).astype(jnp.int32)
    starts = jnp.sum(before_ints * (heights * widths)[:, None, :], axis=2)
    offsets = jnp.arange(count, dtype=jnp.int32)[None, :] - starts
    row_width = jnp.sum(member_ints * widths[:, None, :], axis=2)
    places = jnp.concatenate(
        [segment_ids, offsets // row_width, offsets % row_width, pad_mask], axis=1
    ).astype(BF)
    places = jnp.pad(places, ((0, GROUP - 1), (0, width - 4 * count)))
    token_rows = gather(jnp.concatenate([tokens, places], axis=0), "rep", rep_size)

    cond_float = conditioning.astype(F32)
    activated = jax.nn.silu(cond_float).astype(BF).reshape(slots, width)
    shard_bias, shard_out_bias = projection_bias.shape[0], output_bias.shape[0]
    bias_row = jnp.pad(
        jnp.concatenate([projection_bias, output_bias]), (0, width - shard_bias - shard_out_bias)
    )[None]
    group_rows = jnp.concatenate(
        [activated, bias_row, jnp.zeros((GROUP - slots - 1, width), BF)], axis=0
    )
    line_rows = lax.all_gather(group_rows, "fsdp", axis=0, tiled=True)

    def modulate_kernel(r_ref, *refs):
        groups, weight, bias = refs[:3]
        out, activated_out, bias_out, out_bias, stack, whole = refs[3:]
        stack[...] = groups[...].astype(F32).reshape(fsdp_size, GROUP, width)
        in_group = lax.rem(lax.broadcasted_iota(jnp.int32, (fsdp_size * GROUP, 1), 0), GROUP)
        rows_low = jnp.where(in_group < slots, groups[...].astype(F32), 0.0).astype(BF)
        activated_out[...] = rows_low
        out[...] = dot_rt(rows_low, weight[...]) + bias[...]
        for k in range(fsdp_size):
            row = stack[k, slots : slots + 1, :]
            whole[:, k * shard_bias : (k + 1) * shard_bias] = row[:, :shard_bias]
            at = slice(k * shard_out_bias, (k + 1) * shard_out_bias)
            out_bias[:, at] = row[:, shard_bias : shard_bias + shard_out_bias]
        bias_out[...] = jnp.zeros_like(bias_out)
        for k in range(rep_size):

            @pl.when(r_ref[0] == k)
            def _():
                for t in range(3):
                    first = t * width + k * block
                    bias_out[:, t * padded : t * padded + block] = whole[:, first : first + block]

    line_modulation, line_activated, own_bias, output_bias_all = call(
        order,
        modulate_kernel,
        "modulate",
        [r_index],
        [line_rows, modulation_weight.T, modulation_bias.astype(F32)[None]],
        [
            ((fsdp_size * GROUP, columns), F32),
            ((fsdp_size * GROUP, width), BF),
            ((1, 3 * padded), F32),
            ((1, width), F32),
        ],
        6.0,
        scratch=[((fsdp_size, GROUP, width), F32), ((1, 3 * width), F32)],
        limit=24,
    )
    own_modulation = lax.all_to_all(line_modulation, "fsdp", 0, 0, tiled=True)

    unit_rows, unit_lanes = math.gcd(piece, shard_width), math.gcd(width, block_ff)
    units = []
    for u in range((piece // unit_rows) * (width // unit_lanes)):
        (a, b), (c, d) = divmod(u, width // unit_lanes), divmod(u, block_ff // unit_lanes)
        units.append(
            (
                a * unit_rows,
                slice(b * unit_lanes, (b + 1) * unit_lanes),
                c * unit_rows,
                slice(2 * block_ff + d * unit_lanes, 2 * block_ff + (d + 1) * unit_lanes),
            )
        )

    def feed_shard_kernel(r_ref, gate, up, down, out):
        for k in range(rep_size):

            @pl.when(r_ref[0] == k)
            def _():
                for j in range(fsdp_size):
                    source = slice(j * shard_ff + k * piece, j * shard_ff + (k + 1) * piece)
                    out[:, j * piece : (j + 1) * piece] = gate[:, source]
                    first = block_ff + j * piece
                    out[:, first : first + piece] = up[:, source]
                for a, lanes, c, packed_lanes in units:
                    out[c : c + unit_rows, packed_lanes] = down[
                        k * piece + a : k * piece + a + unit_rows, lanes
                    ]

    (feed_shard,) = call(
        order,
        feed_shard_kernel,
        "feed_shard",
        [r_index],
        [gate_weight, up_weight, down_weight],
        [((shard_width, 3 * block_ff), BF)],
        4.5,
        limit=16,
    )
    qkv_block = lax.all_gather(qkv_shard, "fsdp", axis=0, tiled=True)
    feed_block = lax.all_gather(feed_shard, "fsdp", axis=0, tiled=True)

    def norm_rows_kernel(*refs):
        out, columns_out, rows_out = refs[rep_size:]
        for j in range(rep_size):
            ref = refs[j]

            def step(at, ref=ref, j=j):
                normed, _ = normalize_keep(ref[at, :].astype(F32))
                out[pl.ds(j * count + at.start, CHUNK), :] = normed

            chunks(count, step)
            line = ref[count:, :].astype(F32)
            for q in range(4):
                rows_out[j, q : q + 1, :] = line[:1, q * count : (q + 1) * count]
            rows_out[j, 4:, :] = jnp.zeros((4, count), F32)
            columns_out[j] = rows_out[j].T

    normed_rows, place_columns, place_rows = call(
        order,
        norm_rows_kernel,
        "first_norm",
        [],
        token_rows,
        [((flat, width), F32), ((rep_size, count, 8), F32), ((rep_size, 8, count), F32)],
        18.0,
        limit=24,
        near=range(1, rep_size),
        free=(0,),
    )
    pair_count = head_width // 4
    most_rows, most_columns = count // 4, 32
    lane = np.arange(padded)
    in_head = lane % head_width
    lane_frequency = 10000.0 ** (-(in_head % pair_count) / pair_count)
    of_row = (lane < block) & (in_head < 2 * pair_count)
    of_column = (lane < block) & (in_head >= 2 * pair_count)
    sign = np.where((in_head // pair_count) % 2 == 1, 1.0, -1.0)
    row_angle = np.arange(most_rows)[:, None] * lane_frequency
    column_angle = np.arange(most_columns)[:, None] * lane_frequency
    tables = np.concatenate(
        [
            np.concatenate(
                [
                    np.where(of_row, np.cos(row_angle), 0.0),
                    np.where(of_column, np.cos(column_angle), 0.0),
                ]
            ),
            np.concatenate(
                [
                    np.where(of_row, sign * np.sin(row_angle), 0.0),
                    np.where(of_column, sign * np.sin(column_angle), 0.0),
                ]
            ),
        ],
        axis=1,
    ).astype(np.float32)
    pieces, left = [], tables
    for _ in range(3):
        pieces.append(left.astype(jnp.bfloat16))
        left = left - pieces[-1].astype(np.float32)
    tables = jnp.asarray(np.stack(pieces))

    def rotary(tables_ref, places):
        numbers = lax.broadcasted_iota(jnp.int32, (count, most_rows + most_columns), 1).astype(F32)
        is_row = (numbers < most_rows) & (numbers == places[:, 1:2])
        is_column = (numbers >= most_rows) & (numbers - most_rows == places[:, 2:3])
        chosen = jnp.where(is_row | is_column, 1.0, 0.0).astype(BF)
        both = dot(chosen, tables_ref[2]) + dot(chosen, tables_ref[1]) + dot(chosen, tables_ref[0])
        return both[:, :padded], both[:, padded:]

    def modulation_kernel(arrived, modulation, sent):
        for k in range(fsdp_size):
            at = slice(k * columns, (k + 1) * columns)
            modulation[:, at] = arrived[k * GROUP : k * GROUP + slots, :]
        sent[:, : 2 * width] = modulation[:, : 2 * width]
        sent[:, 2 * width :] = modulation[:, 5 * width :]

    modulation, sent_modulation = call(
        order,
        modulation_kernel,
        "modulation",
        [],
        [wait_for(own_modulation, normed_rows)],
        [((slots, 6 * width), F32), ((slots, 3 * width), F32)],
        3.0,
        limit=8,
    )
    modulation_rows = gather(sent_modulation, "rep", rep_size)
    cotangent_rows = gather(wait_for(cotangent, modulation_rows), "rep", rep_size)

    def head_mask(h):
        lanes = lax.broadcasted_iota(jnp.int32, (1, padded), 1)
        inside = (lanes >= h * head_width) & (lanes < (h + 1) * head_width)
        return jnp.where(inside, 1.0, 0.0).astype(BF)

    def probabilities(query_head, key, same):
        scores = jnp.where(same, dot_rt(query_head, key) * score_scale, -1e30)
        exponent = jnp.exp(scores - jnp.max(scores, axis=-1, keepdims=True))
        return exponent / jnp.sum(exponent, axis=-1, keepdims=True)

    def turn(values, cosine_row, sine_row, sense):
        before = pltpu.roll(values, pair_count, 1)
        after = pltpu.roll(values, padded - pair_count, 1)
        lanes = lax.broadcasted_iota(jnp.int32, (1, padded), 1)
        second = lax.rem(lanes, 2 * pair_count) >= pair_count
        return values * cosine_row + jnp.where(second, before, after) * (sense * sine_row)

    def attention_kernel(r_ref, *refs):
        modulations = refs[:rep_size]
        normed, weight, bias, tables_ref, column_ref, row_ref = refs[rep_size : rep_size + 6]
        hidden_all, wide, query_out, key_out, value_out, attended_out, modulation_stack = refs[
            rep_size + 6 :
        ]
        for j in range(rep_size):
            modulation_stack[j] = modulations[j][:, : 2 * width]
        for t in range(3):
            first = width + t * block
            wide[:, t * padded : t * padded + block] = weight[:, first : first + block]
            if padded > block:
                wide[:, t * padded + block : (t + 1) * padded] = jnp.zeros(
                    (width, padded - block), BF
                )

        def row(j, carry):
            first = pl.multiple_of(j * count, count)

            def step(at):
                here = pl.ds(pl.multiple_of(first + at.start, CHUNK), CHUNK)
                slot_of = column_ref[j, at, 0:1]
                scale = pick(modulation_stack[j], slot_of, width, width)
                shift = pick(modulation_stack[j], slot_of, 0, width)
                hidden_all[here, :] = (normed[here, :] * (1.0 + scale) + shift).astype(BF)

            chunks(count, step)
            projected = dot(hidden_all[pl.ds(first, count), :], wide[...]) + bias[...]
            cos_row, sin_row = rotary(tables_ref, column_ref[j])
            query = turn(projected[:, :padded], cos_row, sin_row, 1.0).astype(BF)
            key = turn(projected[:, padded : 2 * padded], cos_row, sin_row, 1.0).astype(BF)
            value = projected[:, 2 * padded :].astype(BF)
            query_out[j], key_out[j], value_out[j] = query, key, value
            same = column_ref[j, :, 0:1] == row_ref[j, 0:1, :]
            total = jnp.zeros((count, padded), F32)
            for h in range(local_heads):
                mask = head_mask(h)
                probs = probabilities(query * mask, key, same)
                total = total + dot(probs.astype(BF), value * mask)
            owner = pl.ds(pl.multiple_of((r_ref[0] ^ j) * group_tokens, 16), group_tokens)
            low = total[:, :block].astype(BF)
            for g in range(rep_size):
                attended_out[owner, g * block : (g + 1) * block] = low[
                    g * group_tokens : (g + 1) * group_tokens, :
                ]
            return carry

        lax.fori_loop(0, rep_size, row, 0)

    hidden_one_all, wide_weight, query_all, key_all, value_all, attended_heads = call(
        order,
        attention_kernel,
        "attention",
        [r_index],
        modulation_rows
        + [normed_rows, qkv_block, own_bias, tables, place_columns, place_rows],
        [((flat, width), BF), ((width, 3 * padded), BF)]
        + [((rep_size, count, padded), BF)] * 3
        + [((count, width), BF)],
        66.0,
        scratch=[((rep_size, slots, 2 * width), F32)],
        limit=44,
        near=range(1, rep_size + 1),
    )
    own_heads = exchange(attended_heads, "rep")

    def feed_back_kernel(*refs):
        cotangents, modulations = refs[:rep_size], refs[rep_size : 2 * rep_size]
        columns_ref, out = refs[2 * rep_size :]
        for j in range(rep_size):

            def step(at, j=j):
                masked = cotangents[j][at, :].astype(F32) * columns_ref[j, at, 3:4]
                gate = pick(modulations[j], columns_ref[j, at, 0:1], 2 * width, width)
                out[pl.ds(j * count + at.start, CHUNK), :] = (gate * masked).astype(BF)

            chunks(count, step)

    (feed_back_all,) = call(
        order,
        feed_back_kernel,
        "feed_back",
        [],
        cotangent_rows + modulation_rows + [place_columns],
        [((flat, width), BF)],
        12.0,
        limit=24,
        near=(*range(1, rep_size), *range(rep_size + 1, 2 * rep_size)),
        free=(0,),
    )

    def middle_kernel(
        heads, weight, bias, tokens_ref, modulation, places, branch, normed_out, inverse_out,
        top, low, attended,
    ):
        for k in range(rep_size):
            for g in range(rep_size):
                attended[
                    g * group_tokens : (g + 1) * group_tokens, k * block : (k + 1) * block
                ] = heads[k * group_tokens : (k + 1) * group_tokens, g * block : (g + 1) * block]
        branch[...] = dot(attended[...], weight[...]) + bias[...]

        for p, hidden in enumerate((top, low)):

            def step(at, p=p, hidden=hidden):
                here = pl.ds(p * half + at.start, CHUNK)
                slot_of = places[0, here, 0:1]
                gate = pick(modulation, slot_of, 2 * width, width)
                middle = tokens_ref[here, :].astype(F32) + gate * branch[here, :]
                normed, inverse = normalize_keep(middle)
                normed_out[here, :] = normed
                inverse_out[here, :] = inverse
                scale = pick(modulation, slot_of, 4 * width, width)
                hidden[at, :] = (
                    normed * (1.0 + scale) + pick(modulation, slot_of, 3 * width, width)
                ).astype(BF)

            chunks(half, step)

    branch, normed_two, inverse_two, hidden_top, hidden_low, attended = call(
        order,
        middle_kernel,
        "second_norm",
        [],
        [own_heads, (qkv_block, (width, width)), output_bias_all, tokens, modulation, place_columns],
        [((count, width), F32), ((count, width), F32), ((count, 1), F32)]
        + [((half, width), BF)] * 2
        + [((count, width), BF)],
        21.0,
        limit=24,
    )
    hidden_two_rows = halves_gather(hidden_top, hidden_low, "rep", rep_size)
    hidden_two_rows = [piece for row in hidden_two_rows for piece in row]


    step_ff = 256 if block_ff % 256 == 0 else 128
    taken = count

    def feed_kernel(unpack, rows_here, *refs):
        back, weight = refs[2 * rows_here : 2 * rows_here + 2]
        refs_here = refs[2 * rows_here + 2 :]
        if unpack:
            hidden_out, three, both_back, down = refs_here[:4]
        else:
            down, hidden_out, three, both_back = refs_here[:4]
        parts_out, hidden_all = refs_here[4:-1], refs_here[-1]
        j = pl.program_id(0)

        @pl.when(j == 0)
        def _():
            for n in range(2 * rows_here):
                hidden_all[n * half : (n + 1) * half, :] = refs[n][...]
            if not unpack:
                return
            for k in range(fsdp_size):
                for a, lanes, c, packed_lanes in units:
                    from_row, to_row = k * shard_width + c, k * piece + a
                    down[to_row : to_row + unit_rows, lanes] = weight[
                        from_row : from_row + unit_rows, packed_lanes
                    ]

        hidden = hidden_all[pl.ds(pl.multiple_of(j * count, count), count), :]
        hidden_out[...] = hidden
        for c in range(block_ff // step_ff):
            at = slice(c * step_ff, (c + 1) * step_ff)
            up_at = slice(block_ff + c * step_ff, block_ff + (c + 1) * step_ff)
            gate = dot(hidden, weight[:, at])
            up = dot(hidden, weight[:, up_at])
            hidden_back = dot_rt(back[...], down[at, :])
            sigmoid = jax.nn.sigmoid(gate)
            silu = gate * sigmoid
            three[:, at] = (silu * up).astype(BF)
            slope = sigmoid * (1.0 + gate * (1.0 - sigmoid))
            both_back[:, at] = (hidden_back * up * slope).astype(BF)
            both_back[:, up_at] = (hidden_back * silu).astype(BF)
        store_part(j, dot_rt(both_back[...], weight[:, : 2 * block_ff]), parts_out)

    near_rows = rep_size - 1
    far_rows = rep_size - near_rows
    row_outs = [((width,), BF), ((block_ff,), BF), ((2 * block_ff,), BF)]

    def rows_out(row_count):
        return [((row_count * count,) + w, d, (count,) + w) for w, d in row_outs]

    far_hidden, far_three, far_both, down_block, *far_parts = call(
        order,
        lambda *refs: feed_kernel(True, far_rows, *refs),
        "feed_far",
        [],
        hidden_two_rows[2 * near_rows :]
        + [(feed_back_all, (count, width), True, near_rows), feed_block],
        rows_out(far_rows) + [((block_ff, width), BF)] + [((count, width), BF)] * far_rows,
        15.0,
        scratch=[((far_rows * count, width), BF)],
        limit=40,
        near=range(2 * far_rows + 1),
        steps=far_rows,
        free=range(3),
    )
    near_hidden, near_three, near_both, *near_parts = call(
        order,
        lambda *refs: feed_kernel(False, near_rows, *refs),
        "feed_near",
        [],
        hidden_two_rows[: 2 * near_rows]
        + [(feed_back_all, (count, width), True, 0), feed_block, down_block],
        rows_out(near_rows) + part_shapes(near_rows, count, width),
        45.0,
        scratch=[((near_rows * count, width), BF)],
        limit=40,
        near=range(2, 2 * near_rows + 1),
        steps=near_rows,
        free=range(3),
    )
    back_parts = near_parts + far_parts
    back_addends = send(back_parts, "rep", rep_size)

    def sent_gradient(value):
        return lax.psum_scatter(value, "fsdp", scatter_dimension=0, tiled=True)

    def feed_gradient_kernel(
        hidden, far_hidden, back_all, three, far_three, both, far_both, out
    ):
        step_width, split = width // 3, near_rows * count
        for m in range(3):
            at = slice(m * step_width, (m + 1) * step_width)
            gradient = dot_lt(hidden[:, at], both[...]) + dot_lt(far_hidden[:, at], far_both[...])
            out[at, : 2 * block_ff] = gradient.astype(BF)
        together = max(1, fsdp_size // 2)
        for first in range(0, fsdp_size, together):
            at = slice(first * piece, (first + together) * piece)
            gradient = dot_lt(three[:, at], back_all[:split, :]) + dot_lt(
                far_three[:, at], back_all[split:, :]
            )
            gradient = gradient.astype(BF)
            for j in range(together):
                for a, lanes, c, packed_lanes in units:
                    to_row = (first + j) * shard_width + c
                    out[to_row : to_row + unit_rows, packed_lanes] = gradient[
                        j * piece + a : j * piece + a + unit_rows, lanes
                    ]

    (feed_gradient,) = call(
        order,
        feed_gradient_kernel,
        "feed_gradient",
        [],
        [wait_for(near_hidden, back_addends[near_rows:])]
        + [far_hidden, feed_back_all, near_three, far_three, near_both, far_both],
        [((width, 3 * block_ff), BF)],
        12.0,
        limit=36,
        near=range(7),
    )
    feed_sum = sent_gradient(feed_gradient)

    def middle_back_kernel(*refs):
        addends = refs[:rep_size]
        cotangent_ref, places, modulation, normed_ref, inverse_ref, branch_ref, weight = refs[
            rep_size : rep_size + 7
        ]
        middle_back, branch_back, sums_out, bias_out, heads_out, sums = refs[
            rep_size + 7 :
        ]
        sums[...] = jnp.zeros_like(sums)

        def step(here):
            slot_of = places[0, here, 0:1]
            upstream = addends[0][here, :]
            for ref in addends[1:]:
                upstream = upstream + ref[here, :].astype(F32)
            normed = normed_ref[here, :]
            masked = cotangent_ref[here, :].astype(F32) * places[0, here, 3:4]
            scale = pick(modulation, slot_of, 4 * width, width)
            back = masked + normalize_back(normed, inverse_ref[here, :], upstream * (1.0 + scale))
            middle_back[here, :] = back
            gate = pick(modulation, slot_of, 2 * width, width)
            low = (back * gate).astype(BF)
            branch_back[here, :] = low
            add_slots(sums, 0, slots, slot_of, back * branch_ref[here, :])
            add_slots(sums, slots, slots, slot_of, upstream)
            add_slots(sums, 2 * slots, slots, slot_of, upstream * normed)
            sums[3 * slots] += jnp.sum(low.astype(F32).reshape(CHUNK // 8, 8, width), axis=0)

        chunks(count, step, 1)
        total = jnp.sum(sums[...], axis=1)
        sums_out[...] = total[: 3 * slots]
        bias_out[...] = total[3 * slots :]
        heads = dot_rt(branch_back[...], weight[...])
        for k in range(rep_size):
            to, at = slice(k * group_tokens, (k + 1) * group_tokens), slice(k * block, (k + 1) * block)
            for g in range(rep_size):
                heads_out[to, g * block : (g + 1) * block] = heads[
                    g * group_tokens : (g + 1) * group_tokens, at
                ].astype(BF)

    middle_back, branch_back, middle_sums, output_bias_sum, sent_heads = call(
        order,
        middle_back_kernel,
        "second_norm_back",
        [],
        back_addends
        + [cotangent, place_columns, modulation, normed_two, inverse_two]
        + [branch, (qkv_block, (width, width))],
        [
            ((count, width), F32),
            ((count, width), BF),
            ((3 * slots, width), F32),
            ((1, width), F32),
            ((count, width), BF),
        ],
        150.0,
        scratch=[((3 * slots + 1, 8, width), F32)],
        limit=28,
        near=range(1, rep_size),
    )
    heads_back = exchange(sent_heads, "rep")

    def feed_out_kernel(three, far_three, down, *outs):
        for j in range(rep_size):
            source, k = (three, j) if j < near_rows else (far_three, j - near_rows)
            rows_here = slice(k * count, (k + 1) * count)
            outs[j][...] = dot(source[rows_here, :], down[...]).astype(outs[j].dtype)

    feed_parts = call(
        order,
        feed_out_kernel,
        "feed_out",
        [],
        [near_three, far_three, down_block],
        part_shapes(rep_size, count, width),
        5.0,
        limit=24,
        near=(0, 1),
    )
    feed_addends = send(list(feed_parts), "rep", rep_size)

    def attention_back_kernel(r_ref, *refs):
        heads, query_ref, key_ref, value_ref, wide, tables_ref = refs[:6]
        column_ref, row_ref, projected_back, bias_out = refs[6:10]
        parts_out, head_stack = refs[10:-1], refs[-1]
        if padded > block:
            head_stack[:, :, block:] = jnp.zeros((rep_size, count, padded - block), BF)
        for j in range(rep_size):
            owner = pl.ds(pl.multiple_of((r_ref[0] ^ j) * group_tokens, 16), group_tokens)
            for g in range(rep_size):
                head_stack[j, g * group_tokens : (g + 1) * group_tokens, :block] = heads[
                    owner, g * block : (g + 1) * block
                ]
        bias_out[...] = jnp.zeros_like(bias_out)

        def row(j, carry):
            here = pl.ds(pl.multiple_of(j * count, count), count)
            query, key, value, back = query_ref[j], key_ref[j], value_ref[j], head_stack[j]
            same = column_ref[j, :, 0:1] == row_ref[j, 0:1, :]
            query_back = jnp.zeros((count, padded), F32)
            key_back = jnp.zeros((count, padded), F32)
            value_back = jnp.zeros((count, padded), F32)
            for h in range(local_heads):
                mask = head_mask(h)
                query_head, back_head = query * mask, back * mask
                probs = probabilities(query_head, key, same)
                probs_back = dot_rt(back_head, value)
                scores_back = (
                    probs
                    * (probs_back - jnp.sum(probs * probs_back, axis=-1, keepdims=True))
                ).astype(BF)
                value_back = value_back + dot_lt(probs.astype(BF), back_head)
                query_back = query_back + dot(scores_back, key * mask)
                key_back = key_back + dot_lt(scores_back, query_head)
            cos_row, sin_row = rotary(tables_ref, column_ref[j])
            query_back = turn(query_back * score_scale, cos_row, sin_row, -1.0)
            key_back = turn(key_back * score_scale, cos_row, sin_row, -1.0)
            low = [value.astype(BF) for value in (query_back, key_back, value_back)]
            for t in range(3):
                projected_back[here, t * block : (t + 1) * block] = low[t][:, :block]
                bias_out[:, t * padded : (t + 1) * padded] += jnp.sum(
                    low[t].astype(F32), axis=0, keepdims=True
                )
            store_part(j, dot_rt(jnp.concatenate(low, axis=1), wide[...]), parts_out)
            return carry

        lax.fori_loop(0, rep_size, row, 0)

    projected_back, projection_bias_sum, *one_parts = call(
        order,
        attention_back_kernel,
        "attention_back",
        [r_index],
        [heads_back, query_all, key_all, value_all, wide_weight, tables]
        + [place_columns, place_rows],
        [((flat, 3 * block), BF), ((1, 3 * padded), F32)] + part_shapes(rep_size, count, width),
        90.0,
        scratch=[((rep_size, count, padded), BF)],
        limit=44,
        free=(0,),
    )
    one_addends = send(one_parts, "rep", rep_size)

    def attention_gradient_kernel(attended_ref, own_back, hidden_all, back, out):
        step_width = width // 3
        for m in range(3):
            at = slice(m * step_width, (m + 1) * step_width)
            out[at, :width] = dot_lt(attended_ref[:, at], own_back[...]).astype(BF)
            out[at, width:] = dot_lt(hidden_all[:, at], back[...]).astype(BF)

    (attention_gradient,) = call(
        order,
        attention_gradient_kernel,
        "attention_gradient",
        [],
        [wait_for(attended, feed_addends), branch_back, hidden_one_all, projected_back],
        [((width, width + 3 * block), BF)],
        6.4,
        limit=32,
        near=(3,),
    )
    attention_sum = sent_gradient(attention_gradient)

    def output_kernel(*refs):
        feeds = refs[:rep_size]
        tokens_ref, branch_ref, cotangent_ref, places, modulation = refs[rep_size : rep_size + 5]
        block_out, sums_out, sums = refs[rep_size + 5 :]
        sums[...] = jnp.zeros_like(sums)

        def step(here):
            slot_of = places[0, here, 0:1]
            feed = feeds[0][here, :]
            for ref in feeds[1:]:
                feed = feed + ref[here, :].astype(F32)
            gate_one = pick(modulation, slot_of, 2 * width, width)
            middle = tokens_ref[here, :].astype(F32) + gate_one * branch_ref[here, :]
            gate_two = pick(modulation, slot_of, 5 * width, width)
            block_out[here, :] = (middle + gate_two * feed).astype(BF)
            masked = cotangent_ref[here, :].astype(F32) * places[0, here, 3:4]
            add_slots(sums, 0, slots, slot_of, masked * feed)

        chunks(count, step, 1)
        sums_out[...] = jnp.sum(sums[...], axis=1)

    block_output, gate_two_sums = call(
        order,
        output_kernel,
        "layer_output",
        [],
        feed_addends + [tokens, branch, cotangent, place_columns, modulation],
        [((count, width), BF), ((slots, width), F32)],
        30.0,
        scratch=[((slots, 8, width), F32)],
        limit=16,
        near=range(1, rep_size),
    )

    def first_back_kernel(r_ref, *refs):
        addends = refs[:rep_size]
        tokens_ref, back_ref, modulation, places, middle_ref, gate_two_ref, bias, out_bias = refs[
            rep_size : rep_size + 8
        ]
        gradient, back_blocks, sums, whole, whole_bias, stack = refs[rep_size + 8 :]
        sums[...] = jnp.zeros_like(sums)

        def step(here):
            slot_of = places[0, here, 0:1]
            upstream = addends[0][here, :]
            for ref in addends[1:]:
                upstream = upstream + ref[here, :].astype(F32)
            normed, inverse = normalize_keep(tokens_ref[here, :].astype(F32))
            scale = pick(modulation, slot_of, width, width)
            gradient[here, :] = back_ref[here, :] + normalize_back(
                normed, inverse, upstream * (1.0 + scale)
            )
            add_slots(sums, 0, slots, slot_of, upstream)
            add_slots(sums, slots, slots, slot_of, upstream * normed)

        chunks(count, step)
        total = jnp.sum(sums[...], axis=1)
        whole[:, :width] = total[:slots]
        whole[:, width : 2 * width] = total[slots:]
        for t in range(3):
            at = slice((2 + t) * width, (3 + t) * width)
            whole[:, at] = middle_ref[t * slots : (t + 1) * slots, :]
        whole[:, 5 * width :] = gate_two_ref[...]
        whole_bias[...] = jnp.zeros_like(whole_bias)
        for k in range(rep_size):

            @pl.when(r_ref[0] == k)
            def _():
                for t in range(3):
                    first = t * width + k * block
                    whole_bias[:, first : first + block] = bias[:, t * padded : t * padded + block]

        stack[...] = jnp.zeros_like(stack)
        for k in range(fsdp_size):
            stack[k, :slots, :] = whole[:, k * columns : (k + 1) * columns]
            at = slice(k * shard_bias, (k + 1) * shard_bias)
            stack[k, slots : slots + 1, :shard_bias] = whole_bias[:, at]
            at = slice(k * shard_out_bias, (k + 1) * shard_out_bias)
            lanes = slice(shard_bias, shard_bias + shard_out_bias)
            stack[k, slots : slots + 1, lanes] = out_bias[:, at]
        back_blocks[...] = stack[...].reshape(fsdp_size * GROUP, columns).astype(BF)

    tokens_gradient, back_blocks = call(
        order,
        first_back_kernel,
        "first_norm_back",
        [r_index],
        one_addends
        + [tokens, middle_back, modulation, place_columns, middle_sums, gate_two_sums]
        + [projection_bias_sum, output_bias_sum],
        [((count, width), F32), ((fsdp_size * GROUP, columns), BF)],
        30.0,
        scratch=[
            ((2 * slots, 8, width), F32),
            ((slots, 6 * width), F32),
            ((1, 3 * width), F32),
            ((fsdp_size, GROUP, columns), F32),
        ],
        limit=20,
        near=range(1, rep_size),
    )

    line_backs = exchange(back_blocks, "fsdp")
    feed_sums = gather(wait_for(feed_sum, one_addends), "rep", rep_size)

    def conditioning_kernel(groups, activated_ref, weight, out, line_out):
        stack = groups[...].astype(F32)
        bias = jnp.sum(stack.reshape(fsdp_size, GROUP, columns), axis=0)[slots : slots + 1]
        row_ids = lax.broadcasted_iota(jnp.int32, (fsdp_size * GROUP, 1), 0)
        rows_back = jnp.where(lax.rem(row_ids, GROUP) < slots, stack, 0.0)
        line_out[:, :width] = activated_ref[...]
        line_out[:, width:] = jnp.where(row_ids == slots, bias, rows_back).astype(BF)
        result = dot(rows_back.astype(BF), weight[...])
        for k in range(fsdp_size):
            out[k * slots : (k + 1) * slots, :] = result[k * GROUP : k * GROUP + slots, :]

    activated_backs, line_back = call(
        order,
        conditioning_kernel,
        "conditioning_back",
        [],
        [wait_for(line_backs, feed_sums[1:3]), line_activated, modulation_weight.T],
        [((fsdp_size * slots, width), F32), ((fsdp_size * GROUP, width + columns), BF)],
        40.0,
        limit=24,
    )
    activated_backs = exchange(activated_backs, "fsdp")
    all_lines = gather(line_back, "rep", rep_size)

    def feed_blocks_kernel(r_ref, *refs):
        gate_out, up_out, down_out, stack = refs[rep_size:]
        for j in range(rep_size):
            stack[j] = refs[j][...].astype(F32)
        for k in range(rep_size):
            here = r_ref[0] ^ k
            for j in range(fsdp_size):
                target = slice(j * shard_ff + k * piece, j * shard_ff + (k + 1) * piece)
                first = block_ff + j * piece
                gate_out[:, target] = stack[here, :, j * piece : (j + 1) * piece]
                up_out[:, target] = stack[here, :, first : first + piece]
            for a, lanes, c, packed_lanes in units:
                to_row = k * piece + a
                down_out[to_row : to_row + unit_rows, lanes] = stack[
                    here, c : c + unit_rows, packed_lanes
                ]

    gate_gradient, up_gradient, down_gradient = call(
        order,
        feed_blocks_kernel,
        "feed_blocks",
        [r_index],
        feed_sums,
        [((shard_width, fsdp_size * shard_ff), F32)] * 2 + [((shard_ff, width), F32)],
        5.2,
        scratch=[((rep_size, shard_width, 3 * block_ff), F32)],
        limit=24,
        near=range(1, rep_size),
    )

    def table_kernel(*refs):
        lines, (condition, activated_back) = refs[:rep_size], refs[rep_size : rep_size + 2]
        table, table_bias, bias, out_bias, gradient, activated_stack, back_stack = refs[
            rep_size + 2 :
        ]
        upstream = jnp.sum(activated_back[...].reshape(fsdp_size, slots, width), axis=0)
        gradient[...] = upstream * silu_slope(condition[...].astype(F32))
        line = fsdp_size * GROUP
        total = jnp.zeros((1, columns), F32)
        for j in range(rep_size):
            back = lines[j][:, width:]
            activated_stack[j * line : (j + 1) * line, :] = lines[j][:, :width]
            back_stack[j * line : (j + 1) * line, :] = back
            total = total + back.astype(F32)[slots : slots + 1, :]
        bias[...] = total[:, :shard_bias]
        out_bias[...] = total[:, shard_bias : shard_bias + shard_out_bias]
        back = back_stack[...].astype(F32)
        in_group = lax.rem(lax.broadcasted_iota(jnp.int32, (rep_size * line, 1), 0), GROUP)
        table_bias[...] = jnp.sum(
            jnp.where(in_group < slots, back, 0.0), axis=0, keepdims=True
        )
        table[...] = dot_lt(back_stack[...], activated_stack[...])

    table_gradient, table_bias_gradient, bias_gradient, out_bias_gradient, activated_gradient = call(
        order,
        table_kernel,
        "table_gradient",
        [],
        all_lines + [conditioning[0], activated_backs],
        [((columns, width), F32), ((1, columns), F32)]
        + [((1, shard_bias), F32), ((1, shard_out_bias), F32), ((slots, width), F32)],
        4.0,
        scratch=[
            ((rep_size * fsdp_size * GROUP, width), BF),
            ((rep_size * fsdp_size * GROUP, columns), BF),
        ],
        limit=24,
        near=range(1, rep_size),
    )

    attention_late = wait_for(attention_sum, table_gradient)
    output_gradient = attention_late[:, :width].astype(F32)
    projection_sums = gather(attention_late[:, width:], "rep", rep_size)
    for bit in [1 << k for k in range(rep_size.bit_length() - 1)]:
        came = swap_with(output_gradient.astype(BF), "rep", rep_size, bit)
        came = wait_for(came, projection_sums[2 % rep_size]) if bit == 1 else came
        output_gradient = output_gradient + came.astype(F32)

    def projection_blocks_kernel(r_ref, *refs):
        out, stack = refs[rep_size:]
        for j in range(rep_size):
            stack[j] = refs[j][...].astype(F32)
        for k in range(rep_size):
            here = r_ref[0] ^ k
            for t in range(3):
                first = t * width + k * block
                out[:, first : first + block] = stack[here, :, t * block : (t + 1) * block]

    (projection_gradient,) = call(
        order,
        projection_blocks_kernel,
        "projection_blocks",
        [r_index],
        projection_sums,
        [((shard_width, 3 * width), F32)],
        3.0,
        scratch=[((rep_size, shard_width, 3 * block), F32)],
        limit=24,
        near=range(1, rep_size),
    )
    return (
        block_output[None],
        tokens_gradient[None],
        activated_gradient[None],
        table_gradient.T,
        table_bias_gradient[0],
        projection_gradient,
        bias_gradient[0],
        output_gradient,
        out_bias_gradient[0],
        gate_gradient,
        up_gradient,
        down_gradient,
    )


def solution(mesh):
    sizes = dict(mesh.shape)

    def body(*arrays):
        return on_device(sizes["rep"], sizes["fsdp"], *arrays)

    rows = ("rep", "fsdp")
    in_specs = (
        P(rows, None, None),
        P(rows, None, None),
        P(rows, None),
        P(rows, None),
        P(rows, None),
        P(rows, None),
        P(None, "fsdp"),
        P("fsdp"),
        P("fsdp", None),
        P("fsdp"),
        P("fsdp", None),
        P("fsdp"),
        P("fsdp", None),
        P("fsdp", None),
        P("fsdp", None),
        P(rows, None, None),
    )
    out_specs = (
        P(rows, None, None),
        P(rows, None, None),
        P(rows, None, None),
        P(None, "fsdp"),
        P("fsdp"),
        P("fsdp", None),
        P("fsdp"),
        P("fsdp", None),
        P("fsdp"),
        P("fsdp", None),
        P("fsdp", None),
        P("fsdp", None),
    )
    return jax.shard_map(
        body, mesh=mesh, in_specs=in_specs, out_specs=out_specs, check_vma=False
    )
```

```python
import math

import jax
import jax.numpy as jnp
import numpy as np
from jax import lax
from jax.experimental import pallas as pl
from jax.experimental.pallas import tpu as pltpu
from jax.sharding import PartitionSpec as P

HEADS = 16
BF = jnp.bfloat16
F32 = jnp.float32
LANES = 128
CHUNK = 32
GROUP = 8


def wait_for(value, *others):
    return lax.optimization_barrier((value, others))[0]


def swap_with(value, axis, size, bit):
    return lax.ppermute(value, axis, [(i, i ^ bit) for i in range(size)])


def gather(value, axis, size):
    return [value] + [swap_with(value, axis, size, j) for j in range(1, size)]


def halves_gather(top, low, axis, size):
    if size != 4:
        return list(zip(gather(top, axis, size), gather(low, axis, size), strict=True))
    top_one, low_two = swap_with(top, axis, size, 1), swap_with(low, axis, size, 2)
    top_three, low_three = swap_with(top_one, axis, size, 2), swap_with(low_two, axis, size, 1)
    low_one, top_two = swap_with(low, axis, size, 1), swap_with(top, axis, size, 2)
    return [(top, low), (top_one, low_one), (top_two, low_two), (top_three, low_three)]


def send(values, axis, size):
    return [values[0]] + [swap_with(values[j], axis, size, j) for j in range(1, size)]


def exchange(value, axis):
    return lax.all_to_all(value, axis, 0, 0, tiled=True)


def block_of(shape, by_step, offset=0):
    if by_step:
        return pl.BlockSpec(shape, lambda i: (i + offset,) + (0,) * (len(shape) - 1))
    zeros = (0,) * len(shape)
    return pl.BlockSpec(shape, lambda i: zeros, pipeline_mode=pl.Buffered(1))


def call(order, body, name, scalars, arrays, outs, micros, scratch=(), limit=48, near=(), steps=1, free=()):
    shapes = [
        jax.ShapeDtypeStruct(*out[:2]) if n in free else pltpu.HBM(*out[:2])
        for n, out in enumerate(outs)
    ]
    out_specs = [block_of(out[-1], True) if len(out) > 2 else block_of(out[0], False) for out in outs]
    in_specs = [
        block_of(array[1], len(array) > 2, *array[3:])
        if isinstance(array, tuple)
        else block_of(array.shape, False)
        for array in arrays
    ]
    arrays = [array[0] if isinstance(array, tuple) else array for array in arrays]
    if order:
        first, _ = lax.optimization_barrier((arrays[0], order.pop()))
        arrays = [first] + list(arrays[1:])
    arrays = [
        array if n in near else pltpu.with_memory_space_constraint(array, pltpu.HBM)
        for n, array in enumerate(arrays)
    ]
    results = pl.pallas_call(
        body,
        name=name,
        grid=(steps,),
        out_shape=shapes,
        in_specs=[pl.BlockSpec(memory_space=pltpu.SMEM)] * len(scalars)
        + in_specs,
        out_specs=out_specs,
        scratch_shapes=[pltpu.VMEM(shape, dtype) for shape, dtype in scratch],
        compiler_params=pltpu.CompilerParams(vmem_limit_bytes=limit << 20),
        cost_estimate=pl.CostEstimate(
            flops=int(micros * 1.000e+09), bytes_accessed=int(micros * 3.000e+06), transcendentals=0
        ),
    )(*scalars, *arrays)
    order.append(results[0])
    return results


def part_shapes(size, tokens, width):
    return [((tokens, width), F32)] + [((tokens, width), BF)] * (size - 1)


def store_part(j, value, refs):
    for k, ref in enumerate(refs):

        @pl.when(j == k)
        def _(ref=ref):
            ref[...] = value.astype(ref.dtype)


def dot(left, right):
    return jnp.dot(left, right, preferred_element_type=F32)


def dot_rt(left, right):
    return lax.dot_general(left, right, (((1,), (1,)), ((), ())), preferred_element_type=F32)


def dot_lt(left, right):
    return lax.dot_general(left, right, (((0,), (0,)), ((), ())), preferred_element_type=F32)


def pick(modulation, slot_of, first, width):
    total = jnp.zeros((slot_of.shape[0], width), F32)
    for k in range(modulation.shape[0]):
        total = jnp.where(slot_of == k, modulation[k : k + 1, first : first + width], total)
    return total


def normalize_keep(values):
    centered = values - jnp.mean(values, axis=-1, keepdims=True)
    variance = jnp.mean(centered * centered, axis=-1, keepdims=True)
    inverse = lax.rsqrt(variance + 1e-06)
    return centered * inverse, inverse


def normalize_back(normed, inverse, upstream):
    return inverse * (
        upstream
        - jnp.mean(upstream, axis=-1, keepdims=True)
        - normed * jnp.mean(upstream * normed, axis=-1, keepdims=True)
    )


def add_slots(sums, base, count, slot_of, values):
    rows, width = values.shape
    for k in range(count):
        chosen = jnp.where(slot_of == k, values, 0.0)
        sums[base + k] += jnp.sum(chosen.reshape(rows // 8, 8, width), axis=0)


def chunks(tokens, step, unroll=2):
    def body(i, carry):
        step(pl.ds(pl.multiple_of(i * CHUNK, CHUNK), CHUNK))
        return carry

    lax.fori_loop(0, tokens // CHUNK, body, 0, unroll=unroll)


def silu_slope(values):
    sigmoid = jax.nn.sigmoid(values)
    return sigmoid * (1.0 + values * (1.0 - sigmoid))


def on_device(
    rep_size,
    fsdp_size,
    tokens,
    conditioning,
    segment_ids,
    heights,
    widths,
    pad_mask,
    modulation_weight,
    modulation_bias,
    projection_weight,
    projection_bias,
    output_weight,
    output_bias,
    gate_weight,
    up_weight,
    down_weight,
    cotangent,
):
    rows, count, width = tokens.shape
    assert rows == 1
    slots = conditioning.shape[1]
    head_width = width // HEADS
    local_heads = HEADS // rep_size
    block = width // rep_size
    padded = -(-block // LANES) * LANES
    score_scale = 1.0 / math.sqrt(head_width)
    shard_ff = down_weight.shape[0]
    piece = shard_ff // rep_size
    block_ff = fsdp_size * piece
    shard_width = projection_weight.shape[0]
    columns = modulation_weight.shape[1]
    flat = rep_size * count
    half = count // 2
    group_tokens = count // rep_size
    others = rep_size - 1
    r = lax.axis_index("rep")
    r_index = r.reshape(1).astype(jnp.int32)
    tokens, cotangent = tokens[0], cotangent[0]
    order = []

    def qkv_shard_kernel(r_ref, projection, output, out):
        out[:, :width] = output[...]
        for k in range(rep_size):

            @pl.when(r_ref[0] == k)
            def _():
                for t in range(3):
                    first, to = t * width + k * block, width + t * block
                    out[:, to : to + block] = projection[:, first : first + block]

    (qkv_shard,) = call(
        order,
        qkv_shard_kernel,
        "qkv_shard",
        [r_index],
        [projection_weight, output_weight],
        [((shard_width, width + 3 * block), BF)],
        4.5,
        limit=16,
    )

    slot_ids = jnp.arange(slots, dtype=jnp.int32)
    member_ints = (segment_ids[:, :, None] == slot_ids).astype(jnp.int32)
    before_ints = (slot_ids < segment_ids[:, :, None]).astype(jnp.int32)
    starts = jnp.sum(before_ints * (heights * widths)[:, None, :], axis=2)
    offsets = jnp.arange(count, dtype=jnp.int32)[None, :] - starts
    row_width = jnp.sum(member_ints * widths[:, None, :], axis=2)
    places = jnp.concatenate(
        [segment_ids, offsets // row_width, offsets % row_width, pad_mask], axis=1
    ).astype(BF)
    places = jnp.pad(places, ((0, GROUP - 1), (0, width - 4 * count)))
    token_rows = gather(jnp.concatenate([tokens, places], axis=0), "rep", rep_size)

    cond_float = conditioning.astype(F32)
    activated = jax.nn.silu(cond_float).astype(BF).reshape(slots, width)
    shard_bias, shard_out_bias = projection_bias.shape[0], output_bias.shape[0]
    bias_row = jnp.pad(
        jnp.concatenate([projection_bias, output_bias]), (0, width - shard_bias - shard_out_bias)
    )[None]
    group_rows = jnp.concatenate(
        [activated, bias_row, jnp.zeros((GROUP - slots - 1, width), BF)], axis=0
    )
    line_rows = lax.all_gather(group_rows, "fsdp", axis=0, tiled=True)

    def modulate_kernel(r_ref, *refs):
        groups, weight, bias = refs[:3]
        out, activated_out, bias_out, out_bias, stack, whole = refs[3:]
        stack[...] = groups[...].astype(F32).reshape(fsdp_size, GROUP, width)
        in_group = lax.rem(lax.broadcasted_iota(jnp.int32, (fsdp_size * GROUP, 1), 0), GROUP)
        rows_low = jnp.where(in_group < slots, groups[...].astype(F32), 0.0).astype(BF)
        activated_out[...] = rows_low
        out[...] = dot_rt(rows_low, weight[...]) + bias[...]
        for k in range(fsdp_size):
            row = stack[k, slots : slots + 1, :]
            whole[:, k * shard_bias : (k + 1) * shard_bias] = row[:, :shard_bias]
            at = slice(k * shard_out_bias, (k + 1) * shard_out_bias)
            out_bias[:, at] = row[:, shard_bias : shard_bias + shard_out_bias]
        bias_out[...] = jnp.zeros_like(bias_out)
        for k in range(rep_size):

            @pl.when(r_ref[0] == k)
            def _():
                for t in range(3):
                    first = t * width + k * block
                    bias_out[:, t * padded : t * padded + block] = whole[:, first : first + block]

    line_modulation, line_activated, own_bias, output_bias_all = call(
        order,
        modulate_kernel,
        "modulate",
        [r_index],
        [line_rows, modulation_weight.T, modulation_bias.astype(F32)[None]],
        [
            ((fsdp_size * GROUP, columns), F32),
            ((fsdp_size * GROUP, width), BF),
            ((1, 3 * padded), F32),
            ((1, width), F32),
        ],
        6.0,
        scratch=[((fsdp_size, GROUP, width), F32), ((1, 3 * width), F32)],
        limit=24,
    )
    own_modulation = lax.all_to_all(line_modulation, "fsdp", 0, 0, tiled=True)

    unit_rows, unit_lanes = math.gcd(piece, shard_width), math.gcd(width, block_ff)
    units = []
    for u in range((piece // unit_rows) * (width // unit_lanes)):
        (a, b), (c, d) = divmod(u, width // unit_lanes), divmod(u, block_ff // unit_lanes)
        units.append(
            (
                a * unit_rows,
                slice(b * unit_lanes, (b + 1) * unit_lanes),
                c * unit_rows,
                slice(2 * block_ff + d * unit_lanes, 2 * block_ff + (d + 1) * unit_lanes),
            )
        )

    def feed_shard_kernel(r_ref, gate, up, down, out):
        for k in range(rep_size):

            @pl.when(r_ref[0] == k)
            def _():
                for j in range(fsdp_size):
                    source = slice(j * shard_ff + k * piece, j * shard_ff + (k + 1) * piece)
                    out[:, j * piece : (j + 1) * piece] = gate[:, source]
                    first = block_ff + j * piece
                    out[:, first : first + piece] = up[:, source]
                for a, lanes, c, packed_lanes in units:
                    out[c : c + unit_rows, packed_lanes] = down[
                        k * piece + a : k * piece + a + unit_rows, lanes
                    ]

    (feed_shard,) = call(
        order,
        feed_shard_kernel,
        "feed_shard",
        [r_index],
        [gate_weight, up_weight, down_weight],
        [((shard_width, 3 * block_ff), BF)],
        4.5,
        limit=16,
    )
    qkv_block = lax.all_gather(qkv_shard, "fsdp", axis=0, tiled=True)
    feed_block = lax.all_gather(feed_shard, "fsdp", axis=0, tiled=True)

    def norm_rows_kernel(*refs):
        out, columns_out, rows_out = refs[rep_size:]
        for j in range(rep_size):
            ref = refs[j]

            def step(at, ref=ref, j=j):
                normed, _ = normalize_keep(ref[at, :].astype(F32))
                out[pl.ds(j * count + at.start, CHUNK), :] = normed

            chunks(count, step)
            line = ref[count:, :].astype(F32)
            for q in range(4):
                rows_out[j, q : q + 1, :] = line[:1, q * count : (q + 1) * count]
            rows_out[j, 4:, :] = jnp.zeros((4, count), F32)
            columns_out[j] = rows_out[j].T

    normed_rows, place_columns, place_rows = call(
        order,
        norm_rows_kernel,
        "first_norm",
        [],
        token_rows,
        [((flat, width), F32), ((rep_size, count, 8), F32), ((rep_size, 8, count), F32)],
        18.0,
        limit=24,
        near=range(1, rep_size),
        free=(0,),
    )
    pair_count = head_width // 4
    most_rows, most_columns = count // 4, 32
    lane = np.arange(padded)
    in_head = lane % head_width
    lane_frequency = 10000.0 ** (-(in_head % pair_count) / pair_count)
    of_row = (lane < block) & (in_head < 2 * pair_count)
    of_column = (lane < block) & (in_head >= 2 * pair_count)
    sign = np.where((in_head // pair_count) % 2 == 1, 1.0, -1.0)
    row_angle = np.arange(most_rows)[:, None] * lane_frequency
    column_angle = np.arange(most_columns)[:, None] * lane_frequency
    tables = np.concatenate(
        [
            np.concatenate(
                [
                    np.where(of_row, np.cos(row_angle), 0.0),
                    np.where(of_column, np.cos(column_angle), 0.0),
                ]
            ),
            np.concatenate(
                [
                    np.where(of_row, sign * np.sin(row_angle), 0.0),
                    np.where(of_column, sign * np.sin(column_angle), 0.0),
                ]
            ),
        ],
        axis=1,
    ).astype(np.float32)
    pieces, left = [], tables
    for _ in range(3):
        pieces.append(left.astype(jnp.bfloat16))
        left = left - pieces[-1].astype(np.float32)
    tables = jnp.asarray(np.stack(pieces))

    def rotary(tables_ref, places):
        numbers = lax.broadcasted_iota(jnp.int32, (count, most_rows + most_columns), 1).astype(F32)
        is_row = (numbers < most_rows) & (numbers == places[:, 1:2])
        is_column = (numbers >= most_rows) & (numbers - most_rows == places[:, 2:3])
        chosen = jnp.where(is_row | is_column, 1.0, 0.0).astype(BF)
        both = dot(chosen, tables_ref[2]) + dot(chosen, tables_ref[1]) + dot(chosen, tables_ref[0])
        return both[:, :padded], both[:, padded:]

    def modulation_kernel(arrived, modulation, sent):
        for k in range(fsdp_size):
            at = slice(k * columns, (k + 1) * columns)
            modulation[:, at] = arrived[k * GROUP : k * GROUP + slots, :]
        sent[:, : 2 * width] = modulation[:, : 2 * width]
        sent[:, 2 * width :] = modulation[:, 5 * width :]

    modulation, sent_modulation = call(
        order,
        modulation_kernel,
        "modulation",
        [],
        [wait_for(own_modulation, normed_rows)],
        [((slots, 6 * width), F32), ((slots, 3 * width), F32)],
        3.0,
        limit=8,
    )
    modulation_rows = gather(sent_modulation, "rep", rep_size)
    cotangent_rows = gather(wait_for(cotangent, modulation_rows), "rep", rep_size)

    def head_mask(h):
        lanes = lax.broadcasted_iota(jnp.int32, (1, padded), 1)
        inside = (lanes >= h * head_width) & (lanes < (h + 1) * head_width)
        return jnp.where(inside, 1.0, 0.0).astype(BF)

    def probabilities(query_head, key, same):
        scores = jnp.where(same, dot_rt(query_head, key) * score_scale, -1e30)
        exponent = jnp.exp(scores - jnp.max(scores, axis=-1, keepdims=True))
        return exponent / jnp.sum(exponent, axis=-1, keepdims=True)

    def turn(values, cosine_row, sine_row, sense):
        before = pltpu.roll(values, pair_count, 1)
        after = pltpu.roll(values, padded - pair_count, 1)
        lanes = lax.broadcasted_iota(jnp.int32, (1, padded), 1)
        second = lax.rem(lanes, 2 * pair_count) >= pair_count
        return values * cosine_row + jnp.where(second, before, after) * (sense * sine_row)

    def attention_kernel(r_ref, *refs):
        modulations = refs[:rep_size]
        normed, weight, bias, tables_ref, column_ref, row_ref = refs[rep_size : rep_size + 6]
        hidden_all, wide, query_out, key_out, value_out, attended_out, modulation_stack = refs[
            rep_size + 6 :
        ]
        for j in range(rep_size):
            modulation_stack[j] = modulations[j][:, : 2 * width]
        for t in range(3):
            first = width + t * block
            wide[:, t * padded : t * padded + block] = weight[:, first : first + block]
            if padded > block:
                wide[:, t * padded + block : (t + 1) * padded] = jnp.zeros(
                    (width, padded - block), BF
                )

        def row(j, carry):
            first = pl.multiple_of(j * count, count)

            def step(at):
                here = pl.ds(pl.multiple_of(first + at.start, CHUNK), CHUNK)
                slot_of = column_ref[j, at, 0:1]
                scale = pick(modulation_stack[j], slot_of, width, width)
                shift = pick(modulation_stack[j], slot_of, 0, width)
                hidden_all[here, :] = (normed[here, :] * (1.0 + scale) + shift).astype(BF)

            chunks(count, step)
            projected = dot(hidden_all[pl.ds(first, count), :], wide[...]) + bias[...]
            cos_row, sin_row = rotary(tables_ref, column_ref[j])
            query = turn(projected[:, :padded], cos_row, sin_row, 1.0).astype(BF)
            key = turn(projected[:, padded : 2 * padded], cos_row, sin_row, 1.0).astype(BF)
            value = projected[:, 2 * padded :].astype(BF)
            query_out[j], key_out[j], value_out[j] = query, key, value
            same = column_ref[j, :, 0:1] == row_ref[j, 0:1, :]
            total = jnp.zeros((count, padded), F32)
            for h in range(local_heads):
                mask = head_mask(h)
                probs = probabilities(query * mask, key, same)
                total = total + dot(probs.astype(BF), value * mask)
            owner = pl.ds(pl.multiple_of((r_ref[0] ^ j) * group_tokens, 16), group_tokens)
            low = total[:, :block].astype(BF)
            for g in range(rep_size):
                attended_out[owner, g * block : (g + 1) * block] = low[
                    g * group_tokens : (g + 1) * group_tokens, :
                ]
            return carry

        lax.fori_loop(0, rep_size, row, 0)

    hidden_one_all, wide_weight, query_all, key_all, value_all, attended_heads = call(
        order,
        attention_kernel,
        "attention",
        [r_index],
        modulation_rows
        + [normed_rows, qkv_block, own_bias, tables, place_columns, place_rows],
        [((flat, width), BF), ((width, 3 * padded), BF)]
        + [((rep_size, count, padded), BF)] * 3
        + [((count, width), BF)],
        66.0,
        scratch=[((rep_size, slots, 2 * width), F32)],
        limit=44,
        near=range(1, rep_size + 1),
    )
    own_heads = exchange(attended_heads, "rep")

    def feed_back_kernel(*refs):
        cotangents, modulations = refs[:rep_size], refs[rep_size : 2 * rep_size]
        columns_ref, out = refs[2 * rep_size :]
        for j in range(rep_size):

            def step(at, j=j):
                masked = cotangents[j][at, :].astype(F32) * columns_ref[j, at, 3:4]
                gate = pick(modulations[j], columns_ref[j, at, 0:1], 2 * width, width)
                out[pl.ds(j * count + at.start, CHUNK), :] = (gate * masked).astype(BF)

            chunks(count, step)

    (feed_back_all,) = call(
        order,
        feed_back_kernel,
        "feed_back",
        [],
        cotangent_rows + modulation_rows + [place_columns],
        [((flat, width), BF)],
        12.0,
        limit=24,
        near=(*range(1, rep_size), *range(rep_size + 1, 2 * rep_size)),
        free=(0,),
    )

    def middle_kernel(
        heads, weight, bias, tokens_ref, modulation, places, branch, normed_out, inverse_out,
        top, low, attended,
    ):
        for k in range(rep_size):
            for g in range(rep_size):
                attended[
                    g * group_tokens : (g + 1) * group_tokens, k * block : (k + 1) * block
                ] = heads[k * group_tokens : (k + 1) * group_tokens, g * block : (g + 1) * block]
        branch[...] = dot(attended[...], weight[...]) + bias[...]

        for p, hidden in enumerate((top, low)):

            def step(at, p=p, hidden=hidden):
                here = pl.ds(p * half + at.start, CHUNK)
                slot_of = places[0, here, 0:1]
                gate = pick(modulation, slot_of, 2 * width, width)
                middle = tokens_ref[here, :].astype(F32) + gate * branch[here, :]
                normed, inverse = normalize_keep(middle)
                normed_out[here, :] = normed
                inverse_out[here, :] = inverse
                scale = pick(modulation, slot_of, 4 * width, width)
                hidden[at, :] = (
                    normed * (1.0 + scale) + pick(modulation, slot_of, 3 * width, width)
                ).astype(BF)

            chunks(half, step)

    branch, normed_two, inverse_two, hidden_top, hidden_low, attended = call(
        order,
        middle_kernel,
        "second_norm",
        [],
        [own_heads, (qkv_block, (width, width)), output_bias_all, tokens, modulation, place_columns],
        [((count, width), F32), ((count, width), F32), ((count, 1), F32)]
        + [((half, width), BF)] * 2
        + [((count, width), BF)],
        21.0,
        limit=24,
    )
    hidden_two_rows = halves_gather(hidden_top, hidden_low, "rep", rep_size)
    hidden_two_rows = [piece for row in hidden_two_rows for piece in row]


    step_ff = 256 if block_ff % 256 == 0 else 128
    taken = count

    def feed_kernel(unpack, rows_here, *refs):
        back, weight = refs[2 * rows_here : 2 * rows_here + 2]
        refs_here = refs[2 * rows_here + 2 :]
        if unpack:
            hidden_out, three, both_back, down = refs_here[:4]
        else:
            down, hidden_out, three, both_back = refs_here[:4]
        parts_out, hidden_all = refs_here[4:-1], refs_here[-1]
        j = pl.program_id(0)

        @pl.when(j == 0)
        def _():
            for n in range(2 * rows_here):
                hidden_all[n * half : (n + 1) * half, :] = refs[n][...]
            if not unpack:
                return
            for k in range(fsdp_size):
                for a, lanes, c, packed_lanes in units:
                    from_row, to_row = k * shard_width + c, k * piece + a
                    down[to_row : to_row + unit_rows, lanes] = weight[
                        from_row : from_row + unit_rows, packed_lanes
                    ]

        hidden = hidden_all[pl.ds(pl.multiple_of(j * count, count), count), :]
        hidden_out[...] = hidden
        for c in range(block_ff // step_ff):
            at = slice(c * step_ff, (c + 1) * step_ff)
            up_at = slice(block_ff + c * step_ff, block_ff + (c + 1) * step_ff)
            gate = dot(hidden, weight[:, at])
            up = dot(hidden, weight[:, up_at])
            hidden_back = dot_rt(back[...], down[at, :])
            sigmoid = jax.nn.sigmoid(gate)
            silu = gate * sigmoid
            three[:, at] = (silu * up).astype(BF)
            slope = sigmoid * (1.0 + gate * (1.0 - sigmoid))
            both_back[:, at] = (hidden_back * up * slope).astype(BF)
            both_back[:, up_at] = (hidden_back * silu).astype(BF)
        store_part(j, dot_rt(both_back[...], weight[:, : 2 * block_ff]), parts_out)

    near_rows = rep_size - 1
    far_rows = rep_size - near_rows
    row_outs = [((width,), BF), ((block_ff,), BF), ((2 * block_ff,), BF)]

    def rows_out(row_count):
        return [((row_count * count,) + w, d, (count,) + w) for w, d in row_outs]

    far_hidden, far_three, far_both, down_block, *far_parts = call(
        order,
        lambda *refs: feed_kernel(True, far_rows, *refs),
        "feed_far",
        [],
        hidden_two_rows[2 * near_rows :]
        + [(feed_back_all, (count, width), True, near_rows), feed_block],
        rows_out(far_rows) + [((block_ff, width), BF)] + [((count, width), BF)] * far_rows,
        15.0,
        scratch=[((far_rows * count, width), BF)],
        limit=40,
        near=range(2 * far_rows + 1),
        steps=far_rows,
        free=range(3),
    )
    near_hidden, near_three, near_both, *near_parts = call(
        order,
        lambda *refs: feed_kernel(False, near_rows, *refs),
        "feed_near",
        [],
        hidden_two_rows[: 2 * near_rows]
        + [(feed_back_all, (count, width), True, 0), feed_block, down_block],
        rows_out(near_rows) + part_shapes(near_rows, count, width),
        45.0,
        scratch=[((near_rows * count, width), BF)],
        limit=40,
        near=range(2, 2 * near_rows + 1),
        steps=near_rows,
        free=range(3),
    )
    back_parts = near_parts + far_parts
    back_addends = send(back_parts, "rep", rep_size)

    def sent_gradient(value):
        return lax.psum_scatter(value, "fsdp", scatter_dimension=0, tiled=True)

    def feed_gradient_kernel(
        hidden, far_hidden, back_all, three, far_three, both, far_both, out
    ):
        step_width, split = width // 3, near_rows * count
        for m in range(3):
            at = slice(m * step_width, (m + 1) * step_width)
            gradient = dot_lt(hidden[:, at], both[...]) + dot_lt(far_hidden[:, at], far_both[...])
            out[at, : 2 * block_ff] = gradient.astype(BF)
        together = max(1, fsdp_size // 2)
        for first in range(0, fsdp_size, together):
            at = slice(first * piece, (first + together) * piece)
            gradient = dot_lt(three[:, at], back_all[:split, :]) + dot_lt(
                far_three[:, at], back_all[split:, :]
            )
            gradient = gradient.astype(BF)
            for j in range(together):
                for a, lanes, c, packed_lanes in units:
                    to_row = (first + j) * shard_width + c
                    out[to_row : to_row + unit_rows, packed_lanes] = gradient[
                        j * piece + a : j * piece + a + unit_rows, lanes
                    ]

    (feed_gradient,) = call(
        order,
        feed_gradient_kernel,
        "feed_gradient",
        [],
        [wait_for(near_hidden, back_addends[near_rows:])]
        + [far_hidden, feed_back_all, near_three, far_three, near_both, far_both],
        [((width, 3 * block_ff), BF)],
        12.0,
        limit=36,
        near=range(7),
    )
    feed_sum = sent_gradient(feed_gradient)

    def middle_back_kernel(*refs):
        addends = refs[:rep_size]
        cotangent_ref, places, modulation, normed_ref, inverse_ref, branch_ref, weight = refs[
            rep_size : rep_size + 7
        ]
        middle_back, branch_back, sums_out, bias_out, heads_out, sums = refs[
            rep_size + 7 :
        ]
        sums[...] = jnp.zeros_like(sums)

        def step(here):
            slot_of = places[0, here, 0:1]
            upstream = addends[0][here, :]
            for ref in addends[1:]:
                upstream = upstream + ref[here, :].astype(F32)
            normed = normed_ref[here, :]
            masked = cotangent_ref[here, :].astype(F32) * places[0, here, 3:4]
            scale = pick(modulation, slot_of, 4 * width, width)
            back = masked + normalize_back(normed, inverse_ref[here, :], upstream * (1.0 + scale))
            middle_back[here, :] = back
            gate = pick(modulation, slot_of, 2 * width, width)
            low = (back * gate).astype(BF)
            branch_back[here, :] = low
            add_slots(sums, 0, slots, slot_of, back * branch_ref[here, :])
            add_slots(sums, slots, slots, slot_of, upstream)
            add_slots(sums, 2 * slots, slots, slot_of, upstream * normed)
            sums[3 * slots] += jnp.sum(low.astype(F32).reshape(CHUNK // 8, 8, width), axis=0)

        chunks(count, step, 1)
        total = jnp.sum(sums[...], axis=1)
        sums_out[...] = total[: 3 * slots]
        bias_out[...] = total[3 * slots :]
        heads = dot_rt(branch_back[...], weight[...])
        for k in range(rep_size):
            to, at = slice(k * group_tokens, (k + 1) * group_tokens), slice(k * block, (k + 1) * block)
            for g in range(rep_size):
                heads_out[to, g * block : (g + 1) * block] = heads[
                    g * group_tokens : (g + 1) * group_tokens, at
                ].astype(BF)

    middle_back, branch_back, middle_sums, output_bias_sum, sent_heads = call(
        order,
        middle_back_kernel,
        "second_norm_back",
        [],
        back_addends
        + [cotangent, place_columns, modulation, normed_two, inverse_two]
        + [branch, (qkv_block, (width, width))],
        [
            ((count, width), F32),
            ((count, width), BF),
            ((3 * slots, width), F32),
            ((1, width), F32),
            ((count, width), BF),
        ],
        150.0,
        scratch=[((3 * slots + 1, 8, width), F32)],
        limit=28,
        near=range(1, rep_size),
        free=(1,),
    )
    heads_back = exchange(sent_heads, "rep")

    def feed_out_kernel(three, far_three, down, *outs):
        for j in range(rep_size):
            source, k = (three, j) if j < near_rows else (far_three, j - near_rows)
            rows_here = slice(k * count, (k + 1) * count)
            outs[j][...] = dot(source[rows_here, :], down[...]).astype(outs[j].dtype)

    feed_parts = call(
        order,
        feed_out_kernel,
        "feed_out",
        [],
        [near_three, far_three, down_block],
        part_shapes(rep_size, count, width),
        5.0,
        limit=24,
        near=(0, 1),
    )
    feed_addends = send(list(feed_parts), "rep", rep_size)

    def attention_back_kernel(r_ref, *refs):
        heads, query_ref, key_ref, value_ref, wide, tables_ref = refs[:6]
        column_ref, row_ref, projected_back, bias_out = refs[6:10]
        parts_out, head_stack = refs[10:-1], refs[-1]
        if padded > block:
            head_stack[:, :, block:] = jnp.zeros((rep_size, count, padded - block), BF)
        for j in range(rep_size):
            owner = pl.ds(pl.multiple_of((r_ref[0] ^ j) * group_tokens, 16), group_tokens)
            for g in range(rep_size):
                head_stack[j, g * group_tokens : (g + 1) * group_tokens, :block] = heads[
                    owner, g * block : (g + 1) * block
                ]
        bias_out[...] = jnp.zeros_like(bias_out)

        def row(j, carry):
            here = pl.ds(pl.multiple_of(j * count, count), count)
            query, key, value, back = query_ref[j], key_ref[j], value_ref[j], head_stack[j]
            same = column_ref[j, :, 0:1] == row_ref[j, 0:1, :]
            query_back = jnp.zeros((count, padded), F32)
            key_back = jnp.zeros((count, padded), F32)
            value_back = jnp.zeros((count, padded), F32)
            for h in range(local_heads):
                mask = head_mask(h)
                query_head, back_head = query * mask, back * mask
                probs = probabilities(query_head, key, same)
                probs_back = dot_rt(back_head, value)
                scores_back = (
                    probs
                    * (probs_back - jnp.sum(probs * probs_back, axis=-1, keepdims=True))
                ).astype(BF)
                value_back = value_back + dot_lt(probs.astype(BF), back_head)
                query_back = query_back + dot(scores_back, key * mask)
                key_back = key_back + dot_lt(scores_back, query_head)
            cos_row, sin_row = rotary(tables_ref, column_ref[j])
            query_back = turn(query_back * score_scale, cos_row, sin_row, -1.0)
            key_back = turn(key_back * score_scale, cos_row, sin_row, -1.0)
            low = [value.astype(BF) for value in (query_back, key_back, value_back)]
            for t in range(3):
                projected_back[here, t * block : (t + 1) * block] = low[t][:, :block]
                bias_out[:, t * padded : (t + 1) * padded] += jnp.sum(
                    low[t].astype(F32), axis=0, keepdims=True
                )
            store_part(j, dot_rt(jnp.concatenate(low, axis=1), wide[...]), parts_out)
            return carry

        lax.fori_loop(0, rep_size, row, 0)

    projected_back, projection_bias_sum, *one_parts = call(
        order,
        attention_back_kernel,
        "attention_back",
        [r_index],
        [heads_back, query_all, key_all, value_all, wide_weight, tables]
        + [place_columns, place_rows],
        [((flat, 3 * block), BF), ((1, 3 * padded), F32)] + part_shapes(rep_size, count, width),
        90.0,
        scratch=[((rep_size, count, padded), BF)],
        limit=44,
        free=(0,),
    )
    one_addends = send(one_parts, "rep", rep_size)

    def attention_gradient_kernel(attended_ref, own_back, hidden_all, back, out):
        step_width = width // 3
        for m in range(3):
            at = slice(m * step_width, (m + 1) * step_width)
            out[at, :width] = dot_lt(attended_ref[:, at], own_back[...]).astype(BF)
            out[at, width:] = dot_lt(hidden_all[:, at], back[...]).astype(BF)

    (attention_gradient,) = call(
        order,
        attention_gradient_kernel,
        "attention_gradient",
        [],
        [wait_for(attended, feed_addends), branch_back, hidden_one_all, projected_back],
        [((width, width + 3 * block), BF)],
        6.4,
        limit=32,
        near=(1, 3),
    )
    attention_sum = sent_gradient(attention_gradient)

    def output_kernel(*refs):
        feeds = refs[:rep_size]
        tokens_ref, branch_ref, cotangent_ref, places, modulation = refs[rep_size : rep_size + 5]
        block_out, sums_out, sums = refs[rep_size + 5 :]
        sums[...] = jnp.zeros_like(sums)

        def step(here):
            slot_of = places[0, here, 0:1]
            feed = feeds[0][here, :]
            for ref in feeds[1:]:
                feed = feed + ref[here, :].astype(F32)
            gate_one = pick(modulation, slot_of, 2 * width, width)
            middle = tokens_ref[here, :].astype(F32) + gate_one * branch_ref[here, :]
            gate_two = pick(modulation, slot_of, 5 * width, width)
            block_out[here, :] = (middle + gate_two * feed).astype(BF)
            masked = cotangent_ref[here, :].astype(F32) * places[0, here, 3:4]
            add_slots(sums, 0, slots, slot_of, masked * feed)

        chunks(count, step, 1)
        sums_out[...] = jnp.sum(sums[...], axis=1)

    block_output, gate_two_sums = call(
        order,
        output_kernel,
        "layer_output",
        [],
        feed_addends + [tokens, branch, cotangent, place_columns, modulation],
        [((count, width), BF), ((slots, width), F32)],
        30.0,
        scratch=[((slots, 8, width), F32)],
        limit=16,
        near=range(1, rep_size),
    )

    def first_back_kernel(r_ref, *refs):
        addends = refs[:rep_size]
        tokens_ref, back_ref, modulation, places, middle_ref, gate_two_ref, bias, out_bias = refs[
            rep_size : rep_size + 8
        ]
        gradient, back_blocks, sums, whole, whole_bias, stack = refs[rep_size + 8 :]
        sums[...] = jnp.zeros_like(sums)

        def step(here):
            slot_of = places[0, here, 0:1]
            upstream = addends[0][here, :]
            for ref in addends[1:]:
                upstream = upstream + ref[here, :].astype(F32)
            normed, inverse = normalize_keep(tokens_ref[here, :].astype(F32))
            scale = pick(modulation, slot_of, width, width)
            gradient[here, :] = back_ref[here, :] + normalize_back(
                normed, inverse, upstream * (1.0 + scale)
            )
            add_slots(sums, 0, slots, slot_of, upstream)
            add_slots(sums, slots, slots, slot_of, upstream * normed)

        chunks(count, step)
        total = jnp.sum(sums[...], axis=1)
        whole[:, :width] = total[:slots]
        whole[:, width : 2 * width] = total[slots:]
        for t in range(3):
            at = slice((2 + t) * width, (3 + t) * width)
            whole[:, at] = middle_ref[t * slots : (t + 1) * slots, :]
        whole[:, 5 * width :] = gate_two_ref[...]
        whole_bias[...] = jnp.zeros_like(whole_bias)
        for k in range(rep_size):

            @pl.when(r_ref[0] == k)
            def _():
                for t in range(3):
                    first = t * width + k * block
                    whole_bias[:, first : first + block] = bias[:, t * padded : t * padded + block]

        stack[...] = jnp.zeros_like(stack)
        for k in range(fsdp_size):
            stack[k, :slots, :] = whole[:, k * columns : (k + 1) * columns]
            at = slice(k * shard_bias, (k + 1) * shard_bias)
            stack[k, slots : slots + 1, :shard_bias] = whole_bias[:, at]
            at = slice(k * shard_out_bias, (k + 1) * shard_out_bias)
            lanes = slice(shard_bias, shard_bias + shard_out_bias)
            stack[k, slots : slots + 1, lanes] = out_bias[:, at]
        back_blocks[...] = stack[...].reshape(fsdp_size * GROUP, columns).astype(BF)

    tokens_gradient, back_blocks = call(
        order,
        first_back_kernel,
        "first_norm_back",
        [r_index],
        one_addends
        + [tokens, middle_back, modulation, place_columns, middle_sums, gate_two_sums]
        + [projection_bias_sum, output_bias_sum],
        [((count, width), F32), ((fsdp_size * GROUP, columns), BF)],
        30.0,
        scratch=[
            ((2 * slots, 8, width), F32),
            ((slots, 6 * width), F32),
            ((1, 3 * width), F32),
            ((fsdp_size, GROUP, columns), F32),
        ],
        limit=20,
        near=range(1, rep_size),
    )

    line_backs = exchange(back_blocks, "fsdp")
    feed_sums = gather(wait_for(feed_sum, one_addends), "rep", rep_size)

    def conditioning_kernel(groups, activated_ref, weight, out, line_out):
        stack = groups[...].astype(F32)
        bias = jnp.sum(stack.reshape(fsdp_size, GROUP, columns), axis=0)[slots : slots + 1]
        row_ids = lax.broadcasted_iota(jnp.int32, (fsdp_size * GROUP, 1), 0)
        rows_back = jnp.where(lax.rem(row_ids, GROUP) < slots, stack, 0.0)
        line_out[:, :width] = activated_ref[...]
        line_out[:, width:] = jnp.where(row_ids == slots, bias, rows_back).astype(BF)
        result = dot(rows_back.astype(BF), weight[...])
        for k in range(fsdp_size):
            out[k * slots : (k + 1) * slots, :] = result[k * GROUP : k * GROUP + slots, :]

    activated_backs, line_back = call(
        order,
        conditioning_kernel,
        "conditioning_back",
        [],
        [wait_for(line_backs, feed_sums[1:3]), line_activated, modulation_weight.T],
        [((fsdp_size * slots, width), F32), ((fsdp_size * GROUP, width + columns), BF)],
        40.0,
        limit=24,
    )
    activated_backs = exchange(activated_backs, "fsdp")
    all_lines = gather(line_back, "rep", rep_size)

    def feed_blocks_kernel(r_ref, *refs):
        gate_out, up_out, down_out, stack = refs[rep_size:]
        for j in range(rep_size):
            stack[j] = refs[j][...].astype(F32)
        for k in range(rep_size):
            here = r_ref[0] ^ k
            for j in range(fsdp_size):
                target = slice(j * shard_ff + k * piece, j * shard_ff + (k + 1) * piece)
                first = block_ff + j * piece
                gate_out[:, target] = stack[here, :, j * piece : (j + 1) * piece]
                up_out[:, target] = stack[here, :, first : first + piece]
            for a, lanes, c, packed_lanes in units:
                to_row = k * piece + a
                down_out[to_row : to_row + unit_rows, lanes] = stack[
                    here, c : c + unit_rows, packed_lanes
                ]

    gate_gradient, up_gradient, down_gradient = call(
        order,
        feed_blocks_kernel,
        "feed_blocks",
        [r_index],
        feed_sums,
        [((shard_width, fsdp_size * shard_ff), F32)] * 2 + [((shard_ff, width), F32)],
        5.2,
        scratch=[((rep_size, shard_width, 3 * block_ff), F32)],
        limit=24,
        near=range(1, rep_size),
    )

    def table_kernel(*refs):
        lines, (condition, activated_back) = refs[:rep_size], refs[rep_size : rep_size + 2]
        table, table_bias, bias, out_bias, gradient, activated_stack, back_stack = refs[
            rep_size + 2 :
        ]
        upstream = jnp.sum(activated_back[...].reshape(fsdp_size, slots, width), axis=0)
        gradient[...] = upstream * silu_slope(condition[...].astype(F32))
        line = fsdp_size * GROUP
        total = jnp.zeros((1, columns), F32)
        for j in range(rep_size):
            back = lines[j][:, width:]
            activated_stack[j * line : (j + 1) * line, :] = lines[j][:, :width]
            back_stack[j * line : (j + 1) * line, :] = back
            total = total + back.astype(F32)[slots : slots + 1, :]
        bias[...] = total[:, :shard_bias]
        out_bias[...] = total[:, shard_bias : shard_bias + shard_out_bias]
        back = back_stack[...].astype(F32)
        in_group = lax.rem(lax.broadcasted_iota(jnp.int32, (rep_size * line, 1), 0), GROUP)
        table_bias[...] = jnp.sum(
            jnp.where(in_group < slots, back, 0.0), axis=0, keepdims=True
        )
        table[...] = dot_lt(back_stack[...], activated_stack[...])

    table_gradient, table_bias_gradient, bias_gradient, out_bias_gradient, activated_gradient = call(
        order,
        table_kernel,
        "table_gradient",
        [],
        all_lines + [conditioning[0], activated_backs],
        [((columns, width), F32), ((1, columns), F32)]
        + [((1, shard_bias), F32), ((1, shard_out_bias), F32), ((slots, width), F32)],
        4.0,
        scratch=[
            ((rep_size * fsdp_size * GROUP, width), BF),
            ((rep_size * fsdp_size * GROUP, columns), BF),
        ],
        limit=24,
        near=range(1, rep_size),
    )

    attention_late = wait_for(attention_sum, table_gradient)
    output_gradient = attention_late[:, :width].astype(F32)
    projection_sums = gather(attention_late[:, width:], "rep", rep_size)
    for bit in [1 << k for k in range(rep_size.bit_length() - 1)]:
        came = swap_with(output_gradient.astype(BF), "rep", rep_size, bit)
        came = wait_for(came, projection_sums[2 % rep_size]) if bit == 1 else came
        output_gradient = output_gradient + came.astype(F32)

    def projection_blocks_kernel(r_ref, *refs):
        out, stack = refs[rep_size:]
        for j in range(rep_size):
            stack[j] = refs[j][...].astype(F32)
        for k in range(rep_size):
            here = r_ref[0] ^ k
            for t in range(3):
                first = t * width + k * block
                out[:, first : first + block] = stack[here, :, t * block : (t + 1) * block]

    (projection_gradient,) = call(
        order,
        projection_blocks_kernel,
        "projection_blocks",
        [r_index],
        projection_sums,
        [((shard_width, 3 * width), F32)],
        3.0,
        scratch=[((rep_size, shard_width, 3 * block), F32)],
        limit=24,
        near=range(1, rep_size),
    )
    return (
        block_output[None],
        tokens_gradient[None],
        activated_gradient[None],
        table_gradient.T,
        table_bias_gradient[0],
        projection_gradient,
        bias_gradient[0],
        output_gradient,
        out_bias_gradient[0],
        gate_gradient,
        up_gradient,
        down_gradient,
    )


def solution(mesh):
    sizes = dict(mesh.shape)

    def body(*arrays):
        return on_device(sizes["rep"], sizes["fsdp"], *arrays)

    rows = ("rep", "fsdp")
    in_specs = (
        P(rows, None, None),
        P(rows, None, None),
        P(rows, None),
        P(rows, None),
        P(rows, None),
        P(rows, None),
        P(None, "fsdp"),
        P("fsdp"),
        P("fsdp", None),
        P("fsdp"),
        P("fsdp", None),
        P("fsdp"),
        P("fsdp", None),
        P("fsdp", None),
        P("fsdp", None),
        P(rows, None, None),
    )
    out_specs = (
        P(rows, None, None),
        P(rows, None, None),
        P(rows, None, None),
        P(None, "fsdp"),
        P("fsdp"),
        P("fsdp", None),
        P("fsdp"),
        P("fsdp", None),
        P("fsdp"),
        P("fsdp", None),
        P("fsdp", None),
        P("fsdp", None),
    )
    return jax.shard_map(
        body, mesh=mesh, in_specs=in_specs, out_specs=out_specs, check_vma=False
    )
```
